256 devices in a mesh: head: 8 (over z_lo, core), blk: 32 (over y, x, z_hi).
Axes of the slice: x: 4, y: 4, z: 8 (z_hi: 2, z_lo: 4; z = z_hi * 4 + z_lo), core: 2. Of those that a mesh axis runs over, the one named last changes fastest.
Arguments:
- query_act: bfloat16 [8192, 5120], P(('blk', 'head')), may hold values from -6 to 6
- key_act: bfloat16 [8192, 1024], P(('blk', 'head')), may hold values from -6 to 6
- value_act: bfloat16 [8192, 1024], P(('blk', 'head')), may hold values from -6 to 6
- attn_out: bfloat16 [8192, 5120], P(('blk', 'head')), may hold values from -4 to 4
- grad_out: bfloat16 [8192, 5120], P(('blk', 'head')), may hold values from -6 to 6
- log_sum: float32 [8192, 40], P(('blk', 'head')), may hold values from 5 to 6.5
- kv_lists: int32 [64, 32], P('blk'), may hold values from -1 to 63, as said below
Outputs:
- grad_query: bfloat16 [8192, 5120], P(('blk', 'head'))
- grad_key: bfloat16 [8192, 1024], P(('blk', 'head'))
- grad_value: bfloat16 [8192, 1024], P(('blk', 'head'))
The draws below stay inside these ranges and needn't reach their ends.
Inputs may be any that keep to these rules, and one draw needn't show every extreme that they name: `kv_lists`: the pack is made of prompt trees: the first holds 16 blocks, the last 16, and those between 32 blocks each, in order. A tree is a prompt, then branches. Row r names in rising order the blocks whose keys block r sees (the tree's prompt blocks up to r, and the earlier blocks of r's branch), then -1 to the end. Every entry lies in the same tree as r and is at most r; r itself is always named.
All inputs are finite; a program needn't handle non-finite values.
Results may differ from the reference program's by a relative error of at most 0.0049.
Values may be sent and summed in bfloat16 or wider, within the bound.
A program may use at most 64 MiB of HBM per device.

```python
import jax
import jax.numpy as jnp
from jax import lax

QH = 40
KVH = 8
HD = 128
BLOCK = 128
TREE_B = 32
SEQ = 8192


def draw_kv_lists(key, part):
    total_blocks = SEQ // BLOCK
    half_tree = TREE_B // 2
    trees = total_blocks // TREE_B + 1
    key_prefix, key_cut = jax.random.split(jax.random.fold_in(key, 17), 2)
    prefix = jax.random.randint(key_prefix, (trees, 1), 1, TREE_B // 4 + 1).astype(jnp.int32)
    cuts = jax.random.randint(key_cut, (trees, TREE_B), 0, 6) == 0
    spots = jnp.arange(TREE_B, dtype=jnp.int32)[None, :]
    branch_starts = (spots == prefix) | (spots > prefix) & cuts
    branch_table = lax.cummax(jnp.where(branch_starts, spots, 0).astype(jnp.int32), axis=1)
    blocks = jnp.arange(total_blocks, dtype=jnp.int32)
    tree_of = (blocks + half_tree) // TREE_B
    tree_start = jnp.maximum(tree_of * TREE_B - half_tree, 0).astype(jnp.int32)
    local = (blocks - tree_start).astype(jnp.int32)
    block_prefix = jnp.take(prefix[:, 0], tree_of)
    block_branch = branch_table[tree_of, local]
    cols = jnp.arange(TREE_B, dtype=jnp.int32)[None, :]
    seen = (cols <= local[:, None]) & ((cols < block_prefix[:, None]) | (cols >= block_branch[:, None]))
    order = jnp.argsort(jnp.where(seen, 0, 1).astype(jnp.int32), axis=1, stable=True).astype(jnp.int32)
    sorted_seen = jnp.take_along_axis(seen, order, axis=1)
    lists = jnp.where(sorted_seen, tree_start[:, None] + order, -1).astype(jnp.int32)
    return lists


def block_scale(stream_key, dims, cuts, least, top_value):
    factor_of = 1.0
    for dim, blocks in cuts:
        steps = jax.random.uniform(jax.random.fold_in(jax.random.fold_in(stream_key, 6), dim), (blocks,), jnp.float32, least / len(cuts), top_value / len(cuts))
        factor_of = factor_of * jnp.repeat(jnp.exp(steps), dims[dim] // blocks).reshape((-1,) + (1,) * (len(dims) - 1 - dim))
    return factor_of


def normal_values(own_key, shape, deviation, limit, pieces=(), kind=jnp.bfloat16):
    entries = deviation * jax.random.normal(own_key, shape, jnp.float32)
    if pieces:
        entries = entries * block_scale(own_key, shape, pieces, -0.22, 0.18)
    return jnp.clip(entries, -limit, limit).astype(kind)


def setup_inputs(seed: int = 0) -> dict:
    seeds = jax.random.split(jax.random.key(seed), 8)
    return {
        "query_act": normal_values(seeds[0], (SEQ, QH * HD), 1.0, 6.0, ((0, 256),)),
        "key_act": normal_values(seeds[1], (SEQ, KVH * HD), 1.0, 6.0, ((0, 256),)),
        "value_act": normal_values(seeds[2], (SEQ, KVH * HD), 1.0, 6.0, ((0, 256),)),
        "attn_out": normal_values(seeds[3], (SEQ, QH * HD), 0.5, 4.0, ((0, 256),)),
        "grad_out": normal_values(seeds[4], (SEQ, QH * HD), 1.0, 6.0, ((0, 256),)),
        "log_sum": jnp.clip(5.0 + 1.5 * jax.random.uniform(seeds[5], (SEQ, QH), jnp.float32) ** block_scale(seeds[5], (SEQ, QH), ((0, 256),), -0.2, 0.2), 5.0, 6.5),
        "kv_lists": draw_kv_lists(jax.random.fold_in(seeds[7], 71), 0),
    }


def head_major(rows, heads):
    return rows.astype(jnp.float32).reshape(SEQ, heads, HD).transpose(1, 0, 2)


def rounded(values):
    return lax.optimization_barrier(values.astype(jnp.bfloat16)).astype(jnp.float32)


def reference(query_act, key_act, value_act, attn_out, grad_out, log_sum, kv_lists):
    group_size = QH // KVH
    scaling = HD ** -0.5
    tile_rows = min(512, SEQ)
    window = min(SEQ, tile_rows + (TREE_B - 1) * BLOCK)
    highest = lax.Precision.HIGHEST
    queries = head_major(query_act, QH).reshape(KVH, group_size, SEQ, HD)
    out_grads = head_major(grad_out, QH).reshape(KVH, group_size, SEQ, HD)
    outputs = head_major(attn_out, QH).reshape(KVH, group_size, SEQ, HD)
    row_delta = jnp.sum(out_grads * outputs, axis=3)
    row_totals = log_sum.astype(jnp.float32).T.reshape(KVH, group_size, SEQ)
    key_heads = head_major(key_act, KVH)
    value_heads = head_major(value_act, KVH)
    tile_starts = jnp.arange(SEQ // tile_rows, dtype=jnp.int32) * tile_rows

    def one_head(operands):
        query_head, grad_head, key_head, value_head, totals, deltas = operands

        def tile_step(carried, tile_start):
            key_sum, value_sum = carried
            query_tile = lax.dynamic_slice_in_dim(query_head, tile_start, tile_rows, 1)
            grad_tile = lax.dynamic_slice_in_dim(grad_head, tile_start, tile_rows, 1)
            total_tile = lax.dynamic_slice_in_dim(totals, tile_start, tile_rows, 1)
            delta_tile = lax.dynamic_slice_in_dim(deltas, tile_start, tile_rows, 1)
            win_start = jnp.clip(tile_start - (TREE_B - 1) * BLOCK, 0, SEQ - window).astype(jnp.int32)
            key_win = lax.dynamic_slice_in_dim(key_head, win_start, window, 0)
            value_win = lax.dynamic_slice_in_dim(value_head, win_start, window, 0)
            row_lists = lax.dynamic_slice_in_dim(kv_lists, (tile_start // BLOCK).astype(jnp.int32), tile_rows // BLOCK, 0)
            key_ids = (win_start // BLOCK).astype(jnp.int32) + jnp.arange(window // BLOCK, dtype=jnp.int32)
            listed = jnp.any(row_lists[:, :, None] == key_ids[None, None, :], axis=1)
            listed = jnp.repeat(jnp.repeat(listed, BLOCK, axis=0), BLOCK, axis=1)
            query_pos = tile_start + jnp.arange(tile_rows, dtype=jnp.int32)
            key_pos = win_start + jnp.arange(window, dtype=jnp.int32)
            visible = listed & (key_pos[None, :] <= query_pos[:, None])
            scores = jnp.einsum("gtd,sd->gts", query_tile, key_win, precision=highest) * scaling
            weights = jnp.where(visible[None], jnp.exp(scores - total_tile[:, :, None]), 0.0)
            grad_probs = jnp.einsum("gtd,sd->gts", grad_tile, value_win, precision=highest)
            grad_scores = rounded(weights * (grad_probs - delta_tile[:, :, None]))
            probs_low = rounded(weights)
            query_part = jnp.einsum("gts,sd->gtd", grad_scores, key_win, precision=highest) * scaling
            key_part = jnp.einsum("gts,gtd->sd", grad_scores, query_tile, precision=highest) * scaling
            value_part = jnp.einsum("gts,gtd->sd", probs_low, grad_tile, precision=highest)
            key_old = lax.dynamic_slice_in_dim(key_sum, win_start, window, 0)
            value_old = lax.dynamic_slice_in_dim(value_sum, win_start, window, 0)
            key_sum = lax.dynamic_update_slice_in_dim(key_sum, key_old + key_part, win_start, 0)
            value_sum = lax.dynamic_update_slice_in_dim(value_sum, value_old + value_part, win_start, 0)
            return (key_sum, value_sum), query_part

        empty_sum = jnp.zeros((SEQ, HD), jnp.float32)
        (key_sum, value_sum), query_parts = lax.scan(tile_step, (empty_sum, empty_sum), tile_starts)
        query_grad = query_parts.transpose(1, 0, 2, 3).reshape(group_size, SEQ, HD)
        return query_grad, key_sum, value_sum

    query_grad, key_grad, value_grad = lax.map(one_head, (queries, out_grads, key_heads, value_heads, row_totals, row_delta))
    grad_query = query_grad.transpose(2, 0, 1, 3).reshape(SEQ, QH * HD).astype(jnp.bfloat16)
    grad_key = key_grad.transpose(1, 0, 2).reshape(SEQ, KVH * HD).astype(jnp.bfloat16)
    grad_value = value_grad.transpose(1, 0, 2).reshape(SEQ, KVH * HD).astype(jnp.bfloat16)
    return (grad_query, grad_key, grad_value)
```

```python
import jax
import jax.numpy as jnp
from jax import lax
from jax.experimental import pallas as pl
from jax.experimental.pallas import tpu as pltpu
from jax.sharding import PartitionSpec as P

QH = 40
KVH = 8
HD = 128
BLOCK = 128
GS = QH // KVH
TOK = 32
GW = GS * HD
PIECE = 64
ROWS = GS * PIECE
NX = 4
NZ = 8
PEERS = 8
LISTW = 32
SCALE = HD ** -0.5
LOG2E = 1.4426950408889634
MESH = pl.DeviceIdType.MESH
F32 = jnp.float32
BF16 = jnp.bfloat16
NT = (((1,), (1,)), ((), ()))
NN = (((1,), (0,)), ((), ()))


def coords():
    blk = lax.axis_index("blk")
    head = lax.axis_index("head")
    y = blk // 8
    x = (blk // 2) % 4
    z = (blk % 2) * 4 + head // 2
    return y, x, z, head % 2


def device(y, x, z, core):
    return {"blk": (y * 4 + x) * 2 + z // 4, "head": (z % 4) * 2 + core}


def remote(src, dst, send_sem, recv_sem, device_id):
    return pltpu.make_async_remote_copy(
        src_ref=src,
        dst_ref=dst,
        send_sem=send_sem,
        recv_sem=recv_sem,
        device_id=device_id,
        device_id_type=MESH,
    )


def signal_group(bar, y, x, z, core, me):
    for d in range(1, PEERS):
        p = (me + d) % PEERS
        pl.semaphore_signal(bar, inc=1, device_id=device(y, p // 2, z, p % 2), device_id_type=MESH)
    for step in (1, NZ - 1):
        pl.semaphore_signal(
            bar, inc=1, device_id=device(y, x, (z + step) % NZ, core), device_id_type=MESH
        )
    cross = (y == 1) | (y == 2)

    @pl.when(cross)
    def _():
        pl.semaphore_signal(bar, inc=1, device_id=device(3 - y, x, z, core), device_id_type=MESH)

    pl.semaphore_wait(bar, PEERS - 1 + 2 + cross.astype(jnp.int32))


CHAINS = ((0, 0, 4), (0, 1, 3), (1, 1, 4), (1, 0, 3))


def gather_kernel(
    q, k, v, o, do, lse, lists,
    qg, dog, stg, lsg, kvg,
    stat_src, list_src,
    kv_s, kv_r, kv_l, big_s, big_r, big_l, st_s, st_r, st_l, ls_s, ls_r, ls_l,
    ring_s, ring_r, cr_s, cr_r, crst_s, crst_r, crls_s, crls_r,
):
    y, x, z, core = coords()
    me = x * 2 + core
    bar = pltpu.get_barrier_semaphore()
    signal_group(bar, y, x, z, core, me)

    def cols(ref, g, width):
        return ref.at[:, pl.ds(pl.multiple_of(g * width, 128), width)]

    def kv_slot(s, piece, zz):
        return kvg.at[zz, piece, s // 2, pl.ds((s % 2) * TOK, TOK), :]

    def kv_copy(d, piece):
        p = (me + d) % PEERS
        src = (k, v)[piece]
        return remote(
            cols(src, p, HD), kv_slot(me, piece, z),
            kv_s.at[piece, p], kv_r.at[piece, me], device(y, p // 2, z, p % 2),
        )

    def kv_recv(d, piece):
        s = (me + PEERS - d) % PEERS
        src = (k, v)[piece]
        return remote(
            cols(src, s, HD), kv_slot(s, piece, z),
            kv_s.at[piece, s], kv_r.at[piece, s], device(y, s // 2, z, s % 2),
        )

    def big_copy(d, which):
        p = (me + d) % PEERS
        src, dst = ((q, qg), (do, dog))[which]
        return remote(
            cols(src, p, GW), dst.at[0, me],
            big_s.at[which, p], big_r.at[which, me], device(y, p // 2, z, p % 2),
        )

    def big_recv(s, which):
        src, dst = ((q, qg), (do, dog))[which]
        return remote(
            cols(src, s, GW), dst.at[0, s],
            big_s.at[which, s], big_r.at[which, s], device(y, s // 2, z, s % 2),
        )

    def st_copy(d):
        p = (me + d) % PEERS
        return remote(
            stat_src.at[p], stg.at[0, me], st_s.at[p], st_r.at[me], device(y, p // 2, z, p % 2)
        )

    def st_recv(d):
        s = (me + PEERS - d) % PEERS
        return remote(
            stat_src.at[s], stg.at[0, s], st_s.at[s], st_r.at[s], device(y, s // 2, z, s % 2)
        )

    def ls_copy(d):
        xx = (x + d) % NX
        return remote(list_src, lsg.at[0, x], ls_s.at[xx], ls_r.at[x], device(y, xx, z, core))

    def ls_recv(d):
        xx = (x + NX - d) % NX
        return remote(list_src, lsg.at[0, xx], ls_s.at[xx], ls_r.at[xx], device(y, xx, z, core))

    order = (2, 3, 4, 5, 6, 7, 1)
    for piece in (0, 1):
        for d in order:
            kv_copy(d, piece).start()
    kv_local = [
        pltpu.make_async_copy(cols((k, v)[piece], me, HD), kv_slot(me, piece, z), kv_l.at[piece])
        for piece in (0, 1)
    ]
    big_local = [
        pltpu.make_async_copy(cols(q, me, GW), qg.at[0, me], big_l.at[0]),
        pltpu.make_async_copy(cols(do, me, GW), dog.at[0, me], big_l.at[1]),
    ]
    for c in kv_local + big_local:
        c.start()
    for d in order:
        for which in (0, 1):
            big_copy(d, which).start()

    rows = lists[...]
    count = jnp.sum(jnp.where(rows >= 0, 1.0, 0.0), axis=1, keepdims=True).astype(jnp.int32)
    early = jnp.sum(
        jnp.where((rows >= 0) & (rows < 32), 1.0, 0.0), axis=1, keepdims=True
    ).astype(jnp.int32)
    list_src[...] = jnp.zeros((8, 128), jnp.int32)
    list_src[0:2, 0:LISTW] = rows
    lane = lax.broadcasted_iota(jnp.int32, (2, 128), 1)
    list_src[4:6, :] = jnp.where(lane == 0, count, early)
    for d in range(1, NX):
        ls_copy(d).start()
    ls_local = pltpu.make_async_copy(list_src, lsg.at[0, x], ls_l)
    ls_local.start()

    lane = lax.broadcasted_iota(jnp.int32, (TOK, 128), 1)
    for g in range(KVH):
        block = jnp.zeros((TOK, 128), F32)
        for r in range(GS):
            h = g * GS + r
            own = slice(h * HD, (h + 1) * HD)
            delta = jnp.sum(do[:, own].astype(F32) * o[:, own].astype(F32), axis=1, keepdims=True)
            block = jnp.where(lane == r, lse[:, h : h + 1] * LOG2E, block)
            block = jnp.where(lane == 8 + r, delta, block)
        stat_src[g] = block
    for d in order:
        st_copy(d).start()
    st_local = pltpu.make_async_copy(stat_src.at[me], stg.at[0, me], st_l)
    st_local.start()

    def ring_copy(direction, piece, step):
        sign = (1, NZ - 1)[direction]
        back = (NZ - 1, 1)[direction]
        chunk = (z + back * step) % NZ
        part = kvg.at[chunk, piece]
        return remote(
            part, part, ring_s.at[direction, piece, step], ring_r.at[direction, piece, step],
            device(y, x, (z + sign) % NZ, core),
        )

    def ring_recv(direction, piece, step):
        back = (NZ - 1, 1)[direction]
        chunk = (z + back * (step + 1)) % NZ
        part = kvg.at[chunk, piece]
        return remote(
            part, part, ring_s.at[direction, piece, step], ring_r.at[direction, piece, step],
            device(y, x, (z + back) % NZ, core),
        )

    for piece in (0, 1):
        for d in range(1, PEERS):
            kv_recv(d, piece).wait_recv()
        kv_local[piece].wait()
        for direction in (0, 1):
            ring_copy(direction, piece, 0).start()

    def cross_copy(s, which):
        ref = (qg, dog)[which]
        return remote(
            ref.at[0, s], ref.at[1, s], cr_s.at[which, s], cr_r.at[which, s],
            device(3 - y, x, z, core),
        )

    for c in big_local:
        c.wait()

    @pl.when(y == 2)
    def _():
        for which in (0, 1):
            cross_copy(me, which).start()

    def forward(ds):
        for d in ds:
            s = (me + PEERS - d) % PEERS
            for which in (0, 1):
                big_recv(s, which).wait_recv()

            @pl.when(y == 2)
            def _():
                for which in (0, 1):
                    cross_copy(s, which).start()

    groups = ((7, 1), (2, 3), (4, 5, 6), ())
    for step in range(4):
        for direction, piece, steps in CHAINS:
            if step < steps:
                ring_recv(direction, piece, step).wait_recv()
                if step + 1 < steps:
                    ring_copy(direction, piece, step + 1).start()
        forward(groups[step])

    for d in range(1, PEERS):
        st_recv(d).wait_recv()
    for d in range(1, NX):
        ls_recv(d).wait_recv()
    st_local.wait()
    ls_local.wait()

    crst = remote(stg.at[0], stg.at[1], crst_s, crst_r, device(3 - y, x, z, core))
    crls = remote(lsg.at[0], lsg.at[1], crls_s, crls_r, device(3 - y, x, z, core))

    @pl.when(y == 2)
    def _():
        crst.start()
        crls.start()

    for d in range(1, PEERS):
        for i in (0, 1):
            kv_copy(d, i).wait_send()
            big_copy(d, i).wait_send()
        st_copy(d).wait_send()
    for d in range(1, NX):
        ls_copy(d).wait_send()
    for direction, piece, steps in CHAINS:
        for step in range(steps):
            ring_copy(direction, piece, step).wait_send()

    @pl.when(y == 2)
    def _():
        for s in range(PEERS):
            for which in (0, 1):
                cross_copy(s, which).wait_send()
        crst.wait_send()
        crls.wait_send()

    @pl.when(y == 1)
    def _():
        for s in range(PEERS):
            for which in (0, 1):
                cross_copy(s, which).wait_recv()
        crst.wait_recv()
        crls.wait_recv()


def gather(q, k, v, o, do, lse, lists):
    vmem = pl.BlockSpec(memory_space=pltpu.VMEM)
    dma = pltpu.SemaphoreType.DMA
    return pl.pallas_call(
        gather_kernel,
        out_shape=(
            jax.ShapeDtypeStruct((2, PEERS, TOK, GW), BF16),
            jax.ShapeDtypeStruct((2, PEERS, TOK, GW), BF16),
            jax.ShapeDtypeStruct((2, PEERS, TOK, 128), F32),
            jax.ShapeDtypeStruct((2, NX, 8, 128), jnp.int32),
            jax.ShapeDtypeStruct((NZ, 2, NX, PIECE, HD), BF16),
        ),
        in_specs=[vmem] * 7,
        out_specs=(vmem,) * 5,
        scratch_shapes=[
            pltpu.VMEM((KVH, TOK, 128), F32),
            pltpu.VMEM((8, 128), jnp.int32),
            dma((2, PEERS)), dma((2, PEERS)), dma((2,)),
            dma((2, PEERS)), dma((2, PEERS)), dma((2,)),
            dma((PEERS,)), dma((PEERS,)), dma,
            dma((NX,)), dma((NX,)), dma,
            dma((2, 2, 4)), dma((2, 2, 4)),
            dma((2, PEERS)), dma((2, PEERS)),
            dma, dma, dma, dma,
        ],
        compiler_params=pltpu.CompilerParams(collective_id=0, has_side_effects=True),
        name="gather",
    )(q, k, v, o, do, lse, lists)


def attend_kernel(
    lists, qg, dog, stg, kvg, dq, dkv,
    qs, dos, qt, dot, lseb, delb, dqa, dka, dva,
):
    y, x, z, core = coords()
    half = (z % 4) // 2
    base = y * 16
    for ref in (dka, dva):
        ref[...] = jnp.zeros_like(ref)
    r_id = lax.broadcasted_iota(jnp.int32, (128, 128), 0)
    c_id = lax.broadcasted_iota(jnp.int32, (128, 128), 1)
    eye = jnp.where(r_id == c_id, 1.0, 0.0).astype(BF16)
    row_tok = (z % 2) * PIECE + lax.broadcasted_iota(jnp.int32, (ROWS, 128), 0) % PIECE
    key_tok = lax.broadcasted_iota(jnp.int32, (ROWS, 128), 1)

    def chunk(i, carry):
        part = i // NX
        xx = i % NX
        total = lists[part, xx, 4 + half, 0]
        early = lists[part, xx, 4 + half, 1]
        own = part == 0
        lo = jnp.where(own & (y == 2), early, 0)
        hi = jnp.where(own, total, jnp.where(y == 1, early, 0))
        n = hi - lo
        diag = jnp.where(own, xx * 4 + z // 2, -1)

        @pl.when(n > 0)
        def _():
            for c in range(2):
                st = stg[part, xx * 2 + c]
                for r in range(GS):
                    at = slice(r * PIECE + c * TOK, r * PIECE + (c + 1) * TOK)
                    col = slice(r * HD, (r + 1) * HD)
                    qs[at, :] = qg[part, xx * 2 + c, :, col]
                    dos[at, :] = dog[part, xx * 2 + c, :, col]
                    lseb[at, :] = jnp.broadcast_to(st[:, r : r + 1], (TOK, 128))
                    delb[at, :] = jnp.broadcast_to(st[:, 8 + r : 9 + r], (TOK, 128))
            qt[...] = lax.dot_general(eye, qs[...], NT, preferred_element_type=F32).astype(BF16)
            dot[...] = lax.dot_general(eye, dos[...], NT, preferred_element_type=F32).astype(BF16)
            dqa[...] = jnp.zeros_like(dqa)

            def block(piece, b):
                zz = (b % 4) * 2
                return jnp.concatenate(
                    [kvg[zz, piece, b // 4], kvg[zz + 1, piece, b // 4]], axis=0
                )

            def pair(j, masked):
                a = lists[part, xx, half, j] - base
                if masked:
                    has = j + 1 < hi
                    b = jnp.where(has, lists[part, xx, half, jnp.where(has, j + 1, j)] - base, a)
                else:
                    b = lists[part, xx, half, j + 1] - base
                keys = jnp.concatenate([block(0, a), block(0, b)], axis=0)
                values = jnp.concatenate([block(1, a), block(1, b)], axis=0)
                s = lax.dot_general(qs[...], keys, NT, preferred_element_type=F32)
                lse2 = jnp.concatenate([lseb[...], lseb[...]], axis=1)
                del2 = jnp.concatenate([delb[...], delb[...]], axis=1)
                p = jnp.exp2(s * (SCALE * LOG2E) - lse2)
                if masked:
                    ta = row_tok + jnp.where(a == diag, 0, BLOCK)
                    tb = row_tok + jnp.where(has, jnp.where(b == diag, 0, BLOCK), -2 * BLOCK)
                    seen = jnp.concatenate([key_tok <= ta, key_tok <= tb], axis=1)
                    p = jnp.where(seen, p, 0.0)
                dp = lax.dot_general(dos[...], values, NT, preferred_element_type=F32)
                ds = (p * (dp - del2)).astype(BF16)
                pb = p.astype(BF16)
                dvt = lax.dot_general(dot[...], pb, NN, preferred_element_type=F32)
                dkt = lax.dot_general(qt[...], ds, NN, preferred_element_type=F32)
                dqa[...] += lax.dot_general(ds, keys, NN, preferred_element_type=F32)
                dva[a] += dvt[:, :BLOCK]
                dka[a] += dkt[:, :BLOCK]
                dva[b] += dvt[:, BLOCK:]
                dka[b] += dkt[:, BLOCK:]

            full = (n - 1) // 2

            def step(t, carry):
                pair(lo + 2 * t, False)
                return carry

            lax.fori_loop(0, full, step, 0)
            pair(lo + 2 * full, True)
            for c in range(2):
                for r in range(GS):
                    at = slice(r * PIECE + c * TOK, r * PIECE + (c + 1) * TOK)
                    col = slice(r * HD, (r + 1) * HD)
                    dq[part, xx * 2 + c, :, col] = (dqa[at, :] * SCALE).astype(BF16)

        @pl.when((n <= 0) & (y == 1))
        def _():
            for c in range(2):
                dq[part, xx * 2 + c] = jnp.zeros((TOK, GW), BF16)

        return carry

    lax.fori_loop(0, jnp.where(y == 1, 2 * NX, NX), chunk, 0)

    def finish(b, carry):
        zz = (b % 4) * 2
        for piece, ref, scale in ((0, dka, SCALE), (1, dva, 1.0)):
            low = (ref[b] * scale).astype(BF16)
            out = lax.dot_general(eye, low, NT, preferred_element_type=F32).astype(BF16)
            dkv[zz, piece, b // 4] = out[:PIECE]
            dkv[zz + 1, piece, b // 4] = out[PIECE:]
        return carry

    lax.fori_loop(0, 16, finish, 0)


def attend(lists, qg, dog, stg, kvg):
    vmem = pl.BlockSpec(memory_space=pltpu.VMEM)
    return pl.pallas_call(
        attend_kernel,
        out_shape=(
            jax.ShapeDtypeStruct((2, PEERS, TOK, GW), BF16),
            jax.ShapeDtypeStruct((NZ, 2, NX, PIECE, HD), BF16),
        ),
        in_specs=[pl.BlockSpec(memory_space=pltpu.SMEM)] + [vmem] * 4,
        out_specs=(vmem, vmem),
        scratch_shapes=[
            pltpu.VMEM((ROWS, HD), BF16),
            pltpu.VMEM((ROWS, HD), BF16),
            pltpu.VMEM((HD, ROWS), BF16),
            pltpu.VMEM((HD, ROWS), BF16),
            pltpu.VMEM((ROWS, 128), F32),
            pltpu.VMEM((ROWS, 128), F32),
            pltpu.VMEM((ROWS, HD), F32),
            pltpu.VMEM((16, HD, BLOCK), F32),
            pltpu.VMEM((16, HD, BLOCK), F32),
        ],
        name="attend",
    )(lists, qg, dog, stg, kvg)


def give_kernel(
    dq, dkv, gq, gk, gv,
    land, total, acc_in, acc_out, final,
    cr_s, cr_r, ring_s, ring_r, q_s, q_r, q_l, kv_s, kv_r, kv_l,
):
    y, x, z, core = coords()
    me = x * 2 + core
    bar = pltpu.get_barrier_semaphore()
    signal_group(bar, y, x, z, core, me)

    def cols(ref, g, width):
        return ref.at[:, pl.ds(pl.multiple_of(g * width, 128), width)]

    def cross_copy(s):
        return remote(dq.at[1, s], land.at[s], cr_s.at[s], cr_r.at[s], device(3 - y, x, z, core))

    slots = [(me + d) % PEERS for d in (2, 3, 4, 5, 6, 7, 1, 0)]

    @pl.when(y == 1)
    def _():
        for s in slots:
            cross_copy(s).start()

    def ring_copy(direction, piece, steps, step):
        sign = (1, NZ - 1)[direction]
        owner = (z + sign * (steps - step)) % NZ
        if step == 0:
            src = dkv.at[owner, piece]
        else:
            src = acc_out.at[direction, piece, step]
        return remote(
            src, acc_in.at[direction, piece, step],
            ring_s.at[direction, piece, step], ring_r.at[direction, piece, step],
            device(y, x, (z + sign) % NZ, core),
        )

    for direction, piece, steps in CHAINS:
        ring_copy(direction, piece, steps, 0).start()

    def q_copy(src, p):
        return remote(
            src.at[p], cols(gq, me, GW), q_s.at[p], q_r.at[me], device(y, p // 2, z, p % 2)
        )

    def q_recv(s):
        return remote(
            total.at[s], cols(gq, s, GW), q_s.at[s], q_r.at[s], device(y, s // 2, z, s % 2)
        )

    q_local = pltpu.make_async_copy(total.at[me], cols(gq, me, GW), q_l)
    q_local_direct = pltpu.make_async_copy(dq.at[0, me], cols(gq, me, GW), q_l)

    @pl.when(y != 2)
    def _():
        for p in slots[:-1]:
            q_copy(dq.at[0], p).start()
        q_local_direct.start()

    def add_cross(some):
        @pl.when(y == 2)
        def _():
            for s in some:
                cross_copy(s).wait_recv()
                total[s] = (dq[0, s].astype(F32) + land[s].astype(F32)).astype(BF16)
                if s is slots[-1]:
                    q_local.start()
                else:
                    q_copy(total, s).start()

    groups = ((), slots[0:2], slots[2:5], slots[5:8])
    for step in range(1, 4):
        for direction, piece, steps in CHAINS:
            if step < steps:
                sign = (1, NZ - 1)[direction]
                owner = (z + sign * (steps - step)) % NZ
                ring_copy(direction, piece, steps, step - 1).wait_recv()
                acc_out[direction, piece, step] = (
                    acc_in[direction, piece, step - 1].astype(F32)
                    + dkv[owner, piece].astype(F32)
                ).astype(BF16)
                ring_copy(direction, piece, steps, step).start()
        add_cross(groups[step])

    def kv_copy(piece, p):
        return remote(
            final.at[piece, p // 2, pl.ds((p % 2) * TOK, TOK), :],
            cols((gk, gv)[piece], me, HD),
            kv_s.at[piece, p], kv_r.at[piece, me], device(y, p // 2, z, p % 2),
        )

    def kv_recv(piece, s):
        return remote(
            final.at[piece, s // 2, pl.ds((s % 2) * TOK, TOK), :],
            cols((gk, gv)[piece], s, HD),
            kv_s.at[piece, s], kv_r.at[piece, s], device(y, s // 2, z, s % 2),
        )

    kv_local = []
    for piece in (0, 1):
        last = [(d, steps) for d, pc, steps in CHAINS if pc == piece]
        for direction, steps in last:
            ring_copy(direction, piece, steps, steps - 1).wait_recv()
        (d0, s0), (d1, s1) = last
        final[piece] = (
            acc_in[d0, piece, s0 - 1].astype(F32)
            + acc_in[d1, piece, s1 - 1].astype(F32)
            + dkv[z, piece].astype(F32)
        ).astype(BF16)
        for p in slots[:-1]:
            kv_copy(piece, p).start()
        local = pltpu.make_async_copy(
            final.at[piece, x, pl.ds(core * TOK, TOK), :], cols((gk, gv)[piece], me, HD), kv_l.at[piece]
        )
        local.start()
        kv_local.append(local)

    @pl.when(y == 1)
    def _():
        for s in slots:
            cross_copy(s).wait_send()

    for direction, piece, steps in CHAINS:
        for step in range(steps):
            ring_copy(direction, piece, steps, step).wait_send()
    for p in slots[:-1]:
        q_copy(total, p).wait_send()
        q_recv(p).wait_recv()
        for piece in (0, 1):
            kv_copy(piece, p).wait_send()
            kv_recv(piece, p).wait_recv()
    q_local.wait()
    for c in kv_local:
        c.wait()


def give(dq, dkv):
    vmem = pl.BlockSpec(memory_space=pltpu.VMEM)
    dma = pltpu.SemaphoreType.DMA
    return pl.pallas_call(
        give_kernel,
        out_shape=(
            jax.ShapeDtypeStruct((TOK, QH * HD), BF16),
            jax.ShapeDtypeStruct((TOK, KVH * HD), BF16),
            jax.ShapeDtypeStruct((TOK, KVH * HD), BF16),
        ),
        in_specs=[vmem] * 2,
        out_specs=(vmem,) * 3,
        scratch_shapes=[
            pltpu.VMEM((PEERS, TOK, GW), BF16),
            pltpu.VMEM((PEERS, TOK, GW), BF16),
            pltpu.VMEM((2, 2, 4, NX, PIECE, HD), BF16),
            pltpu.VMEM((2, 2, 4, NX, PIECE, HD), BF16),
            pltpu.VMEM((2, NX, PIECE, HD), BF16),
            dma((PEERS,)), dma((PEERS,)),
            dma((2, 2, 4)), dma((2, 2, 4)),
            dma((PEERS,)), dma((PEERS,)), dma,
            dma((2, PEERS)), dma((2, PEERS)), dma((2,)),
        ],
        compiler_params=pltpu.CompilerParams(collective_id=1, has_side_effects=True),
        name="give",
    )(dq, dkv)


def local(query_act, key_act, value_act, attn_out, grad_out, log_sum, kv_lists):
    qg, dog, stg, lsg, kvg = gather(
        query_act, key_act, value_act, attn_out, grad_out, log_sum, kv_lists
    )
    dq, dkv = attend(lsg, qg, dog, stg, kvg)
    return give(dq, dkv)


def solution(mesh):
    row = P(("blk", "head"), None)
    return jax.shard_map(
        local,
        mesh=mesh,
        in_specs=(row,) * 6 + (P("blk", None),),
        out_specs=(row,) * 3,
        check_vma=False,
    )
```

```python
import jax
import jax.numpy as jnp
from jax import lax
from jax.experimental import pallas as pl
from jax.experimental.pallas import tpu as pltpu
from jax.sharding import PartitionSpec as P

QH = 40
KVH = 8
HD = 128
BLOCK = 128
GS = QH // KVH
TOK = 32
GW = GS * HD
PIECE = 64
ROWS = GS * PIECE
NX = 4
NZ = 8
PEERS = 8
LISTW = 32
SCALE = HD ** -0.5
LOG2E = 1.4426950408889634
MESH = pl.DeviceIdType.MESH
F32 = jnp.float32
BF16 = jnp.bfloat16
NT = (((1,), (1,)), ((), ()))
NN = (((1,), (0,)), ((), ()))


def coords():
    blk = lax.axis_index("blk")
    head = lax.axis_index("head")
    y = blk // 8
    x = (blk // 2) % 4
    z = (blk % 2) * 4 + head // 2
    return y, x, z, head % 2


def device(y, x, z, core):
    return {"blk": (y * 4 + x) * 2 + z // 4, "head": (z % 4) * 2 + core}


def remote(src, dst, send_sem, recv_sem, device_id):
    return pltpu.make_async_remote_copy(
        src_ref=src,
        dst_ref=dst,
        send_sem=send_sem,
        recv_sem=recv_sem,
        device_id=device_id,
        device_id_type=MESH,
    )


def signal_group(bar, y, x, z, core, me):
    for d in range(1, PEERS):
        p = (me + d) % PEERS
        pl.semaphore_signal(bar, inc=1, device_id=device(y, p // 2, z, p % 2), device_id_type=MESH)
    for step in (1, NZ - 1):
        pl.semaphore_signal(
            bar, inc=1, device_id=device(y, x, (z + step) % NZ, core), device_id_type=MESH
        )
    cross = (y == 1) | (y == 2)

    @pl.when(cross)
    def _():
        pl.semaphore_signal(bar, inc=1, device_id=device(3 - y, x, z, core), device_id_type=MESH)

    pl.semaphore_wait(bar, PEERS - 1 + 2 + cross.astype(jnp.int32))


CHAINS = ((0, 0, 4), (0, 1, 3), (1, 1, 4), (1, 0, 3))


def gather_kernel(
    q, k, v, o, do, lse, lists,
    qg, dog, stg, lsg, kvg,
    stat_src, list_src,
    kv_s, kv_r, kv_l, big_s, big_r, big_l, st_s, st_r, st_l, ls_s, ls_r, ls_l,
    ring_s, ring_r, cr_s, cr_r, crst_s, crst_r, crls_s, crls_r,
):
    y, x, z, core = coords()
    me = x * 2 + core
    bar = pltpu.get_barrier_semaphore()
    signal_group(bar, y, x, z, core, me)

    def cols(ref, g, width):
        return ref.at[:, pl.ds(pl.multiple_of(g * width, 128), width)]

    def kv_slot(s, piece, zz):
        return kvg.at[zz, piece, s // 2, pl.ds((s % 2) * TOK, TOK), :]

    def kv_copy(d, piece):
        p = (me + d) % PEERS
        src = (k, v)[piece]
        return remote(
            cols(src, p, HD), kv_slot(me, piece, z),
            kv_s.at[piece, p], kv_r.at[piece, me], device(y, p // 2, z, p % 2),
        )

    def kv_recv(d, piece):
        s = (me + PEERS - d) % PEERS
        src = (k, v)[piece]
        return remote(
            cols(src, s, HD), kv_slot(s, piece, z),
            kv_s.at[piece, s], kv_r.at[piece, s], device(y, s // 2, z, s % 2),
        )

    def big_copy(d, which):
        p = (me + d) % PEERS
        src, dst = ((q, qg), (do, dog))[which]
        return remote(
            cols(src, p, GW), dst.at[0, me],
            big_s.at[which, p], big_r.at[which, me], device(y, p // 2, z, p % 2),
        )

    def big_recv(s, which):
        src, dst = ((q, qg), (do, dog))[which]
        return remote(
            cols(src, s, GW), dst.at[0, s],
            big_s.at[which, s], big_r.at[which, s], device(y, s // 2, z, s % 2),
        )

    def st_copy(d):
        p = (me + d) % PEERS
        return remote(
            stat_src.at[p], stg.at[0, me], st_s.at[p], st_r.at[me], device(y, p // 2, z, p % 2)
        )

    def st_recv(d):
        s = (me + PEERS - d) % PEERS
        return remote(
            stat_src.at[s], stg.at[0, s], st_s.at[s], st_r.at[s], device(y, s // 2, z, s % 2)
        )

    def ls_copy(d):
        xx = (x + d) % NX
        return remote(list_src, lsg.at[0, x], ls_s.at[xx], ls_r.at[x], device(y, xx, z, core))

    def ls_recv(d):
        xx = (x + NX - d) % NX
        return remote(list_src, lsg.at[0, xx], ls_s.at[xx], ls_r.at[xx], device(y, xx, z, core))

    order = (2, 3, 4, 5, 6, 7, 1)
    for piece in (0, 1):
        for d in order:
            kv_copy(d, piece).start()
    kv_local = [
        pltpu.make_async_copy(cols((k, v)[piece], me, HD), kv_slot(me, piece, z), kv_l.at[piece])
        for piece in (0, 1)
    ]
    big_local = [
        pltpu.make_async_copy(cols(q, me, GW), qg.at[0, me], big_l.at[0]),
        pltpu.make_async_copy(cols(do, me, GW), dog.at[0, me], big_l.at[1]),
    ]
    for c in kv_local + big_local:
        c.start()
    for d in order:
        for which in (0, 1):
            big_copy(d, which).start()

    rows = lists[...]
    count = jnp.sum(jnp.where(rows >= 0, 1.0, 0.0), axis=1, keepdims=True).astype(jnp.int32)
    early = jnp.sum(
        jnp.where((rows >= 0) & (rows < 32), 1.0, 0.0), axis=1, keepdims=True
    ).astype(jnp.int32)
    list_src[...] = jnp.zeros((8, 128), jnp.int32)
    list_src[0:2, 0:LISTW] = rows
    lane = lax.broadcasted_iota(jnp.int32, (2, 128), 1)
    list_src[4:6, :] = jnp.where(lane == 0, count, early)
    for d in range(1, NX):
        ls_copy(d).start()
    ls_local = pltpu.make_async_copy(list_src, lsg.at[0, x], ls_l)
    ls_local.start()

    lane = lax.broadcasted_iota(jnp.int32, (TOK, 128), 1)
    for g in range(KVH):
        block = jnp.zeros((TOK, 128), F32)
        for r in range(GS):
            h = g * GS + r
            own = slice(h * HD, (h + 1) * HD)
            delta = jnp.sum(do[:, own].astype(F32) * o[:, own].astype(F32), axis=1, keepdims=True)
            block = jnp.where(lane == r, lse[:, h : h + 1] * LOG2E, block)
            block = jnp.where(lane == 8 + r, delta, block)
        stat_src[g] = block
    for d in order:
        st_copy(d).start()
    st_local = pltpu.make_async_copy(stat_src.at[me], stg.at[0, me], st_l)
    st_local.start()

    def ring_copy(direction, piece, step):
        sign = (1, NZ - 1)[direction]
        back = (NZ - 1, 1)[direction]
        chunk = (z + back * step) % NZ
        part = kvg.at[chunk, piece]
        return remote(
            part, part, ring_s.at[direction, piece, step], ring_r.at[direction, piece, step],
            device(y, x, (z + sign) % NZ, core),
        )

    def ring_recv(direction, piece, step):
        back = (NZ - 1, 1)[direction]
        chunk = (z + back * (step + 1)) % NZ
        part = kvg.at[chunk, piece]
        return remote(
            part, part, ring_s.at[direction, piece, step], ring_r.at[direction, piece, step],
            device(y, x, (z + back) % NZ, core),
        )

    for piece in (0, 1):
        for d in range(1, PEERS):
            kv_recv(d, piece).wait_recv()
        kv_local[piece].wait()
        for direction in (0, 1):
            ring_copy(direction, piece, 0).start()

    def cross_copy(s, which):
        ref = (qg, dog)[which]
        return remote(
            ref.at[0, s], ref.at[1, s], cr_s.at[which, s], cr_r.at[which, s],
            device(3 - y, x, z, core),
        )

    for c in big_local:
        c.wait()

    @pl.when(y == 2)
    def _():
        for which in (0, 1):
            cross_copy(me, which).start()

    def forward(ds):
        for d in ds:
            s = (me + PEERS - d) % PEERS
            for which in (0, 1):
                big_recv(s, which).wait_recv()

            @pl.when(y == 2)
            def _():
                for which in (0, 1):
                    cross_copy(s, which).start()

    groups = ((7, 1), (2, 3), (4, 5, 6), ())
    for step in range(4):
        for direction, piece, steps in CHAINS:
            if step < steps:
                ring_recv(direction, piece, step).wait_recv()
                if step + 1 < steps:
                    ring_copy(direction, piece, step + 1).start()
        forward(groups[step])

    for d in range(1, PEERS):
        st_recv(d).wait_recv()
    for d in range(1, NX):
        ls_recv(d).wait_recv()
    st_local.wait()
    ls_local.wait()

    crst = remote(stg.at[0], stg.at[1], crst_s, crst_r, device(3 - y, x, z, core))
    crls = remote(lsg.at[0], lsg.at[1], crls_s, crls_r, device(3 - y, x, z, core))

    @pl.when(y == 2)
    def _():
        crst.start()
        crls.start()

    for d in range(1, PEERS):
        for i in (0, 1):
            kv_copy(d, i).wait_send()
            big_copy(d, i).wait_send()
        st_copy(d).wait_send()
    for d in range(1, NX):
        ls_copy(d).wait_send()
    for direction, piece, steps in CHAINS:
        for step in range(steps):
            ring_copy(direction, piece, step).wait_send()

    @pl.when(y == 2)
    def _():
        for s in range(PEERS):
            for which in (0, 1):
                cross_copy(s, which).wait_send()
        crst.wait_send()
        crls.wait_send()

    @pl.when(y == 1)
    def _():
        for s in range(PEERS):
            for which in (0, 1):
                cross_copy(s, which).wait_recv()
        crst.wait_recv()
        crls.wait_recv()


def gather(q, k, v, o, do, lse, lists):
    vmem = pl.BlockSpec(memory_space=pltpu.VMEM)
    dma = pltpu.SemaphoreType.DMA
    return pl.pallas_call(
        gather_kernel,
        out_shape=(
            jax.ShapeDtypeStruct((2, PEERS, TOK, GW), BF16),
            jax.ShapeDtypeStruct((2, PEERS, TOK, GW), BF16),
            jax.ShapeDtypeStruct((2, PEERS, TOK, 128), F32),
            jax.ShapeDtypeStruct((2, NX, 8, 128), jnp.int32),
            jax.ShapeDtypeStruct((NZ, 2, NX, PIECE, HD), BF16),
        ),
        in_specs=[vmem] * 7,
        out_specs=(vmem,) * 5,
        scratch_shapes=[
            pltpu.VMEM((KVH, TOK, 128), F32),
            pltpu.VMEM((8, 128), jnp.int32),
            dma((2, PEERS)), dma((2, PEERS)), dma((2,)),
            dma((2, PEERS)), dma((2, PEERS)), dma((2,)),
            dma((PEERS,)), dma((PEERS,)), dma,
            dma((NX,)), dma((NX,)), dma,
            dma((2, 2, 4)), dma((2, 2, 4)),
            dma((2, PEERS)), dma((2, PEERS)),
            dma, dma, dma, dma,
        ],
        compiler_params=pltpu.CompilerParams(collective_id=0, has_side_effects=True, vmem_limit_bytes=16 << 20),
        name="gather",
    )(q, k, v, o, do, lse, lists)


def attend_kernel(
    lists, qg, dog, stg, kvg, dq, dkv,
    qs, dos, qt, dot, lseb, delb, dqa, dka, dva,
):
    y, x, z, core = coords()
    half = (z % 4) // 2
    base = y * 16
    for ref in (dka, dva):
        ref[...] = jnp.zeros_like(ref)
    r_id = lax.broadcasted_iota(jnp.int32, (128, 128), 0)
    c_id = lax.broadcasted_iota(jnp.int32, (128, 128), 1)
    eye = jnp.where(r_id == c_id, 1.0, 0.0).astype(BF16)
    row_tok = (z % 2) * PIECE + lax.broadcasted_iota(jnp.int32, (ROWS, 128), 0) % PIECE
    key_tok = lax.broadcasted_iota(jnp.int32, (ROWS, 128), 1)

    def chunk(i, carry):
        part = i // NX
        xx = i % NX
        total = lists[part, xx, 4 + half, 0]
        early = lists[part, xx, 4 + half, 1]
        own = part == 0
        lo = jnp.where(own & (y == 2), early, 0)
        hi = jnp.where(own, total, jnp.where(y == 1, early, 0))
        n = hi - lo
        diag = jnp.where(own, xx * 4 + z // 2, -1)

        @pl.when(n > 0)
        def _():
            for c in range(2):
                st = stg[part, xx * 2 + c]
                for r in range(GS):
                    at = slice(r * PIECE + c * TOK, r * PIECE + (c + 1) * TOK)
                    col = slice(r * HD, (r + 1) * HD)
                    qs[at, :] = qg[part, xx * 2 + c, :, col]
                    dos[at, :] = dog[part, xx * 2 + c, :, col]
                    lseb[at, :] = jnp.broadcast_to(st[:, r : r + 1], (TOK, 128))
                    delb[at, :] = jnp.broadcast_to(st[:, 8 + r : 9 + r], (TOK, 128))
            qt[...] = lax.dot_general(eye, qs[...], NT, preferred_element_type=F32).astype(BF16)
            dot[...] = lax.dot_general(eye, dos[...], NT, preferred_element_type=F32).astype(BF16)
            dqa[...] = jnp.zeros_like(dqa)

            def block(piece, b):
                zz = (b % 4) * 2
                return jnp.concatenate(
                    [kvg[zz, piece, b // 4], kvg[zz + 1, piece, b // 4]], axis=0
                )

            def pair(j, masked):
                a = lists[part, xx, half, j] - base
                if masked:
                    has = j + 1 < hi
                    b = jnp.where(has, lists[part, xx, half, jnp.where(has, j + 1, j)] - base, a)
                else:
                    b = lists[part, xx, half, j + 1] - base
                keys = jnp.concatenate([block(0, a), block(0, b)], axis=0)
                values = jnp.concatenate([block(1, a), block(1, b)], axis=0)
                s = lax.dot_general(qs[...], keys, NT, preferred_element_type=F32)
                lse2 = jnp.concatenate([lseb[...], lseb[...]], axis=1)
                del2 = jnp.concatenate([delb[...], delb[...]], axis=1)
                p = jnp.exp2(s * (SCALE * LOG2E) - lse2)
                if masked:
                    ta = row_tok + jnp.where(a == diag, 0, BLOCK)
                    tb = row_tok + jnp.where(has, jnp.where(b == diag, 0, BLOCK), -2 * BLOCK)
                    seen = jnp.concatenate([key_tok <= ta, key_tok <= tb], axis=1)
                    p = jnp.where(seen, p, 0.0)
                dp = lax.dot_general(dos[...], values, NT, preferred_element_type=F32)
                ds = (p * (dp - del2)).astype(BF16)
                pb = p.astype(BF16)
                dvt = lax.dot_general(dot[...], pb, NN, preferred_element_type=F32)
                dkt = lax.dot_general(qt[...], ds, NN, preferred_element_type=F32)
                dqa[...] += lax.dot_general(ds, keys, NN, preferred_element_type=F32)
                dva[a] += dvt[:, :BLOCK]
                dka[a] += dkt[:, :BLOCK]
                dva[b] += dvt[:, BLOCK:]
                dka[b] += dkt[:, BLOCK:]

            full = (n - 1) // 2

            def step(t, carry):
                pair(lo + 2 * t, False)
                return carry

            lax.fori_loop(0, full, step, 0)
            pair(lo + 2 * full, True)
            for c in range(2):
                for r in range(GS):
                    at = slice(r * PIECE + c * TOK, r * PIECE + (c + 1) * TOK)
                    col = slice(r * HD, (r + 1) * HD)
                    dq[part, xx * 2 + c, :, col] = (dqa[at, :] * SCALE).astype(BF16)

        @pl.when((n <= 0) & (y == 1))
        def _():
            for c in range(2):
                dq[part, xx * 2 + c] = jnp.zeros((TOK, GW), BF16)

        return carry

    lax.fori_loop(0, jnp.where(y == 1, 2 * NX, NX), chunk, 0)

    def finish(b, carry):
        zz = (b % 4) * 2
        for piece, ref, scale in ((0, dka, SCALE), (1, dva, 1.0)):
            low = (ref[b] * scale).astype(BF16)
            out = lax.dot_general(eye, low, NT, preferred_element_type=F32).astype(BF16)
            dkv[zz, piece, b // 4] = out[:PIECE]
            dkv[zz + 1, piece, b // 4] = out[PIECE:]
        return carry

    lax.fori_loop(0, 16, finish, 0)


def attend(lists, qg, dog, stg, kvg):
    vmem = pl.BlockSpec(memory_space=pltpu.VMEM)
    return pl.pallas_call(
        attend_kernel,
        out_shape=(
            jax.ShapeDtypeStruct((2, PEERS, TOK, GW), BF16),
            jax.ShapeDtypeStruct((NZ, 2, NX, PIECE, HD), BF16),
        ),
        in_specs=[pl.BlockSpec(memory_space=pltpu.SMEM)] + [vmem] * 4,
        out_specs=(vmem, vmem),
        scratch_shapes=[
            pltpu.VMEM((ROWS, HD), BF16),
            pltpu.VMEM((ROWS, HD), BF16),
            pltpu.VMEM((HD, ROWS), BF16),
            pltpu.VMEM((HD, ROWS), BF16),
            pltpu.VMEM((ROWS, 128), F32),
            pltpu.VMEM((ROWS, 128), F32),
            pltpu.VMEM((ROWS, HD), F32),
            pltpu.VMEM((16, HD, BLOCK), F32),
            pltpu.VMEM((16, HD, BLOCK), F32),
        ],
        compiler_params=pltpu.CompilerParams(vmem_limit_bytes=16 << 20),
        name="attend",
    )(lists, qg, dog, stg, kvg)


def give_kernel(
    dq, dkv, gq, gk, gv,
    land, total, acc_in, acc_out, final,
    cr_s, cr_r, ring_s, ring_r, q_s, q_r, q_l, kv_s, kv_r, kv_l,
):
    y, x, z, core = coords()
    me = x * 2 + core
    bar = pltpu.get_barrier_semaphore()
    signal_group(bar, y, x, z, core, me)

    def cols(ref, g, width):
        return ref.at[:, pl.ds(pl.multiple_of(g * width, 128), width)]

    def cross_copy(s):
        return remote(dq.at[1, s], land.at[s], cr_s.at[s], cr_r.at[s], device(3 - y, x, z, core))

    slots = [(me + d) % PEERS for d in (2, 3, 4, 5, 6, 7, 1, 0)]

    @pl.when(y == 1)
    def _():
        for s in slots:
            cross_copy(s).start()

    def ring_copy(direction, piece, steps, step):
        sign = (1, NZ - 1)[direction]
        owner = (z + sign * (steps - step)) % NZ
        if step == 0:
            src = dkv.at[owner, piece]
        else:
            src = acc_out.at[direction, piece, step]
        return remote(
            src, acc_in.at[direction, piece, step],
            ring_s.at[direction, piece, step], ring_r.at[direction, piece, step],
            device(y, x, (z + sign) % NZ, core),
        )

    for direction, piece, steps in CHAINS:
        ring_copy(direction, piece, steps, 0).start()

    def q_copy(src, p):
        return remote(
            src.at[p], cols(gq, me, GW), q_s.at[p], q_r.at[me], device(y, p // 2, z, p % 2)
        )

    def q_recv(s):
        return remote(
            total.at[s], cols(gq, s, GW), q_s.at[s], q_r.at[s], device(y, s // 2, z, s % 2)
        )

    q_local = pltpu.make_async_copy(total.at[me], cols(gq, me, GW), q_l)
    q_local_direct = pltpu.make_async_copy(dq.at[0, me], cols(gq, me, GW), q_l)

    @pl.when(y != 2)
    def _():
        for p in slots[:-1]:
            q_copy(dq.at[0], p).start()
        q_local_direct.start()

    def add_cross(some):
        @pl.when(y == 2)
        def _():
            for s in some:
                cross_copy(s).wait_recv()
                total[s] = (dq[0, s].astype(F32) + land[s].astype(F32)).astype(BF16)
                if s is slots[-1]:
                    q_local.start()
                else:
                    q_copy(total, s).start()

    groups = ((), slots[0:2], slots[2:5], slots[5:8])
    for step in range(1, 4):
        for direction, piece, steps in CHAINS:
            if step < steps:
                sign = (1, NZ - 1)[direction]
                owner = (z + sign * (steps - step)) % NZ
                ring_copy(direction, piece, steps, step - 1).wait_recv()
                acc_out[direction, piece, step] = (
                    acc_in[direction, piece, step - 1].astype(F32)
                    + dkv[owner, piece].astype(F32)
                ).astype(BF16)
                ring_copy(direction, piece, steps, step).start()
        add_cross(groups[step])

    def kv_copy(piece, p):
        return remote(
            final.at[piece, p // 2, pl.ds((p % 2) * TOK, TOK), :],
            cols((gk, gv)[piece], me, HD),
            kv_s.at[piece, p], kv_r.at[piece, me], device(y, p // 2, z, p % 2),
        )

    def kv_recv(piece, s):
        return remote(
            final.at[piece, s // 2, pl.ds((s % 2) * TOK, TOK), :],
            cols((gk, gv)[piece], s, HD),
            kv_s.at[piece, s], kv_r.at[piece, s], device(y, s // 2, z, s % 2),
        )

    kv_local = []
    for piece in (0, 1):
        last = [(d, steps) for d, pc, steps in CHAINS if pc == piece]
        for direction, steps in last:
            ring_copy(direction, piece, steps, steps - 1).wait_recv()
        (d0, s0), (d1, s1) = last
        final[piece] = (
            acc_in[d0, piece, s0 - 1].astype(F32)
            + acc_in[d1, piece, s1 - 1].astype(F32)
            + dkv[z, piece].astype(F32)
        ).astype(BF16)
        for p in slots[:-1]:
            kv_copy(piece, p).start()
        local = pltpu.make_async_copy(
            final.at[piece, x, pl.ds(core * TOK, TOK), :], cols((gk, gv)[piece], me, HD), kv_l.at[piece]
        )
        local.start()
        kv_local.append(local)

    @pl.when(y == 1)
    def _():
        for s in slots:
            cross_copy(s).wait_send()

    for direction, piece, steps in CHAINS:
        for step in range(steps):
            ring_copy(direction, piece, steps, step).wait_send()
    for p in slots[:-1]:
        q_copy(total, p).wait_send()
        q_recv(p).wait_recv()
        for piece in (0, 1):
            kv_copy(piece, p).wait_send()
            kv_recv(piece, p).wait_recv()
    q_local.wait()
    for c in kv_local:
        c.wait()


def give(dq, dkv):
    vmem = pl.BlockSpec(memory_space=pltpu.VMEM)
    dma = pltpu.SemaphoreType.DMA
    return pl.pallas_call(
        give_kernel,
        out_shape=(
            jax.ShapeDtypeStruct((TOK, QH * HD), BF16),
            jax.ShapeDtypeStruct((TOK, KVH * HD), BF16),
            jax.ShapeDtypeStruct((TOK, KVH * HD), BF16),
        ),
        in_specs=[vmem] * 2,
        out_specs=(vmem,) * 3,
        scratch_shapes=[
            pltpu.VMEM((PEERS, TOK, GW), BF16),
            pltpu.VMEM((PEERS, TOK, GW), BF16),
            pltpu.VMEM((2, 2, 4, NX, PIECE, HD), BF16),
            pltpu.VMEM((2, 2, 4, NX, PIECE, HD), BF16),
            pltpu.VMEM((2, NX, PIECE, HD), BF16),
            dma((PEERS,)), dma((PEERS,)),
            dma((2, 2, 4)), dma((2, 2, 4)),
            dma((PEERS,)), dma((PEERS,)), dma,
            dma((2, PEERS)), dma((2, PEERS)), dma((2,)),
        ],
        compiler_params=pltpu.CompilerParams(collective_id=1, has_side_effects=True, vmem_limit_bytes=16 << 20),
        name="give",
    )(dq, dkv)


def local(query_act, key_act, value_act, attn_out, grad_out, log_sum, kv_lists):
    qg, dog, stg, lsg, kvg = gather(
        query_act, key_act, value_act, attn_out, grad_out, log_sum, kv_lists
    )
    dq, dkv = attend(lsg, qg, dog, stg, kvg)
    return give(dq, dkv)


def solution(mesh):
    row = P(("blk", "head"), None)
    return jax.shard_map(
        local,
        mesh=mesh,
        in_specs=(row,) * 6 + (P("blk", None),),
        out_specs=(row,) * 3,
        check_vma=False,
    )
```

```python
import jax
import jax.numpy as jnp
from jax import lax
from jax.experimental import pallas as pl
from jax.experimental.pallas import tpu as pltpu
from jax.sharding import PartitionSpec as P

QH = 40
KVH = 8
HD = 128
BLOCK = 128
GS = QH // KVH
TOK = 32
GW = GS * HD
PIECE = 64
ROWS = GS * PIECE
NX = 4
NZ = 8
PEERS = 8
LISTW = 32
SCALE = HD ** -0.5
LOG2E = 1.4426950408889634
MESH = pl.DeviceIdType.MESH
F32 = jnp.float32
BF16 = jnp.bfloat16
NT = (((1,), (1,)), ((), ()))
NN = (((1,), (0,)), ((), ()))


def coords():
    blk = lax.axis_index("blk")
    head = lax.axis_index("head")
    y = blk // 8
    x = (blk // 2) % 4
    z = (blk % 2) * 4 + head // 2
    return y, x, z, head % 2


def device(y, x, z, core):
    return {"blk": (y * 4 + x) * 2 + z // 4, "head": (z % 4) * 2 + core}


def remote(src, dst, send_sem, recv_sem, device_id):
    return pltpu.make_async_remote_copy(
        src_ref=src,
        dst_ref=dst,
        send_sem=send_sem,
        recv_sem=recv_sem,
        device_id=device_id,
        device_id_type=MESH,
    )


def signal_peers(bar, y, x, z, core, me):
    for d in range(1, PEERS):
        p = (me + d) % PEERS
        pl.semaphore_signal(bar, inc=1, device_id=device(y, p // 2, z, p % 2), device_id_type=MESH)
    for step in (1, NZ - 1):
        pl.semaphore_signal(
            bar, inc=1, device_id=device(y, x, (z + step) % NZ, core), device_id_type=MESH
        )

    @pl.when((y == 1) | (y == 2))
    def _():
        pl.semaphore_signal(bar, inc=1, device_id=device(3 - y, x, z, core), device_id_type=MESH)


def wait_peers(bar, y):
    pl.semaphore_wait(bar, PEERS - 1 + 2 + ((y == 1) | (y == 2)).astype(jnp.int32))


CHAINS = ((0, 0, 4), (0, 1, 3), (1, 1, 4), (1, 0, 3))


NEAR = ((0, 1), (1, 0), (3, 0), (1, 1), (3, 1), (2, 0), (2, 1))


def gather_kernel(
    q, k, v, o, do, lse, lists,
    qg, dog, stg, lsg, kvg,
    o_buf, do_buf, lse_buf, rows_buf, stat_src, list_src, in_sem,
    kv_s, kv_r, kv_l, big_s, big_r, big_l, st_s, st_r, st_l, ls_s, ls_r, ls_l,
    ring_s, ring_r, cr_s, cr_r, crst_s, crst_r, crls_s, crls_r,
):
    y, x, z, core = coords()
    me = x * 2 + core
    loads = [
        pltpu.make_async_copy(src, dst, in_sem.at[i])
        for i, (src, dst) in enumerate(
            ((lists, rows_buf), (lse, lse_buf), (do, do_buf), (o, o_buf))
        )
    ]
    for c in loads:
        c.start()
    bar = pltpu.get_barrier_semaphore()
    signal_peers(bar, y, x, z, core, me)

    def cols(ref, g, width):
        return ref.at[:, pl.ds(pl.multiple_of(g * width, 128), width)]

    def to(n):
        return ((x + n[0]) % NX) * 2 + (core + n[1]) % 2

    def of(n):
        return ((x + NX - n[0]) % NX) * 2 + (core + n[1]) % 2

    def at(p):
        return device(y, p // 2, z, p % 2)

    def kv_slot(s, piece, zz):
        return kvg.at[zz, piece, s // 2, pl.ds((s % 2) * TOK, TOK), :]

    def kv_copy(p, piece):
        return remote(
            cols((k, v)[piece], p, HD), kv_slot(me, piece, z),
            kv_s.at[piece, p], kv_r.at[piece, me], at(p),
        )

    def kv_recv(s, piece):
        return remote(
            cols((k, v)[piece], s, HD), kv_slot(s, piece, z),
            kv_s.at[piece, s], kv_r.at[piece, s], at(s),
        )

    def big_copy(p, which):
        src, dst = ((q, qg), (do, dog))[which]
        return remote(
            cols(src, p, GW), dst.at[0, me], big_s.at[which, p], big_r.at[which, me], at(p)
        )

    def big_recv(s, which):
        src, dst = ((q, qg), (do, dog))[which]
        return remote(
            cols(src, s, GW), dst.at[0, s], big_s.at[which, s], big_r.at[which, s], at(s)
        )

    def st_copy(p):
        return remote(stat_src.at[p], stg.at[0, me], st_s.at[p], st_r.at[me], at(p))

    def st_recv(s):
        return remote(stat_src.at[s], stg.at[0, s], st_s.at[s], st_r.at[s], at(s))

    def ls_copy(d):
        xx = (x + d) % NX
        return remote(list_src, lsg.at[0, x], ls_s.at[xx], ls_r.at[x], device(y, xx, z, core))

    def ls_recv(d):
        xx = (x + NX - d) % NX
        return remote(list_src, lsg.at[0, xx], ls_s.at[xx], ls_r.at[xx], device(y, xx, z, core))

    def cross_copy(s, which):
        ref = (qg, dog)[which]
        return remote(
            ref.at[0, s], ref.at[1, s], cr_s.at[which, s], cr_r.at[which, s],
            device(3 - y, x, z, core),
        )

    kv_local = [
        pltpu.make_async_copy(cols((k, v)[piece], me, HD), kv_slot(me, piece, z), kv_l.at[piece])
        for piece in (0, 1)
    ]
    big_local = [
        pltpu.make_async_copy(cols(q, me, GW), qg.at[0, me], big_l.at[0]),
        pltpu.make_async_copy(cols(do, me, GW), dog.at[0, me], big_l.at[1]),
    ]
    for c in kv_local + big_local:
        c.start()

    loads[0].wait()
    rows = rows_buf[...]
    count = jnp.sum(jnp.where(rows >= 0, 1.0, 0.0), axis=1, keepdims=True).astype(jnp.int32)
    early = jnp.sum(
        jnp.where((rows >= 0) & (rows < 32), 1.0, 0.0), axis=1, keepdims=True
    ).astype(jnp.int32)
    list_src[...] = jnp.zeros((8, 128), jnp.int32)
    list_src[0:2, 0:LISTW] = rows
    lane = lax.broadcasted_iota(jnp.int32, (2, 128), 1)
    list_src[4:6, :] = jnp.where(lane == 0, count, early)

    for c in loads[1:]:
        c.wait()
    lane = lax.broadcasted_iota(jnp.int32, (TOK, 128), 1)
    for g in range(KVH):
        block = jnp.zeros((TOK, 128), F32)
        for r in range(GS):
            h = g * GS + r
            own = slice(h * HD, (h + 1) * HD)
            delta = jnp.sum(
                do_buf[:, own].astype(F32) * o_buf[:, own].astype(F32), axis=1, keepdims=True
            )
            block = jnp.where(lane == r, lse_buf[:, h : h + 1] * LOG2E, block)
            block = jnp.where(lane == 8 + r, delta, block)
        stat_src[g] = block

    wait_peers(bar, y)
    for piece in (0, 1):
        for n in NEAR[1:] + NEAR[:1]:
            kv_copy(to(n), piece).start()
    for n in NEAR:
        for which in (0, 1):
            big_copy(to(n), which).start()
    for c in big_local:
        c.wait()

    @pl.when(y == 2)
    def _():
        for which in (0, 1):
            cross_copy(me, which).start()

    for n in NEAR:
        st_copy(to(n)).start()
    for d in range(1, NX):
        ls_copy(d).start()
    st_local = pltpu.make_async_copy(stat_src.at[me], stg.at[0, me], st_l)
    st_local.start()
    ls_local = pltpu.make_async_copy(list_src, lsg.at[0, x], ls_l)
    ls_local.start()

    def ring_copy(direction, piece, step):
        sign = (1, NZ - 1)[direction]
        back = (NZ - 1, 1)[direction]
        chunk = (z + back * step) % NZ
        part = kvg.at[chunk, piece]
        return remote(
            part, part, ring_s.at[direction, piece, step], ring_r.at[direction, piece, step],
            device(y, x, (z + sign) % NZ, core),
        )

    def ring_recv(direction, piece, step):
        back = (NZ - 1, 1)[direction]
        chunk = (z + back * (step + 1)) % NZ
        part = kvg.at[chunk, piece]
        return remote(
            part, part, ring_s.at[direction, piece, step], ring_r.at[direction, piece, step],
            device(y, x, (z + back) % NZ, core),
        )

    def forward(some):
        for n in some:
            s = of(n)
            for which in (0, 1):
                big_recv(s, which).wait_recv()

            @pl.when(y == 2)
            def _():
                for which in (0, 1):
                    cross_copy(s, which).start()

    def ring_start(piece):
        for n in NEAR:
            kv_recv(of(n), piece).wait_recv()
        kv_local[piece].wait()
        for direction in (0, 1):
            ring_copy(direction, piece, 0).start()

    def ring_step(step, piece):
        for direction, pc, steps in CHAINS:
            if pc == piece and step < steps:
                ring_recv(direction, piece, step).wait_recv()
                if step + 1 < steps:
                    ring_copy(direction, piece, step + 1).start()

    ring_start(0)
    ring_start(1)
    forward(NEAR[:3])
    ring_step(0, 0)
    forward(NEAR[3:4])
    ring_step(0, 1)
    forward(NEAR[4:5])
    ring_step(1, 0)
    forward(NEAR[5:6])
    ring_step(1, 1)
    forward(NEAR[6:])

    for n in NEAR:
        st_recv(of(n)).wait_recv()
    for d in range(1, NX):
        ls_recv(d).wait_recv()
    st_local.wait()
    ls_local.wait()

    crst = remote(stg.at[0], stg.at[1], crst_s, crst_r, device(3 - y, x, z, core))
    crls = remote(lsg.at[0], lsg.at[1], crls_s, crls_r, device(3 - y, x, z, core))

    @pl.when(y == 2)
    def _():
        crst.start()
        crls.start()

    for step in (2, 3):
        for piece in (0, 1):
            ring_step(step, piece)

    for n in NEAR:
        for i in (0, 1):
            kv_copy(to(n), i).wait_send()
            big_copy(to(n), i).wait_send()
        st_copy(to(n)).wait_send()
    for d in range(1, NX):
        ls_copy(d).wait_send()
    for direction, piece, steps in CHAINS:
        for step in range(steps):
            ring_copy(direction, piece, step).wait_send()

    @pl.when(y == 2)
    def _():
        for s in range(PEERS):
            for which in (0, 1):
                cross_copy(s, which).wait_send()
        crst.wait_send()
        crls.wait_send()

    @pl.when(y == 1)
    def _():
        for s in range(PEERS):
            for which in (0, 1):
                cross_copy(s, which).wait_recv()
        crst.wait_recv()
        crls.wait_recv()


def gather(q, k, v, o, do, lse, lists):
    vmem = pl.BlockSpec(memory_space=pltpu.VMEM)
    hbm = pl.BlockSpec(memory_space=pltpu.HBM)
    dma = pltpu.SemaphoreType.DMA
    return pl.pallas_call(
        gather_kernel,
        out_shape=(
            jax.ShapeDtypeStruct((2, PEERS, TOK, GW), BF16),
            jax.ShapeDtypeStruct((2, PEERS, TOK, GW), BF16),
            jax.ShapeDtypeStruct((2, PEERS, TOK, 128), F32),
            jax.ShapeDtypeStruct((2, NX, 8, 128), jnp.int32),
            jax.ShapeDtypeStruct((NZ, 2, NX, PIECE, HD), BF16),
        ),
        in_specs=[hbm] * 7,
        out_specs=(vmem,) * 5,
        scratch_shapes=[
            pltpu.VMEM((TOK, QH * HD), BF16),
            pltpu.VMEM((TOK, QH * HD), BF16),
            pltpu.VMEM((TOK, QH), F32),
            pltpu.VMEM((2, LISTW), jnp.int32),
            pltpu.VMEM((KVH, TOK, 128), F32),
            pltpu.VMEM((8, 128), jnp.int32),
            dma((4,)),
            dma((2, PEERS)), dma((2, PEERS)), dma((2,)),
            dma((2, PEERS)), dma((2, PEERS)), dma((2,)),
            dma((PEERS,)), dma((PEERS,)), dma,
            dma((NX,)), dma((NX,)), dma,
            dma((2, 2, 4)), dma((2, 2, 4)),
            dma((2, PEERS)), dma((2, PEERS)),
            dma, dma, dma, dma,
        ],
        compiler_params=pltpu.CompilerParams(
            collective_id=0, has_side_effects=True, vmem_limit_bytes=16 << 20
        ),
        name="gather",
    )(q, k, v, o, do, lse, lists)


def attend_kernel(
    lists, qg, dog, stg, kvg, dq, dkv,
    qs, dos, qt, dot, lseb, delb, dqa, dka, dva,
):
    y, x, z, core = coords()
    half = (z % 4) // 2
    base = y * 16
    for ref in (dka, dva):
        ref[...] = jnp.zeros_like(ref)
    r_id = lax.broadcasted_iota(jnp.int32, (128, 128), 0)
    c_id = lax.broadcasted_iota(jnp.int32, (128, 128), 1)
    eye = jnp.where(r_id == c_id, 1.0, 0.0).astype(BF16)
    row_tok = (z % 2) * PIECE + lax.broadcasted_iota(jnp.int32, (ROWS, 128), 0) % PIECE
    key_tok = lax.broadcasted_iota(jnp.int32, (ROWS, 128), 1)

    def chunk(i, carry):
        part = i // NX
        xx = i % NX
        total = lists[part, xx, 4 + half, 0]
        early = lists[part, xx, 4 + half, 1]
        own = part == 0
        lo = jnp.where(own & (y == 2), early, 0)
        hi = jnp.where(own, total, jnp.where(y == 1, early, 0))
        n = hi - lo
        diag = jnp.where(own, xx * 4 + z // 2, -1)

        @pl.when(n > 0)
        def _():
            for c in range(2):
                st = stg[part, xx * 2 + c]
                for r in range(GS):
                    at = slice(r * PIECE + c * TOK, r * PIECE + (c + 1) * TOK)
                    col = slice(r * HD, (r + 1) * HD)
                    qs[at, :] = qg[part, xx * 2 + c, :, col]
                    dos[at, :] = dog[part, xx * 2 + c, :, col]
                    lseb[at, :] = jnp.broadcast_to(st[:, r : r + 1], (TOK, 128))
                    delb[at, :] = jnp.broadcast_to(st[:, 8 + r : 9 + r], (TOK, 128))
            qt[...] = lax.dot_general(eye, qs[...], NT, preferred_element_type=F32).astype(BF16)
            dot[...] = lax.dot_general(eye, dos[...], NT, preferred_element_type=F32).astype(BF16)
            dqa[...] = jnp.zeros_like(dqa)

            def block(piece, b):
                zz = (b % 4) * 2
                return jnp.concatenate(
                    [kvg[zz, piece, b // 4], kvg[zz + 1, piece, b // 4]], axis=0
                )

            def pair(j, masked):
                a = lists[part, xx, half, j] - base
                if masked:
                    has = j + 1 < hi
                    b = jnp.where(has, lists[part, xx, half, jnp.where(has, j + 1, j)] - base, a)
                else:
                    b = lists[part, xx, half, j + 1] - base
                keys = jnp.concatenate([block(0, a), block(0, b)], axis=0)
                values = jnp.concatenate([block(1, a), block(1, b)], axis=0)
                s = lax.dot_general(qs[...], keys, NT, preferred_element_type=F32)
                lse2 = jnp.concatenate([lseb[...], lseb[...]], axis=1)
                del2 = jnp.concatenate([delb[...], delb[...]], axis=1)
                p = jnp.exp2(s * (SCALE * LOG2E) - lse2)
                if masked:
                    ta = row_tok + jnp.where(a == diag, 0, BLOCK)
                    tb = row_tok + jnp.where(has, jnp.where(b == diag, 0, BLOCK), -2 * BLOCK)
                    seen = jnp.concatenate([key_tok <= ta, key_tok <= tb], axis=1)
                    p = jnp.where(seen, p, 0.0)
                dp = lax.dot_general(dos[...], values, NT, preferred_element_type=F32)
                ds = (p * (dp - del2)).astype(BF16)
                pb = p.astype(BF16)
                dvt = lax.dot_general(dot[...], pb, NN, preferred_element_type=F32)
                dkt = lax.dot_general(qt[...], ds, NN, preferred_element_type=F32)
                dqa[...] += lax.dot_general(ds, keys, NN, preferred_element_type=F32)
                dva[a] += dvt[:, :BLOCK]
                dka[a] += dkt[:, :BLOCK]
                dva[b] += dvt[:, BLOCK:]
                dka[b] += dkt[:, BLOCK:]

            full = (n - 1) // 2

            def step(t, carry):
                pair(lo + 2 * t, False)
                return carry

            lax.fori_loop(0, full, step, 0)
            pair(lo + 2 * full, True)
            for c in range(2):
                for r in range(GS):
                    at = slice(r * PIECE + c * TOK, r * PIECE + (c + 1) * TOK)
                    col = slice(r * HD, (r + 1) * HD)
                    dq[part, xx * 2 + c, :, col] = (dqa[at, :] * SCALE).astype(BF16)

        @pl.when((n <= 0) & (y == 1))
        def _():
            for c in range(2):
                dq[part, xx * 2 + c] = jnp.zeros((TOK, GW), BF16)

        return carry

    lax.fori_loop(0, jnp.where(y == 1, 2 * NX, NX), chunk, 0)

    def finish(b, carry):
        zz = (b % 4) * 2
        for piece, ref, scale in ((0, dka, SCALE), (1, dva, 1.0)):
            low = (ref[b] * scale).astype(BF16)
            out = lax.dot_general(eye, low, NT, preferred_element_type=F32).astype(BF16)
            dkv[zz, piece, b // 4] = out[:PIECE]
            dkv[zz + 1, piece, b // 4] = out[PIECE:]
        return carry

    lax.fori_loop(0, 16, finish, 0)


def attend(lists, qg, dog, stg, kvg):
    vmem = pl.BlockSpec(memory_space=pltpu.VMEM)
    return pl.pallas_call(
        attend_kernel,
        out_shape=(
            jax.ShapeDtypeStruct((2, PEERS, TOK, GW), BF16),
            jax.ShapeDtypeStruct((NZ, 2, NX, PIECE, HD), BF16),
        ),
        in_specs=[pl.BlockSpec(memory_space=pltpu.SMEM)] + [vmem] * 4,
        out_specs=(vmem, vmem),
        scratch_shapes=[
            pltpu.VMEM((ROWS, HD), BF16),
            pltpu.VMEM((ROWS, HD), BF16),
            pltpu.VMEM((HD, ROWS), BF16),
            pltpu.VMEM((HD, ROWS), BF16),
            pltpu.VMEM((ROWS, 128), F32),
            pltpu.VMEM((ROWS, 128), F32),
            pltpu.VMEM((ROWS, HD), F32),
            pltpu.VMEM((16, HD, BLOCK), F32),
            pltpu.VMEM((16, HD, BLOCK), F32),
        ],
        compiler_params=pltpu.CompilerParams(vmem_limit_bytes=16 << 20),
        name="attend",
    )(lists, qg, dog, stg, kvg)


def give_kernel(
    dq, dkv, gq, gk, gv,
    land, total, acc_in, acc_out, final,
    cr_s, cr_r, ring_s, ring_r, q_s, q_r, q_l, kv_s, kv_r, kv_l,
):
    y, x, z, core = coords()
    me = x * 2 + core
    bar = pltpu.get_barrier_semaphore()
    signal_peers(bar, y, x, z, core, me)
    wait_peers(bar, y)

    def cols(ref, g, width):
        return ref.at[:, pl.ds(pl.multiple_of(g * width, 128), width)]

    def cross_copy(s):
        return remote(dq.at[1, s], land.at[s], cr_s.at[s], cr_r.at[s], device(3 - y, x, z, core))

    slots = [(me + d) % PEERS for d in (2, 3, 4, 5, 6, 7, 1, 0)]

    @pl.when(y == 1)
    def _():
        for s in slots:
            cross_copy(s).start()

    def ring_copy(direction, piece, steps, step):
        sign = (1, NZ - 1)[direction]
        owner = (z + sign * (steps - step)) % NZ
        if step == 0:
            src = dkv.at[owner, piece]
        else:
            src = acc_out.at[direction, piece, step]
        return remote(
            src, acc_in.at[direction, piece, step],
            ring_s.at[direction, piece, step], ring_r.at[direction, piece, step],
            device(y, x, (z + sign) % NZ, core),
        )

    for direction, piece, steps in CHAINS:
        ring_copy(direction, piece, steps, 0).start()

    def q_copy(src, p):
        return remote(
            src.at[p], cols(gq, me, GW), q_s.at[p], q_r.at[me], device(y, p // 2, z, p % 2)
        )

    def q_recv(s):
        return remote(
            total.at[s], cols(gq, s, GW), q_s.at[s], q_r.at[s], device(y, s // 2, z, s % 2)
        )

    q_local = pltpu.make_async_copy(total.at[me], cols(gq, me, GW), q_l)
    q_local_direct = pltpu.make_async_copy(dq.at[0, me], cols(gq, me, GW), q_l)

    @pl.when(y != 2)
    def _():
        for p in slots[:-1]:
            q_copy(dq.at[0], p).start()
        q_local_direct.start()

    def add_cross(some):
        @pl.when(y == 2)
        def _():
            for s in some:
                cross_copy(s).wait_recv()
                total[s] = (dq[0, s].astype(F32) + land[s].astype(F32)).astype(BF16)
                if s is slots[-1]:
                    q_local.start()
                else:
                    q_copy(total, s).start()

    groups = ((), slots[0:2], slots[2:5], slots[5:8])
    for step in range(1, 4):
        for direction, piece, steps in CHAINS:
            if step < steps:
                sign = (1, NZ - 1)[direction]
                owner = (z + sign * (steps - step)) % NZ
                ring_copy(direction, piece, steps, step - 1).wait_recv()
                acc_out[direction, piece, step] = (
                    acc_in[direction, piece, step - 1].astype(F32)
                    + dkv[owner, piece].astype(F32)
                ).astype(BF16)
                ring_copy(direction, piece, steps, step).start()
        add_cross(groups[step])

    def kv_copy(piece, p):
        return remote(
            final.at[piece, p // 2, pl.ds((p % 2) * TOK, TOK), :],
            cols((gk, gv)[piece], me, HD),
            kv_s.at[piece, p], kv_r.at[piece, me], device(y, p // 2, z, p % 2),
        )

    def kv_recv(piece, s):
        return remote(
            final.at[piece, s // 2, pl.ds((s % 2) * TOK, TOK), :],
            cols((gk, gv)[piece], s, HD),
            kv_s.at[piece, s], kv_r.at[piece, s], device(y, s // 2, z, s % 2),
        )

    kv_local = []
    for piece in (0, 1):
        last = [(d, steps) for d, pc, steps in CHAINS if pc == piece]
        for direction, steps in last:
            ring_copy(direction, piece, steps, steps - 1).wait_recv()
        (d0, s0), (d1, s1) = last
        final[piece] = (
            acc_in[d0, piece, s0 - 1].astype(F32)
            + acc_in[d1, piece, s1 - 1].astype(F32)
            + dkv[z, piece].astype(F32)
        ).astype(BF16)
        for p in slots[:-1]:
            kv_copy(piece, p).start()
        local = pltpu.make_async_copy(
            final.at[piece, x, pl.ds(core * TOK, TOK), :], cols((gk, gv)[piece], me, HD), kv_l.at[piece]
        )
        local.start()
        kv_local.append(local)

    @pl.when(y == 1)
    def _():
        for s in slots:
            cross_copy(s).wait_send()

    for direction, piece, steps in CHAINS:
        for step in range(steps):
            ring_copy(direction, piece, steps, step).wait_send()
    for p in slots[:-1]:
        q_copy(total, p).wait_send()
        q_recv(p).wait_recv()
        for piece in (0, 1):
            kv_copy(piece, p).wait_send()
            kv_recv(piece, p).wait_recv()
    q_local.wait()
    for c in kv_local:
        c.wait()


def give(dq, dkv):
    vmem = pl.BlockSpec(memory_space=pltpu.VMEM)
    dma = pltpu.SemaphoreType.DMA
    return pl.pallas_call(
        give_kernel,
        out_shape=(
            jax.ShapeDtypeStruct((TOK, QH * HD), BF16),
            jax.ShapeDtypeStruct((TOK, KVH * HD), BF16),
            jax.ShapeDtypeStruct((TOK, KVH * HD), BF16),
        ),
        in_specs=[vmem] * 2,
        out_specs=(vmem,) * 3,
        scratch_shapes=[
            pltpu.VMEM((PEERS, TOK, GW), BF16),
            pltpu.VMEM((PEERS, TOK, GW), BF16),
            pltpu.VMEM((2, 2, 4, NX, PIECE, HD), BF16),
            pltpu.VMEM((2, 2, 4, NX, PIECE, HD), BF16),
            pltpu.VMEM((2, NX, PIECE, HD), BF16),
            dma((PEERS,)), dma((PEERS,)),
            dma((2, 2, 4)), dma((2, 2, 4)),
            dma((PEERS,)), dma((PEERS,)), dma,
            dma((2, PEERS)), dma((2, PEERS)), dma((2,)),
        ],
        compiler_params=pltpu.CompilerParams(collective_id=1, has_side_effects=True, vmem_limit_bytes=16 << 20),
        name="give",
    )(dq, dkv)


def local(query_act, key_act, value_act, attn_out, grad_out, log_sum, kv_lists):
    args = (query_act, key_act, value_act, attn_out, grad_out, log_sum, kv_lists)
    qg, dog, stg, lsg, kvg = gather(
        *(pltpu.with_memory_space_constraint(a, pltpu.HBM) for a in args)
    )
    dq, dkv = attend(lsg, qg, dog, stg, kvg)
    return give(dq, dkv)


def solution(mesh):
    row = P(("blk", "head"), None)
    return jax.shard_map(
        local,
        mesh=mesh,
        in_specs=(row,) * 6 + (P("blk", None),),
        out_specs=(row,) * 3,
        check_vma=False,
    )
```

```python
import jax
import jax.numpy as jnp
from jax import lax
from jax.experimental import pallas as pl
from jax.experimental.pallas import tpu as pltpu
from jax.sharding import PartitionSpec as P

QH = 40
KVH = 8
HD = 128
BLOCK = 128
GS = QH // KVH
TOK = 32
GW = GS * HD
PIECE = 64
ROWS = GS * PIECE
NX = 4
NZ = 8
PEERS = 8
LISTW = 32
SCALE = HD ** -0.5
LOG2E = 1.4426950408889634
MESH = pl.DeviceIdType.MESH
F32 = jnp.float32
BF16 = jnp.bfloat16
NT = (((1,), (1,)), ((), ()))
NN = (((1,), (0,)), ((), ()))


def coords():
    blk = lax.axis_index("blk")
    head = lax.axis_index("head")
    y = blk // 8
    x = (blk // 2) % 4
    z = (blk % 2) * 4 + head // 2
    return y, x, z, head % 2


def device(y, x, z, core):
    return {"blk": (y * 4 + x) * 2 + z // 4, "head": (z % 4) * 2 + core}


def remote(src, dst, send_sem, recv_sem, device_id):
    return pltpu.make_async_remote_copy(
        src_ref=src,
        dst_ref=dst,
        send_sem=send_sem,
        recv_sem=recv_sem,
        device_id=device_id,
        device_id_type=MESH,
    )


def signal_peers(bar, y, x, z, core, me):
    for d in range(1, PEERS):
        p = (me + d) % PEERS
        pl.semaphore_signal(bar, inc=1, device_id=device(y, p // 2, z, p % 2), device_id_type=MESH)
    for step in (1, NZ - 1):
        pl.semaphore_signal(
            bar, inc=1, device_id=device(y, x, (z + step) % NZ, core), device_id_type=MESH
        )

    @pl.when((y == 1) | (y == 2))
    def _():
        pl.semaphore_signal(bar, inc=1, device_id=device(3 - y, x, z, core), device_id_type=MESH)


def wait_peers(bar, y):
    pl.semaphore_wait(bar, PEERS - 1 + 2 + ((y == 1) | (y == 2)).astype(jnp.int32))


CHAINS = ((0, 0, 4), (0, 1, 3), (1, 1, 4), (1, 0, 3))


BIG = 1e30
ALLROWS = NX * ROWS


def rows_of(x):
    return slice(x * ROWS, (x + 1) * ROWS)


def seen_bias(lists, part, x, half, base):
    entries = lists[part, x, pl.ds(half, 1), :]
    block = base + lax.broadcasted_iota(jnp.int32, (16, 128), 0)
    hit = jnp.max(jnp.where(entries == block, 1.0, 0.0), axis=1, keepdims=True)
    return jnp.broadcast_to(hit, (16, 128))


def load_rows(x, part, qg, dog, stg, eye, qs, dos, qt, dot, lseb, delb):
    for c in range(2):
        st = stg[part, x * 2 + c]
        for r in range(GS):
            start = x * ROWS + r * PIECE + c * TOK
            at = slice(start, start + TOK)
            col = slice(r * HD, (r + 1) * HD)
            qs[at, :] = qg[part, x * 2 + c, :, col]
            dos[at, :] = dog[part, x * 2 + c, :, col]
            lseb[at, :] = jnp.broadcast_to(st[:, r : r + 1], (TOK, 128))
            delb[at, :] = jnp.broadcast_to(st[:, 8 + r : 9 + r], (TOK, 128))


def turn_rows(lo, hi, eye, qs, dos, qt, dot):
    at = slice(lo * ROWS, hi * ROWS)
    qt[:, at] = lax.dot_general(eye, qs[at, :], NT, preferred_element_type=F32).astype(BF16)
    dot[:, at] = lax.dot_general(eye, dos[at, :], NT, preferred_element_type=F32).astype(BF16)


def identity():
    r_id = lax.broadcasted_iota(jnp.int32, (128, 128), 0)
    c_id = lax.broadcasted_iota(jnp.int32, (128, 128), 1)
    return jnp.where(r_id == c_id, 1.0, 0.0).astype(BF16)


def key_block(kvg, piece, b):
    zz = (b % 4) * 2
    return jnp.concatenate([kvg[zz, piece, b // 4], kvg[zz + 1, piece, b // 4]], axis=0)


def tile(xs, a, b, kvg, bias, diag, qs, dos, qt, dot, lseb, delb, pbuf, dsbuf, dqa, dka, dva):
    keys = jnp.concatenate([key_block(kvg, 0, a), key_block(kvg, 0, b)], axis=0)
    values = jnp.concatenate([key_block(kvg, 1, a), key_block(kvg, 1, b)], axis=0)
    for x in xs:
        at = rows_of(x)
        s = lax.dot_general(qs[at, :], keys, NT, preferred_element_type=F32)
        dp = lax.dot_general(dos[at, :], values, NT, preferred_element_type=F32)
        lse_a = lseb[at, :] + bias[x, pl.ds(a, 1), :]
        lse_b = lseb[at, :] + bias[x, pl.ds(b, 1), :]
        if diag is not None:
            if x % 2 == 0 and x == xs[0]:
                lse_a = lse_a + diag[...]
            if x % 2 == 1 and x == xs[0] + 1:
                lse_b = lse_b + diag[...]
        p = jnp.exp2(s * (SCALE * LOG2E) - jnp.concatenate([lse_a, lse_b], axis=1))
        delta = delb[at, :]
        ds = (p * (dp - jnp.concatenate([delta, delta], axis=1))).astype(BF16)
        pbuf[at, :] = p.astype(BF16)
        dsbuf[at, :] = ds
        dqa[at, :] += lax.dot_general(ds, keys, NN, preferred_element_type=F32)
    at = slice(xs[0] * ROWS, (xs[-1] + 1) * ROWS)
    dvt = lax.dot_general(dot[:, at], pbuf[at, :], NN, preferred_element_type=F32)
    dkt = lax.dot_general(qt[:, at], dsbuf[at, :], NN, preferred_element_type=F32)
    dva[a] += dvt[:, :BLOCK]
    dka[a] += dkt[:, :BLOCK]
    dva[b] += dvt[:, BLOCK:]
    dka[b] += dkt[:, BLOCK:]


def put_dq(dq, dqa):
    for x in range(NX):
        for c in range(2):
            for r in range(GS):
                start = x * ROWS + r * PIECE + c * TOK
                dq[x * 2 + c, :, r * HD : (r + 1) * HD] = (
                    dqa[start : start + TOK, :] * SCALE
                ).astype(BF16)


TILE_SCRATCH = [
    pltpu.VMEM((ALLROWS, HD), BF16),
    pltpu.VMEM((ALLROWS, HD), BF16),
    pltpu.VMEM((HD, ALLROWS), BF16),
    pltpu.VMEM((HD, ALLROWS), BF16),
    pltpu.VMEM((ALLROWS, 128), F32),
    pltpu.VMEM((ALLROWS, 128), F32),
    pltpu.VMEM((ALLROWS, 2 * BLOCK), BF16),
    pltpu.VMEM((ALLROWS, 2 * BLOCK), BF16),
    pltpu.VMEM((ALLROWS, HD), F32),
]


NEAR = ((0, 1), (1, 0), (3, 0), (1, 1), (3, 1), (2, 0), (2, 1))


def gather_kernel(
    q, k, v, o, do, lse, lists,
    qg, dog, stg, kvg, dq, dka, dva, far_bias, far_any,
    o_buf, do_buf, lse_buf, rows_buf, stat_src, list_src, lsg, bias, diag,
    qs, dos, qt, dot, lseb, delb, pbuf, dsbuf, dqa, in_sem,
    kv_s, kv_r, kv_l, big_s, big_r, big_l, st_s, st_r, st_l, ls_s, ls_r, ls_l,
    ring_s, ring_r, cr_s, cr_r, crst_s, crst_r, crls_s, crls_r,
):
    y, x, z, core = coords()
    me = x * 2 + core
    loads = [
        pltpu.make_async_copy(src, dst, in_sem.at[i])
        for i, (src, dst) in enumerate(
            ((lists, rows_buf), (lse, lse_buf), (do, do_buf), (o, o_buf))
        )
    ]
    for c in loads:
        c.start()
    bar = pltpu.get_barrier_semaphore()
    signal_peers(bar, y, x, z, core, me)

    def cols(ref, g, width):
        return ref.at[:, pl.ds(pl.multiple_of(g * width, 128), width)]

    def to(n):
        return ((x + n[0]) % NX) * 2 + (core + n[1]) % 2

    def of(n):
        return ((x + NX - n[0]) % NX) * 2 + (core + n[1]) % 2

    def at(p):
        return device(y, p // 2, z, p % 2)

    def kv_slot(s, piece, zz):
        return kvg.at[zz, piece, s // 2, pl.ds((s % 2) * TOK, TOK), :]

    def kv_copy(p, piece):
        return remote(
            cols((k, v)[piece], p, HD), kv_slot(me, piece, z),
            kv_s.at[piece, p], kv_r.at[piece, me], at(p),
        )

    def kv_recv(s, piece):
        return remote(
            cols((k, v)[piece], s, HD), kv_slot(s, piece, z),
            kv_s.at[piece, s], kv_r.at[piece, s], at(s),
        )

    def big_copy(p, which):
        src, dst = ((q, qg), (do, dog))[which]
        return remote(
            cols(src, p, GW), dst.at[0, me], big_s.at[which, p], big_r.at[which, me], at(p)
        )

    def big_recv(s, which):
        src, dst = ((q, qg), (do, dog))[which]
        return remote(
            cols(src, s, GW), dst.at[0, s], big_s.at[which, s], big_r.at[which, s], at(s)
        )

    def st_copy(p):
        return remote(stat_src.at[p], stg.at[0, me], st_s.at[p], st_r.at[me], at(p))

    def st_recv(s):
        return remote(stat_src.at[s], stg.at[0, s], st_s.at[s], st_r.at[s], at(s))

    def ls_copy(d):
        xx = (x + d) % NX
        return remote(list_src, lsg.at[0, x], ls_s.at[xx], ls_r.at[x], device(y, xx, z, core))

    def ls_recv(d):
        xx = (x + NX - d) % NX
        return remote(list_src, lsg.at[0, xx], ls_s.at[xx], ls_r.at[xx], device(y, xx, z, core))

    def cross_copy(s, which):
        ref = (qg, dog)[which]
        return remote(
            ref.at[0, s], ref.at[1, s], cr_s.at[which, s], cr_r.at[which, s],
            device(3 - y, x, z, core),
        )

    kv_local = [
        pltpu.make_async_copy(cols((k, v)[piece], me, HD), kv_slot(me, piece, z), kv_l.at[piece])
        for piece in (0, 1)
    ]
    big_local = [
        pltpu.make_async_copy(cols(q, me, GW), qg.at[0, me], big_l.at[0]),
        pltpu.make_async_copy(cols(do, me, GW), dog.at[0, me], big_l.at[1]),
    ]
    for c in kv_local + big_local:
        c.start()

    loads[0].wait()
    list_src[...] = jnp.full((8, 128), -1, jnp.int32)
    list_src[0:2, 0:LISTW] = rows_buf[...]

    for c in loads[1:]:
        c.wait()
    lane = lax.broadcasted_iota(jnp.int32, (TOK, 128), 1)
    for g in range(KVH):
        block = jnp.zeros((TOK, 128), F32)
        for r in range(GS):
            h = g * GS + r
            own = slice(h * HD, (h + 1) * HD)
            delta = jnp.sum(
                do_buf[:, own].astype(F32) * o_buf[:, own].astype(F32), axis=1, keepdims=True
            )
            block = jnp.where(lane == r, lse_buf[:, h : h + 1] * LOG2E, block)
            block = jnp.where(lane == 8 + r, delta, block)
        stat_src[g] = block

    for ref in (dka, dva, dqa):
        ref[...] = jnp.zeros_like(ref)
    eye = identity()
    half = (z % 4) // 2
    base = y * 16
    row_tok = (z % 2) * PIECE + lax.broadcasted_iota(jnp.int32, (ROWS, 128), 0) % PIECE
    key_tok = lax.broadcasted_iota(jnp.int32, (ROWS, 128), 1)
    diag[0] = jnp.where(key_tok <= row_tok, 0.0, BIG)
    diag[1] = jnp.zeros((ROWS, 128), F32)

    wait_peers(bar, y)
    for piece in (0, 1):
        for n in NEAR[1:] + NEAR[:1]:
            kv_copy(to(n), piece).start()
    for n in NEAR:
        for which in (0, 1):
            big_copy(to(n), which).start()
    for c in big_local:
        c.wait()

    @pl.when(y == 2)
    def _():
        for which in (0, 1):
            cross_copy(me, which).start()

    for n in NEAR:
        st_copy(to(n)).start()
    for d in range(1, NX):
        ls_copy(d).start()
    st_local = pltpu.make_async_copy(stat_src.at[me], stg.at[0, me], st_l)
    st_local.start()
    ls_local = pltpu.make_async_copy(list_src, lsg.at[0, x], ls_l)
    ls_local.start()

    def ring_copy(direction, piece, step):
        sign = (1, NZ - 1)[direction]
        back = (NZ - 1, 1)[direction]
        chunk = (z + back * step) % NZ
        part = kvg.at[chunk, piece]
        return remote(
            part, part, ring_s.at[direction, piece, step], ring_r.at[direction, piece, step],
            device(y, x, (z + sign) % NZ, core),
        )

    def ring_recv(direction, piece, step):
        back = (NZ - 1, 1)[direction]
        chunk = (z + back * (step + 1)) % NZ
        part = kvg.at[chunk, piece]
        return remote(
            part, part, ring_s.at[direction, piece, step], ring_r.at[direction, piece, step],
            device(y, x, (z + back) % NZ, core),
        )

    def forward(some):
        for n in some:
            s = of(n)
            for which in (0, 1):
                big_recv(s, which).wait_recv()

            @pl.when(y == 2)
            def _():
                for which in (0, 1):
                    cross_copy(s, which).start()

    def ring_start(piece):
        for n in NEAR:
            kv_recv(of(n), piece).wait_recv()
        kv_local[piece].wait()
        for direction in (0, 1):
            ring_copy(direction, piece, 0).start()

    def ring_step(step, piece):
        for direction, pc, steps in CHAINS:
            if pc == piece and step < steps:
                ring_recv(direction, piece, step).wait_recv()
                if step + 1 < steps:
                    ring_copy(direction, piece, step + 1).start()

    ring_start(0)
    ring_start(1)
    forward(NEAR[:3])
    ring_step(0, 0)
    forward(NEAR[3:4])
    ring_step(0, 1)
    forward(NEAR[4:5])
    ring_step(1, 0)
    forward(NEAR[5:6])
    ring_step(1, 1)
    forward(NEAR[6:])

    for n in NEAR:
        st_recv(of(n)).wait_recv()
    for d in range(1, NX):
        ls_recv(d).wait_recv()
    st_local.wait()
    ls_local.wait()

    crst = remote(stg.at[0], stg.at[1], crst_s, crst_r, device(3 - y, x, z, core))
    crls = remote(lsg.at[0], lsg.at[1], crls_s, crls_r, device(3 - y, x, z, core))

    @pl.when(y == 2)
    def _():
        crst.start()
        crls.start()

    state = (qs, dos, qt, dot, lseb, delb)
    for piece in (0, 1):
        for i in (0, 1):
            load_rows(piece * 2 + i, 0, qg, dog, stg, eye, *state)
        turn_rows(piece * 2, piece * 2 + 2, eye, *state[:4])
        ring_step(2, piece)
    for xx in range(NX):
        bias[xx] = jnp.where(seen_bias(lsg, 0, xx, half, base) > 0.0, 0.0, BIG)

    own = z // 2
    side = (z % 2) * 2 - 1

    def column(i, carry):
        @pl.when(i == 3)
        def _():
            ring_step(3, 0)
            ring_step(3, 1)

        move = jnp.where(i == 1, side, jnp.where(i == 2, -side, jnp.where(i == 3, 2, 0)))
        zz = (own + move + 4) % 4
        cut = diag.at[jnp.where(i == 0, 0, 1)]
        rest = (pbuf, dsbuf, dqa, dka, dva)
        tile((0, 1, 2, 3), zz, zz + 4, kvg, bias, cut, *state, *rest)
        tile((2, 3), zz + 8, zz + 12, kvg, bias, cut, *state, *rest)
        return carry

    lax.fori_loop(0, 4, column, 0)
    put_dq(dq, dqa)

    for n in NEAR:
        for i in (0, 1):
            kv_copy(to(n), i).wait_send()
            big_copy(to(n), i).wait_send()
        st_copy(to(n)).wait_send()
    for d in range(1, NX):
        ls_copy(d).wait_send()
    for direction, piece, steps in CHAINS:
        for step in range(steps):
            ring_copy(direction, piece, step).wait_send()

    @pl.when(y == 2)
    def _():
        for s in range(PEERS):
            for which in (0, 1):
                cross_copy(s, which).wait_send()
        crst.wait_send()
        crls.wait_send()

    @pl.when(y == 1)
    def _():
        for s in range(PEERS):
            for which in (0, 1):
                cross_copy(s, which).wait_recv()
        crst.wait_recv()
        crls.wait_recv()
        hits = [seen_bias(lsg, 1, xx, half, base) for xx in range(NX)]
        for xx in range(NX):
            far_bias[xx] = jnp.where(hits[xx] > 0.0, 0.0, BIG)
        some = jnp.maximum(jnp.maximum(hits[0], hits[1]), jnp.maximum(hits[2], hits[3]))
        far_any[...] = some.astype(jnp.int32)


def gather(q, k, v, o, do, lse, lists):
    vmem = pl.BlockSpec(memory_space=pltpu.VMEM)
    hbm = pl.BlockSpec(memory_space=pltpu.HBM)
    dma = pltpu.SemaphoreType.DMA
    return pl.pallas_call(
        gather_kernel,
        out_shape=(
            jax.ShapeDtypeStruct((2, PEERS, TOK, GW), BF16),
            jax.ShapeDtypeStruct((2, PEERS, TOK, GW), BF16),
            jax.ShapeDtypeStruct((2, PEERS, TOK, 128), F32),
            jax.ShapeDtypeStruct((NZ, 2, NX, PIECE, HD), BF16),
            jax.ShapeDtypeStruct((PEERS, TOK, GW), BF16),
            jax.ShapeDtypeStruct((16, HD, BLOCK), F32),
            jax.ShapeDtypeStruct((16, HD, BLOCK), F32),
            jax.ShapeDtypeStruct((NX, 16, 128), F32),
            jax.ShapeDtypeStruct((16, 128), jnp.int32),
        ),
        in_specs=[hbm] * 7,
        out_specs=(vmem,) * 9,
        scratch_shapes=[
            pltpu.VMEM((TOK, QH * HD), BF16),
            pltpu.VMEM((TOK, QH * HD), BF16),
            pltpu.VMEM((TOK, QH), F32),
            pltpu.VMEM((2, LISTW), jnp.int32),
            pltpu.VMEM((KVH, TOK, 128), F32),
            pltpu.VMEM((8, 128), jnp.int32),
            pltpu.VMEM((2, NX, 8, 128), jnp.int32),
            pltpu.VMEM((NX, 16, 128), F32),
            pltpu.VMEM((2, ROWS, 128), F32),
            *TILE_SCRATCH,
            dma((4,)),
            dma((2, PEERS)), dma((2, PEERS)), dma((2,)),
            dma((2, PEERS)), dma((2, PEERS)), dma((2,)),
            dma((PEERS,)), dma((PEERS,)), dma,
            dma((NX,)), dma((NX,)), dma,
            dma((2, 2, 4)), dma((2, 2, 4)),
            dma((2, PEERS)), dma((2, PEERS)),
            dma, dma, dma, dma,
        ],
        compiler_params=pltpu.CompilerParams(
            collective_id=0, has_side_effects=True, vmem_limit_bytes=24 << 20
        ),
        name="gather",
    )(q, k, v, o, do, lse, lists)


def far_kernel(
    far_any, qg, dog, stg, kvg, far_bias, dka_in, dva_in, dq, dkv,
    order, qs, dos, qt, dot, lseb, delb, pbuf, dsbuf, dqa, dka, dva,
):
    y, x, z, core = coords()
    eye = identity()

    def finish(kref, vref):
        def one(b, carry):
            zz = (b % 4) * 2
            for piece, ref, scale in ((0, kref, SCALE), (1, vref, 1.0)):
                low = (ref[b] * scale).astype(BF16)
                out = lax.dot_general(eye, low, NT, preferred_element_type=F32).astype(BF16)
                dkv[zz, piece, b // 4] = out[:PIECE]
                dkv[zz + 1, piece, b // 4] = out[PIECE:]
            return carry

        lax.fori_loop(0, 16, one, 0)

    @pl.when(y == 1)
    def _():
        def note(b, n):
            order[n] = b
            return n + (far_any[b, 0] > 0).astype(jnp.int32)

        n = lax.fori_loop(0, 16, note, 0)

        def unseen(b, first):
            return jnp.where(far_any[b, 0] > 0, first, b)

        order[n] = lax.fori_loop(0, 16, unseen, 0)
        state = (qs, dos, qt, dot, lseb, delb)
        for xx in range(NX):
            load_rows(xx, 1, qg, dog, stg, eye, *state)
        turn_rows(0, NX, eye, *state[:4])
        for ref, src in ((dka, dka_in), (dva, dva_in)):
            ref[...] = src[...]
        dqa[...] = jnp.zeros_like(dqa)

        def pair(i, carry):
            tile(
                (0, 1, 2, 3), order[2 * i], order[2 * i + 1], kvg, far_bias, None,
                *state, pbuf, dsbuf, dqa, dka, dva,
            )
            return carry

        lax.fori_loop(0, (n + 1) // 2, pair, 0)
        put_dq(dq, dqa)
        finish(dka, dva)

    @pl.when(y != 1)
    def _():
        finish(dka_in, dva_in)


def far(far_any, *args):
    vmem = pl.BlockSpec(memory_space=pltpu.VMEM)
    return pl.pallas_call(
        far_kernel,
        out_shape=(
            jax.ShapeDtypeStruct((PEERS, TOK, GW), BF16),
            jax.ShapeDtypeStruct((NZ, 2, NX, PIECE, HD), BF16),
        ),
        in_specs=[pl.BlockSpec(memory_space=pltpu.SMEM)] + [vmem] * 7,
        out_specs=(vmem, vmem),
        scratch_shapes=[
            pltpu.SMEM((32,), jnp.int32),
            *TILE_SCRATCH,
            pltpu.VMEM((16, HD, BLOCK), F32),
            pltpu.VMEM((16, HD, BLOCK), F32),
        ],
        compiler_params=pltpu.CompilerParams(vmem_limit_bytes=24 << 20),
        name="far",
    )(far_any, *args)


def give_kernel(
    dq, far_dq, dkv, gq, gk, gv,
    land, total, acc_in, acc_out, final,
    cr_s, cr_r, ring_s, ring_r, q_s, q_r, q_l, kv_s, kv_r, kv_l,
):
    y, x, z, core = coords()
    me = x * 2 + core
    bar = pltpu.get_barrier_semaphore()
    signal_peers(bar, y, x, z, core, me)
    wait_peers(bar, y)

    def cols(ref, g, width):
        return ref.at[:, pl.ds(pl.multiple_of(g * width, 128), width)]

    def cross_copy(s):
        return remote(far_dq.at[s], land.at[s], cr_s.at[s], cr_r.at[s], device(3 - y, x, z, core))

    slots = [(me + d) % PEERS for d in (2, 3, 4, 5, 6, 7, 1, 0)]

    @pl.when(y == 1)
    def _():
        for s in slots:
            cross_copy(s).start()

    def ring_copy(direction, piece, steps, step):
        sign = (1, NZ - 1)[direction]
        owner = (z + sign * (steps - step)) % NZ
        if step == 0:
            src = dkv.at[owner, piece]
        else:
            src = acc_out.at[direction, piece, step]
        return remote(
            src, acc_in.at[direction, piece, step],
            ring_s.at[direction, piece, step], ring_r.at[direction, piece, step],
            device(y, x, (z + sign) % NZ, core),
        )

    for direction, piece, steps in CHAINS:
        ring_copy(direction, piece, steps, 0).start()

    def q_copy(src, p):
        return remote(
            src.at[p], cols(gq, me, GW), q_s.at[p], q_r.at[me], device(y, p // 2, z, p % 2)
        )

    def q_recv(s):
        return remote(
            total.at[s], cols(gq, s, GW), q_s.at[s], q_r.at[s], device(y, s // 2, z, s % 2)
        )

    q_local = pltpu.make_async_copy(total.at[me], cols(gq, me, GW), q_l)
    q_local_direct = pltpu.make_async_copy(dq.at[me], cols(gq, me, GW), q_l)

    @pl.when(y != 2)
    def _():
        for p in slots[:-1]:
            q_copy(dq, p).start()
        q_local_direct.start()

    def add_cross(some):
        @pl.when(y == 2)
        def _():
            for s in some:
                cross_copy(s).wait_recv()
                total[s] = (dq[s].astype(F32) + land[s].astype(F32)).astype(BF16)
                if s is slots[-1]:
                    q_local.start()
                else:
                    q_copy(total, s).start()

    groups = ((), slots[0:2], slots[2:5], slots[5:8])
    for step in range(1, 4):
        for direction, piece, steps in CHAINS:
            if step < steps:
                sign = (1, NZ - 1)[direction]
                owner = (z + sign * (steps - step)) % NZ
                ring_copy(direction, piece, steps, step - 1).wait_recv()
                acc_out[direction, piece, step] = (
                    acc_in[direction, piece, step - 1].astype(F32)
                    + dkv[owner, piece].astype(F32)
                ).astype(BF16)
                ring_copy(direction, piece, steps, step).start()
        add_cross(groups[step])

    def kv_copy(piece, p):
        return remote(
            final.at[piece, p // 2, pl.ds((p % 2) * TOK, TOK), :],
            cols((gk, gv)[piece], me, HD),
            kv_s.at[piece, p], kv_r.at[piece, me], device(y, p // 2, z, p % 2),
        )

    def kv_recv(piece, s):
        return remote(
            final.at[piece, s // 2, pl.ds((s % 2) * TOK, TOK), :],
            cols((gk, gv)[piece], s, HD),
            kv_s.at[piece, s], kv_r.at[piece, s], device(y, s // 2, z, s % 2),
        )

    kv_local = []
    for piece in (0, 1):
        last = [(d, steps) for d, pc, steps in CHAINS if pc == piece]
        for direction, steps in last:
            ring_copy(direction, piece, steps, steps - 1).wait_recv()
        (d0, s0), (d1, s1) = last
        final[piece] = (
            acc_in[d0, piece, s0 - 1].astype(F32)
            + acc_in[d1, piece, s1 - 1].astype(F32)
            + dkv[z, piece].astype(F32)
        ).astype(BF16)
        for p in slots[:-1]:
            kv_copy(piece, p).start()
        local = pltpu.make_async_copy(
            final.at[piece, x, pl.ds(core * TOK, TOK), :], cols((gk, gv)[piece], me, HD), kv_l.at[piece]
        )
        local.start()
        kv_local.append(local)

    @pl.when(y == 1)
    def _():
        for s in slots:
            cross_copy(s).wait_send()

    for direction, piece, steps in CHAINS:
        for step in range(steps):
            ring_copy(direction, piece, steps, step).wait_send()
    for p in slots[:-1]:
        q_copy(total, p).wait_send()
        q_recv(p).wait_recv()
        for piece in (0, 1):
            kv_copy(piece, p).wait_send()
            kv_recv(piece, p).wait_recv()
    q_local.wait()
    for c in kv_local:
        c.wait()


def give(dq, far_dq, dkv):
    vmem = pl.BlockSpec(memory_space=pltpu.VMEM)
    dma = pltpu.SemaphoreType.DMA
    return pl.pallas_call(
        give_kernel,
        out_shape=(
            jax.ShapeDtypeStruct((TOK, QH * HD), BF16),
            jax.ShapeDtypeStruct((TOK, KVH * HD), BF16),
            jax.ShapeDtypeStruct((TOK, KVH * HD), BF16),
        ),
        in_specs=[vmem] * 3,
        out_specs=(vmem,) * 3,
        scratch_shapes=[
            pltpu.VMEM((PEERS, TOK, GW), BF16),
            pltpu.VMEM((PEERS, TOK, GW), BF16),
            pltpu.VMEM((2, 2, 4, NX, PIECE, HD), BF16),
            pltpu.VMEM((2, 2, 4, NX, PIECE, HD), BF16),
            pltpu.VMEM((2, NX, PIECE, HD), BF16),
            dma((PEERS,)), dma((PEERS,)),
            dma((2, 2, 4)), dma((2, 2, 4)),
            dma((PEERS,)), dma((PEERS,)), dma,
            dma((2, PEERS)), dma((2, PEERS)), dma((2,)),
        ],
        compiler_params=pltpu.CompilerParams(collective_id=1, has_side_effects=True, vmem_limit_bytes=16 << 20),
        name="give",
    )(dq, far_dq, dkv)


def local(query_act, key_act, value_act, attn_out, grad_out, log_sum, kv_lists):
    args = (query_act, key_act, value_act, attn_out, grad_out, log_sum, kv_lists)
    qg, dog, stg, kvg, dq, dka, dva, far_bias, far_any = gather(
        *(pltpu.with_memory_space_constraint(a, pltpu.HBM) for a in args)
    )
    far_dq, dkv = far(far_any, qg, dog, stg, kvg, far_bias, dka, dva)
    return give(dq, far_dq, dkv)


def solution(mesh):
    row = P(("blk", "head"), None)
    return jax.shard_map(
        local,
        mesh=mesh,
        in_specs=(row,) * 6 + (P("blk", None),),
        out_specs=(row,) * 3,
        check_vma=False,
    )
```

```python
import jax
import jax.numpy as jnp
from jax import lax
from jax.experimental import pallas as pl
from jax.experimental.pallas import tpu as pltpu
from jax.sharding import PartitionSpec as P

QH = 40
KVH = 8
HD = 128
BLOCK = 128
GS = QH // KVH
TOK = 32
GW = GS * HD
PIECE = 64
ROWS = GS * PIECE
NX = 4
NZ = 8
PEERS = 8
LISTW = 32
SCALE = HD ** -0.5
LOG2E = 1.4426950408889634
MESH = pl.DeviceIdType.MESH
F32 = jnp.float32
BF16 = jnp.bfloat16
NT = (((1,), (1,)), ((), ()))
NN = (((1,), (0,)), ((), ()))


def coords():
    blk = lax.axis_index("blk")
    head = lax.axis_index("head")
    y = blk // 8
    x = (blk // 2) % 4
    z = (blk % 2) * 4 + head // 2
    return y, x, z, head % 2


def device(y, x, z, core):
    return {"blk": (y * 4 + x) * 2 + z // 4, "head": (z % 4) * 2 + core}


def remote(src, dst, send_sem, recv_sem, device_id):
    return pltpu.make_async_remote_copy(
        src_ref=src,
        dst_ref=dst,
        send_sem=send_sem,
        recv_sem=recv_sem,
        device_id=device_id,
        device_id_type=MESH,
    )


def signal_peers(bar, y, x, z, core, me):
    for d in range(1, PEERS):
        p = (me + d) % PEERS
        pl.semaphore_signal(bar, inc=1, device_id=device(y, p // 2, z, p % 2), device_id_type=MESH)
    for step in (1, NZ - 1):
        pl.semaphore_signal(
            bar, inc=1, device_id=device(y, x, (z + step) % NZ, core), device_id_type=MESH
        )

    @pl.when((y == 1) | (y == 2))
    def _():
        pl.semaphore_signal(bar, inc=1, device_id=device(3 - y, x, z, core), device_id_type=MESH)


def wait_peers(bar, y):
    pl.semaphore_wait(bar, PEERS - 1 + 2 + ((y == 1) | (y == 2)).astype(jnp.int32))


CHAINS = ((0, 0, 4), (0, 1, 3), (1, 1, 4), (1, 0, 3))


BIG = 1e30
ALLROWS = NX * ROWS


def rows_of(x):
    return slice(x * ROWS, (x + 1) * ROWS)


def seen_bias(lists, part, x, half, base):
    entries = lists[part, x, pl.ds(half, 1), :]
    block = base + lax.broadcasted_iota(jnp.int32, (16, 128), 0)
    hit = jnp.max(jnp.where(entries == block, 1.0, 0.0), axis=1, keepdims=True)
    return jnp.broadcast_to(hit, (16, 128))


def load_rows(x, part, qg, dog, stg, eye, qs, dos, qt, dot, lseb, delb):
    for c in range(2):
        st = stg[part, x * 2 + c]
        for r in range(GS):
            start = x * ROWS + r * PIECE + c * TOK
            at = slice(start, start + TOK)
            col = slice(r * HD, (r + 1) * HD)
            qs[at, :] = qg[part, x * 2 + c, :, col]
            dos[at, :] = dog[part, x * 2 + c, :, col]
            lseb[at, :] = jnp.broadcast_to(st[:, r : r + 1], (TOK, 128))
            delb[at, :] = jnp.broadcast_to(st[:, 8 + r : 9 + r], (TOK, 128))


def turn_rows(lo, hi, eye, qs, dos, qt, dot):
    at = slice(lo * ROWS, hi * ROWS)
    qt[:, at] = lax.dot_general(eye, qs[at, :], NT, preferred_element_type=F32).astype(BF16)
    dot[:, at] = lax.dot_general(eye, dos[at, :], NT, preferred_element_type=F32).astype(BF16)


def identity():
    r_id = lax.broadcasted_iota(jnp.int32, (128, 128), 0)
    c_id = lax.broadcasted_iota(jnp.int32, (128, 128), 1)
    return jnp.where(r_id == c_id, 1.0, 0.0).astype(BF16)


def key_block(kvg, piece, b):
    zz = (b % 4) * 2
    return jnp.concatenate([kvg[zz, piece, b // 4], kvg[zz + 1, piece, b // 4]], axis=0)


def tile(xs, a, b, kvg, bias, diag, qs, dos, qt, dot, lseb, delb, pbuf, dsbuf, dqa, dka, dva):
    keys = jnp.concatenate([key_block(kvg, 0, a), key_block(kvg, 0, b)], axis=0)
    values = jnp.concatenate([key_block(kvg, 1, a), key_block(kvg, 1, b)], axis=0)
    for x in xs:
        at = rows_of(x)
        s = lax.dot_general(qs[at, :], keys, NT, preferred_element_type=F32)
        dp = lax.dot_general(dos[at, :], values, NT, preferred_element_type=F32)
        lse_a = lseb[at, :] + bias[x, pl.ds(a, 1), :]
        lse_b = lseb[at, :] + bias[x, pl.ds(b, 1), :]
        if diag is not None:
            if x % 2 == 0 and x == xs[0]:
                lse_a = lse_a + diag[...]
            if x % 2 == 1 and x == xs[0] + 1:
                lse_b = lse_b + diag[...]
        p = jnp.exp2(s * (SCALE * LOG2E) - jnp.concatenate([lse_a, lse_b], axis=1))
        delta = delb[at, :]
        ds = (p * (dp - jnp.concatenate([delta, delta], axis=1))).astype(BF16)
        pbuf[at, :] = p.astype(BF16)
        dsbuf[at, :] = ds
        dqa[at, :] += lax.dot_general(ds, keys, NN, preferred_element_type=F32)
    at = slice(xs[0] * ROWS, (xs[-1] + 1) * ROWS)
    dvt = lax.dot_general(dot[:, at], pbuf[at, :], NN, preferred_element_type=F32)
    dkt = lax.dot_general(qt[:, at], dsbuf[at, :], NN, preferred_element_type=F32)
    dva[a] += dvt[:, :BLOCK]
    dka[a] += dkt[:, :BLOCK]
    dva[b] += dvt[:, BLOCK:]
    dka[b] += dkt[:, BLOCK:]


def put_dq(dq, dqa):
    for x in range(NX):
        for c in range(2):
            for r in range(GS):
                start = x * ROWS + r * PIECE + c * TOK
                dq[x * 2 + c, :, r * HD : (r + 1) * HD] = (
                    dqa[start : start + TOK, :] * SCALE
                ).astype(BF16)


TILE_SCRATCH = [
    pltpu.VMEM((ALLROWS, HD), BF16),
    pltpu.VMEM((ALLROWS, HD), BF16),
    pltpu.VMEM((HD, ALLROWS), BF16),
    pltpu.VMEM((HD, ALLROWS), BF16),
    pltpu.VMEM((ALLROWS, 128), F32),
    pltpu.VMEM((ALLROWS, 128), F32),
    pltpu.VMEM((ALLROWS, 2 * BLOCK), BF16),
    pltpu.VMEM((ALLROWS, 2 * BLOCK), BF16),
    pltpu.VMEM((ALLROWS, HD), F32),
]


NEAR = ((0, 1), (1, 0), (3, 0), (1, 1), (3, 1), (2, 0), (2, 1))


def whole_kernel(
    q, k, v, o, do, lse, lists,
    gq, gk, gv,
    qg, dog, stg, kvg, dq, far_dq, dka, dva, dkv, land, total, acc_in, acc_out, final,
    o_buf, do_buf, lse_buf, rows_buf, stat_src, list_src, lsg, bias, diag,
    qs, dos, qt, dot, lseb, delb, pbuf, dsbuf, dqa, in_sem,
    kv_s, kv_r, kv_l, big_s, big_r, big_l, st_s, st_r, st_l, ls_s, ls_r, ls_l,
    ring_s, ring_r, cr_s, cr_r, crst_s, crst_r, crls_s, crls_r,
    dq_s, dq_r, red_s, red_r, out_s, out_r, out_l, kvo_s, kvo_r, kvo_l,
):
    y, x, z, core = coords()
    me = x * 2 + core
    loads = [
        pltpu.make_async_copy(src, dst, in_sem.at[i])
        for i, (src, dst) in enumerate(
            ((lists, rows_buf), (lse, lse_buf), (do, do_buf), (o, o_buf))
        )
    ]
    for c in loads:
        c.start()
    bar = pltpu.get_barrier_semaphore()
    signal_peers(bar, y, x, z, core, me)

    def cols(ref, g, width):
        return ref.at[:, pl.ds(pl.multiple_of(g * width, 128), width)]

    def to(n):
        return ((x + n[0]) % NX) * 2 + (core + n[1]) % 2

    def of(n):
        return ((x + NX - n[0]) % NX) * 2 + (core + n[1]) % 2

    def at(p):
        return device(y, p // 2, z, p % 2)

    def kv_slot(s, piece, zz):
        return kvg.at[zz, piece, s // 2, pl.ds((s % 2) * TOK, TOK), :]

    def kv_copy(p, piece):
        return remote(
            cols((k, v)[piece], p, HD), kv_slot(me, piece, z),
            kv_s.at[piece, p], kv_r.at[piece, me], at(p),
        )

    def kv_recv(s, piece):
        return remote(
            cols((k, v)[piece], s, HD), kv_slot(s, piece, z),
            kv_s.at[piece, s], kv_r.at[piece, s], at(s),
        )

    def big_copy(p, which):
        src, dst = ((q, qg), (do, dog))[which]
        return remote(
            cols(src, p, GW), dst.at[0, me], big_s.at[which, p], big_r.at[which, me], at(p)
        )

    def big_recv(s, which):
        src, dst = ((q, qg), (do, dog))[which]
        return remote(
            cols(src, s, GW), dst.at[0, s], big_s.at[which, s], big_r.at[which, s], at(s)
        )

    def st_copy(p):
        return remote(stat_src.at[p], stg.at[0, me], st_s.at[p], st_r.at[me], at(p))

    def st_recv(s):
        return remote(stat_src.at[s], stg.at[0, s], st_s.at[s], st_r.at[s], at(s))

    def ls_copy(d):
        xx = (x + d) % NX
        return remote(list_src, lsg.at[0, x], ls_s.at[xx], ls_r.at[x], device(y, xx, z, core))

    def ls_recv(d):
        xx = (x + NX - d) % NX
        return remote(list_src, lsg.at[0, xx], ls_s.at[xx], ls_r.at[xx], device(y, xx, z, core))

    def cross_copy(s, which):
        ref = (qg, dog)[which]
        return remote(
            ref.at[0, s], ref.at[1, s], cr_s.at[which, s], cr_r.at[which, s],
            device(3 - y, x, z, core),
        )

    kv_local = [
        pltpu.make_async_copy(cols((k, v)[piece], me, HD), kv_slot(me, piece, z), kv_l.at[piece])
        for piece in (0, 1)
    ]
    big_local = [
        pltpu.make_async_copy(cols(q, me, GW), qg.at[0, me], big_l.at[0]),
        pltpu.make_async_copy(cols(do, me, GW), dog.at[0, me], big_l.at[1]),
    ]
    for c in kv_local + big_local:
        c.start()

    loads[0].wait()
    list_src[...] = jnp.full((8, 128), -1, jnp.int32)
    list_src[0:2, 0:LISTW] = rows_buf[...]

    for c in loads[1:]:
        c.wait()
    lane = lax.broadcasted_iota(jnp.int32, (TOK, 128), 1)
    for g in range(KVH):
        block = jnp.zeros((TOK, 128), F32)
        for r in range(GS):
            h = g * GS + r
            own = slice(h * HD, (h + 1) * HD)
            delta = jnp.sum(
                do_buf[:, own].astype(F32) * o_buf[:, own].astype(F32), axis=1, keepdims=True
            )
            block = jnp.where(lane == r, lse_buf[:, h : h + 1] * LOG2E, block)
            block = jnp.where(lane == 8 + r, delta, block)
        stat_src[g] = block

    for ref in (dka, dva, dqa):
        ref[...] = jnp.zeros_like(ref)
    eye = identity()
    half = (z % 4) // 2
    base = y * 16
    row_tok = (z % 2) * PIECE + lax.broadcasted_iota(jnp.int32, (ROWS, 128), 0) % PIECE
    key_tok = lax.broadcasted_iota(jnp.int32, (ROWS, 128), 1)
    diag[0] = jnp.where(key_tok <= row_tok, 0.0, BIG)
    diag[1] = jnp.zeros((ROWS, 128), F32)

    wait_peers(bar, y)
    for piece in (0, 1):
        for n in NEAR[1:] + NEAR[:1]:
            kv_copy(to(n), piece).start()
    for n in NEAR:
        for which in (0, 1):
            big_copy(to(n), which).start()
    for c in big_local:
        c.wait()

    @pl.when(y == 2)
    def _():
        for which in (0, 1):
            cross_copy(me, which).start()

    for n in NEAR:
        st_copy(to(n)).start()
    for d in range(1, NX):
        ls_copy(d).start()
    st_local = pltpu.make_async_copy(stat_src.at[me], stg.at[0, me], st_l)
    st_local.start()
    ls_local = pltpu.make_async_copy(list_src, lsg.at[0, x], ls_l)
    ls_local.start()

    def ring_copy(direction, piece, step):
        sign = (1, NZ - 1)[direction]
        back = (NZ - 1, 1)[direction]
        chunk = (z + back * step) % NZ
        part = kvg.at[chunk, piece]
        return remote(
            part, part, ring_s.at[direction, piece, step], ring_r.at[direction, piece, step],
            device(y, x, (z + sign) % NZ, core),
        )

    def ring_recv(direction, piece, step):
        back = (NZ - 1, 1)[direction]
        chunk = (z + back * (step + 1)) % NZ
        part = kvg.at[chunk, piece]
        return remote(
            part, part, ring_s.at[direction, piece, step], ring_r.at[direction, piece, step],
            device(y, x, (z + back) % NZ, core),
        )

    def forward(some):
        for n in some:
            s = of(n)
            for which in (0, 1):
                big_recv(s, which).wait_recv()

            @pl.when(y == 2)
            def _():
                for which in (0, 1):
                    cross_copy(s, which).start()

    def ring_start(piece):
        for n in NEAR:
            kv_recv(of(n), piece).wait_recv()
        kv_local[piece].wait()
        for direction in (0, 1):
            ring_copy(direction, piece, 0).start()

    def ring_step(step, piece):
        for direction, pc, steps in CHAINS:
            if pc == piece and step < steps:
                ring_recv(direction, piece, step).wait_recv()
                if step + 1 < steps:
                    ring_copy(direction, piece, step + 1).start()

    ring_start(0)
    ring_start(1)
    forward(NEAR[:3])
    ring_step(0, 0)
    forward(NEAR[3:4])
    ring_step(0, 1)
    forward(NEAR[4:5])
    ring_step(1, 0)
    forward(NEAR[5:6])
    ring_step(1, 1)
    forward(NEAR[6:])

    for n in NEAR:
        st_recv(of(n)).wait_recv()
    for d in range(1, NX):
        ls_recv(d).wait_recv()
    st_local.wait()
    ls_local.wait()

    crst = remote(stg.at[0], stg.at[1], crst_s, crst_r, device(3 - y, x, z, core))
    crls = remote(lsg.at[0], lsg.at[1], crls_s, crls_r, device(3 - y, x, z, core))

    @pl.when(y == 2)
    def _():
        crst.start()
        crls.start()

    state = (qs, dos, qt, dot, lseb, delb)
    for piece in (0, 1):
        for i in (0, 1):
            load_rows(piece * 2 + i, 0, qg, dog, stg, eye, *state)
        turn_rows(piece * 2, piece * 2 + 2, eye, *state[:4])
        ring_step(2, piece)
    for xx in range(NX):
        bias[xx] = jnp.where(seen_bias(lsg, 0, xx, half, base) > 0.0, 0.0, BIG)

    own = z // 2
    side = (z % 2) * 2 - 1

    def column(i, carry):
        @pl.when(i == 3)
        def _():
            ring_step(3, 0)
            ring_step(3, 1)

        move = jnp.where(i == 1, side, jnp.where(i == 2, -side, jnp.where(i == 3, 2, 0)))
        zz = (own + move + 4) % 4
        cut = diag.at[jnp.where(i == 0, 0, 1)]
        rest = (pbuf, dsbuf, dqa, dka, dva)
        tile((0, 1, 2, 3), zz, zz + 4, kvg, bias, cut, *state, *rest)
        tile((2, 3), zz + 8, zz + 12, kvg, bias, cut, *state, *rest)
        return carry

    lax.fori_loop(0, 4, column, 0)
    put_dq(dq, dqa)

    def cross_dq(s):
        return remote(far_dq.at[s], land.at[s], dq_s.at[s], dq_r.at[s], device(3 - y, x, z, core))

    def dq_copy(src, p):
        return remote(src.at[p], cols(gq, me, GW), out_s.at[p], out_r.at[me], at(p))

    def dq_recv(s):
        return remote(total.at[s], cols(gq, s, GW), out_s.at[s], out_r.at[s], at(s))

    dq_local = pltpu.make_async_copy(total.at[me], cols(gq, me, GW), out_l)

    @pl.when(y != 2)
    def _():
        for n in NEAR:
            dq_copy(dq, to(n)).start()
        pltpu.make_async_copy(dq.at[me], cols(gq, me, GW), out_l).start()

    @pl.when(y == 1)
    def _():
        for s in range(PEERS):
            for which in (0, 1):
                cross_copy(s, which).wait_recv()
        crst.wait_recv()
        crls.wait_recv()
        for xx in range(NX):
            load_rows(xx, 1, qg, dog, stg, eye, *state)
            bias[xx] = jnp.where(seen_bias(lsg, 1, xx, half, base) > 0.0, 0.0, BIG)
        turn_rows(0, NX, eye, *state[:4])
        dqa[...] = jnp.zeros_like(dqa)

    def red_copy(direction, piece, steps, step):
        sign = (1, NZ - 1)[direction]
        owner = (z + sign * (steps - step)) % NZ
        if step == 0:
            src = dkv.at[owner, piece]
        else:
            src = acc_out.at[direction, piece, step]
        return remote(
            src, acc_in.at[direction, piece, step],
            red_s.at[direction, piece, step], red_r.at[direction, piece, step],
            device(y, x, (z + sign) % NZ, core),
        )

    def red_step(direction, piece, steps, step):
        sign = (1, NZ - 1)[direction]
        owner = (z + sign * (steps - step)) % NZ
        red_copy(direction, piece, steps, step - 1).wait_recv()
        acc_out[direction, piece, step] = (
            acc_in[direction, piece, step - 1].astype(F32) + dkv[owner, piece].astype(F32)
        ).astype(BF16)
        red_copy(direction, piece, steps, step).start()

    def finish(zz):
        @pl.when(y == 1)
        def _():
            rest = (pbuf, dsbuf, dqa, dka, dva)
            tile((0, 1, 2, 3), zz, zz + 4, kvg, bias, None, *state, *rest)
            tile((0, 1, 2, 3), zz + 8, zz + 12, kvg, bias, None, *state, *rest)

        for xx in range(NX):
            for piece, ref, scale in ((0, dka, SCALE), (1, dva, 1.0)):
                low = (ref[zz + 4 * xx] * scale).astype(BF16)
                turned = lax.dot_general(eye, low, NT, preferred_element_type=F32).astype(BF16)
                dkv[2 * zz, piece, xx] = turned[:PIECE]
                dkv[2 * zz + 1, piece, xx] = turned[PIECE:]

    long = ((0, 0, 4), (1, 1, 4))
    short = ((0, 1, 3), (1, 0, 3))

    def reduce_column(i, carry):
        move = jnp.where(i == 0, 2, jnp.where(i == 1, -side, jnp.where(i == 2, side, 0)))
        finish((own + move + 4) % 4)

        @pl.when(i == 0)
        def _():
            for c in long:
                red_copy(*c, 0).start()

        @pl.when(i == 1)
        def _():
            for c in short:
                red_copy(*c, 0).start()
            for c in long:
                red_step(*c, 1)

        @pl.when(i == 2)
        def _():
            for c in short:
                red_step(*c, 1)
            for c in long:
                red_step(*c, 2)

        return carry

    lax.fori_loop(0, 4, reduce_column, 0)

    @pl.when(y == 1)
    def _():
        put_dq(far_dq, dqa)
        for s in range(PEERS):
            cross_dq(s).start()

    for c in short:
        red_step(*c, 2)
    for c in long:
        red_step(*c, 3)

    def grad_copy(piece, p):
        return remote(
            final.at[piece, p // 2, pl.ds((p % 2) * TOK, TOK), :],
            cols((gk, gv)[piece], me, HD),
            kvo_s.at[piece, p], kvo_r.at[piece, me], at(p),
        )

    def grad_recv(piece, s):
        return remote(
            final.at[piece, s // 2, pl.ds((s % 2) * TOK, TOK), :],
            cols((gk, gv)[piece], s, HD),
            kvo_s.at[piece, s], kvo_r.at[piece, s], at(s),
        )

    grad_local = []
    for piece in (0, 1):
        (d0, s0), (d1, s1) = [(d, steps) for d, pc, steps in CHAINS if pc == piece]
        red_copy(d0, piece, s0, s0 - 1).wait_recv()
        red_copy(d1, piece, s1, s1 - 1).wait_recv()
        final[piece] = (
            acc_in[d0, piece, s0 - 1].astype(F32)
            + acc_in[d1, piece, s1 - 1].astype(F32)
            + dkv[z, piece].astype(F32)
        ).astype(BF16)
        for n in NEAR:
            grad_copy(piece, to(n)).start()
        grad_local.append(
            pltpu.make_async_copy(
                final.at[piece, x, pl.ds(core * TOK, TOK), :],
                cols((gk, gv)[piece], me, HD), kvo_l.at[piece],
            )
        )
        grad_local[piece].start()

    @pl.when(y == 2)
    def _():
        for s in range(PEERS):
            cross_dq(s).wait_recv()
            total[s] = (dq[s].astype(F32) + land[s].astype(F32)).astype(BF16)

            @pl.when(s == me)
            def _():
                dq_local.start()

            @pl.when(s != me)
            def _():
                dq_copy(total, s).start()


    for n in NEAR:
        for i in (0, 1):
            kv_copy(to(n), i).wait_send()
            big_copy(to(n), i).wait_send()
        st_copy(to(n)).wait_send()
    for d in range(1, NX):
        ls_copy(d).wait_send()
    for direction, piece, steps in CHAINS:
        for step in range(steps):
            ring_copy(direction, piece, step).wait_send()

    @pl.when(y == 2)
    def _():
        for s in range(PEERS):
            for which in (0, 1):
                cross_copy(s, which).wait_send()
        crst.wait_send()
        crls.wait_send()


    @pl.when(y == 1)
    def _():
        for s in range(PEERS):
            cross_dq(s).wait_send()

    for direction, piece, steps in CHAINS:
        for step in range(steps):
            red_copy(direction, piece, steps, step).wait_send()
    for n in NEAR:
        for piece in (0, 1):
            grad_copy(piece, to(n)).wait_send()
            grad_recv(piece, of(n)).wait_recv()
        dq_copy(total, to(n)).wait_send()
        dq_recv(of(n)).wait_recv()
    for c in grad_local:
        c.wait()
    dq_local.wait()


def whole(*args):
    vmem = pl.BlockSpec(memory_space=pltpu.VMEM)
    hbm = pl.BlockSpec(memory_space=pltpu.HBM)
    dma = pltpu.SemaphoreType.DMA
    return pl.pallas_call(
        whole_kernel,
        out_shape=(
            jax.ShapeDtypeStruct((TOK, QH * HD), BF16),
            jax.ShapeDtypeStruct((TOK, KVH * HD), BF16),
            jax.ShapeDtypeStruct((TOK, KVH * HD), BF16),
        ),
        in_specs=[hbm] * 7,
        out_specs=(vmem,) * 3,
        scratch_shapes=[
            pltpu.VMEM((2, PEERS, TOK, GW), BF16),
            pltpu.VMEM((2, PEERS, TOK, GW), BF16),
            pltpu.VMEM((2, PEERS, TOK, 128), F32),
            pltpu.VMEM((NZ, 2, NX, PIECE, HD), BF16),
            pltpu.VMEM((PEERS, TOK, GW), BF16),
            pltpu.VMEM((PEERS, TOK, GW), BF16),
            pltpu.VMEM((16, HD, BLOCK), F32),
            pltpu.VMEM((16, HD, BLOCK), F32),
            pltpu.VMEM((NZ, 2, NX, PIECE, HD), BF16),
            pltpu.VMEM((PEERS, TOK, GW), BF16),
            pltpu.VMEM((PEERS, TOK, GW), BF16),
            pltpu.VMEM((2, 2, 4, NX, PIECE, HD), BF16),
            pltpu.VMEM((2, 2, 4, NX, PIECE, HD), BF16),
            pltpu.VMEM((2, NX, PIECE, HD), BF16),
            pltpu.VMEM((TOK, QH * HD), BF16),
            pltpu.VMEM((TOK, QH * HD), BF16),
            pltpu.VMEM((TOK, QH), F32),
            pltpu.VMEM((2, LISTW), jnp.int32),
            pltpu.VMEM((KVH, TOK, 128), F32),
            pltpu.VMEM((8, 128), jnp.int32),
            pltpu.VMEM((2, NX, 8, 128), jnp.int32),
            pltpu.VMEM((NX, 16, 128), F32),
            pltpu.VMEM((2, ROWS, 128), F32),
            *TILE_SCRATCH,
            dma((4,)),
            dma((2, PEERS)), dma((2, PEERS)), dma((2,)),
            dma((2, PEERS)), dma((2, PEERS)), dma((2,)),
            dma((PEERS,)), dma((PEERS,)), dma,
            dma((NX,)), dma((NX,)), dma,
            dma((2, 2, 4)), dma((2, 2, 4)),
            dma((2, PEERS)), dma((2, PEERS)),
            dma, dma, dma, dma,
            dma((PEERS,)), dma((PEERS,)),
            dma((2, 2, 4)), dma((2, 2, 4)),
            dma((PEERS,)), dma((PEERS,)), dma,
            dma((2, PEERS)), dma((2, PEERS)), dma((2,)),
        ],
        compiler_params=pltpu.CompilerParams(
            collective_id=0, has_side_effects=True, vmem_limit_bytes=40 << 20
        ),
        name="whole",
    )(*args)


def local(query_act, key_act, value_act, attn_out, grad_out, log_sum, kv_lists):
    args = (query_act, key_act, value_act, attn_out, grad_out, log_sum, kv_lists)
    return whole(*(pltpu.with_memory_space_constraint(a, pltpu.HBM) for a in args))


def solution(mesh):
    row = P(("blk", "head"), None)
    return jax.shard_map(
        local,
        mesh=mesh,
        in_specs=(row,) * 6 + (P("blk", None),),
        out_specs=(row,) * 3,
        check_vma=False,
    )
```

```python
import jax
import jax.numpy as jnp
from jax import lax
from jax.experimental import pallas as pl
from jax.experimental.pallas import tpu as pltpu
from jax.sharding import PartitionSpec as P

QH = 40
KVH = 8
HD = 128
BLOCK = 128
GS = QH // KVH
TOK = 32
GW = GS * HD
PIECE = 64
ROWS = GS * PIECE
NX = 4
NZ = 8
PEERS = 8
LISTW = 32
SCALE = HD ** -0.5
LOG2E = 1.4426950408889634
MESH = pl.DeviceIdType.MESH
F32 = jnp.float32
BF16 = jnp.bfloat16
NT = (((1,), (1,)), ((), ()))
NN = (((1,), (0,)), ((), ()))


def coords():
    blk = lax.axis_index("blk")
    head = lax.axis_index("head")
    y = blk // 8
    x = (blk // 2) % 4
    z = (blk % 2) * 4 + head // 2
    return y, x, z, head % 2


def device(y, x, z, core):
    return {"blk": (y * 4 + x) * 2 + z // 4, "head": (z % 4) * 2 + core}


def remote(src, dst, send_sem, recv_sem, device_id):
    return pltpu.make_async_remote_copy(
        src_ref=src,
        dst_ref=dst,
        send_sem=send_sem,
        recv_sem=recv_sem,
        device_id=device_id,
        device_id_type=MESH,
    )


def signal_peers(bar, y, x, z, core, me):
    for d in range(1, PEERS):
        p = (me + d) % PEERS
        pl.semaphore_signal(bar, inc=1, device_id=device(y, p // 2, z, p % 2), device_id_type=MESH)
    for step in (1, NZ - 1):
        pl.semaphore_signal(
            bar, inc=1, device_id=device(y, x, (z + step) % NZ, core), device_id_type=MESH
        )

    @pl.when((y == 1) | (y == 2))
    def _():
        for p in range(PEERS):
            pl.semaphore_signal(
                bar, inc=1, device_id=device(3 - y, p // 2, z, p % 2), device_id_type=MESH
            )


def wait_peers(bar, y):
    pl.semaphore_wait(bar, PEERS - 1 + 2 + PEERS * ((y == 1) | (y == 2)).astype(jnp.int32))


CHAINS = ((0, 0, 4), (0, 1, 3), (1, 1, 4), (1, 0, 3))


BIG = 1e30
ALLROWS = NX * ROWS


def rows_of(x):
    return slice(x * ROWS, (x + 1) * ROWS)


def seen_bias(lists, part, x, half, base):
    entries = lists[part, x, pl.ds(half, 1), :]
    block = base + lax.broadcasted_iota(jnp.int32, (16, 128), 0)
    hit = jnp.max(jnp.where(entries == block, 1.0, 0.0), axis=1, keepdims=True)
    return jnp.broadcast_to(hit, (16, 128))


def load_rows(x, part, qg, dog, stg, eye, qs, dos, qt, dot, lseb, delb):
    for c in range(2):
        st = stg[part, x * 2 + c]
        for r in range(GS):
            start = x * ROWS + r * PIECE + c * TOK
            at = slice(start, start + TOK)
            col = slice(r * HD, (r + 1) * HD)
            qs[at, :] = qg[part, x * 2 + c, :, col]
            dos[at, :] = dog[part, x * 2 + c, :, col]
            lseb[at, :] = jnp.broadcast_to(st[:, r : r + 1], (TOK, 128))
            delb[at, :] = jnp.broadcast_to(st[:, 8 + r : 9 + r], (TOK, 128))


def turn_rows(lo, hi, eye, qs, dos, qt, dot):
    at = slice(lo * ROWS, hi * ROWS)
    qt[:, at] = lax.dot_general(eye, qs[at, :], NT, preferred_element_type=F32).astype(BF16)
    dot[:, at] = lax.dot_general(eye, dos[at, :], NT, preferred_element_type=F32).astype(BF16)


def identity():
    r_id = lax.broadcasted_iota(jnp.int32, (128, 128), 0)
    c_id = lax.broadcasted_iota(jnp.int32, (128, 128), 1)
    return jnp.where(r_id == c_id, 1.0, 0.0).astype(BF16)


def key_block(kvg, piece, b):
    zz = (b % 4) * 2
    return jnp.concatenate([kvg[zz, piece, b // 4], kvg[zz + 1, piece, b // 4]], axis=0)


def tile(xs, a, b, kvg, bias, diag, qs, dos, qt, dot, lseb, delb, pbuf, dsbuf, dqa, dka, dva):
    keys = jnp.concatenate([key_block(kvg, 0, a), key_block(kvg, 0, b)], axis=0)
    values = jnp.concatenate([key_block(kvg, 1, a), key_block(kvg, 1, b)], axis=0)
    for x in xs:
        at = rows_of(x)
        s = lax.dot_general(qs[at, :], keys, NT, preferred_element_type=F32)
        dp = lax.dot_general(dos[at, :], values, NT, preferred_element_type=F32)
        lse_a = lseb[at, :] + bias[x, pl.ds(a, 1), :]
        lse_b = lseb[at, :] + bias[x, pl.ds(b, 1), :]
        if diag is not None:
            if x % 2 == 0 and x == xs[0]:
                lse_a = lse_a + diag[...]
            if x % 2 == 1 and x == xs[0] + 1:
                lse_b = lse_b + diag[...]
        p = jnp.exp2(s * (SCALE * LOG2E) - jnp.concatenate([lse_a, lse_b], axis=1))
        delta = delb[at, :]
        ds = (p * (dp - jnp.concatenate([delta, delta], axis=1))).astype(BF16)
        pbuf[at, :] = p.astype(BF16)
        dsbuf[at, :] = ds
        dqa[at, :] += lax.dot_general(ds, keys, NN, preferred_element_type=F32)
    at = slice(xs[0] * ROWS, (xs[-1] + 1) * ROWS)
    dvt = lax.dot_general(dot[:, at], pbuf[at, :], NN, preferred_element_type=F32)
    dkt = lax.dot_general(qt[:, at], dsbuf[at, :], NN, preferred_element_type=F32)
    dva[a] += dvt[:, :BLOCK]
    dka[a] += dkt[:, :BLOCK]
    dva[b] += dvt[:, BLOCK:]
    dka[b] += dkt[:, BLOCK:]


def put_dq(dq, dqa):
    for x in range(NX):
        for c in range(2):
            for r in range(GS):
                start = x * ROWS + r * PIECE + c * TOK
                dq[x * 2 + c, :, r * HD : (r + 1) * HD] = (
                    dqa[start : start + TOK, :] * SCALE
                ).astype(BF16)


TILE_SCRATCH = [
    pltpu.VMEM((ALLROWS, HD), BF16),
    pltpu.VMEM((ALLROWS, HD), BF16),
    pltpu.VMEM((HD, ALLROWS), BF16),
    pltpu.VMEM((HD, ALLROWS), BF16),
    pltpu.VMEM((ALLROWS, 128), F32),
    pltpu.VMEM((ALLROWS, 128), F32),
    pltpu.VMEM((ALLROWS, 2 * BLOCK), BF16),
    pltpu.VMEM((ALLROWS, 2 * BLOCK), BF16),
    pltpu.VMEM((ALLROWS, HD), F32),
]


NEAR = ((0, 1), (1, 0), (3, 0), (1, 1), (3, 1), (2, 0), (2, 1))


def whole_kernel(
    q, k, v, o, do, lse, lists,
    gq, gk, gv,
    qg, dog, stg, kvg, dq, far_dq, dka, dva, dkv, land, acc_in, acc_out, final,
    o_buf, do_buf, lse_buf, rows_buf, stat_src, list_src, lsg, bias, diag,
    qs, dos, qt, dot, lseb, delb, pbuf, dsbuf, dqa, in_sem,
    kv_s, kv_r, kv_l, big_s, big_r, big_l, st_s, st_r, st_l, ls_s, ls_r, ls_l,
    ring_s, ring_r, cr_s, cr_r, crst_s, crst_r, crls_s, crls_r,
    dq_s, dq_r, red_s, red_r, out_s, out_r, out_l, kvo_s, kvo_r, kvo_l,
):
    y, x, z, core = coords()
    me = x * 2 + core
    loads = [
        pltpu.make_async_copy(src, dst, in_sem.at[i])
        for i, (src, dst) in enumerate(
            ((lists, rows_buf), (lse, lse_buf), (do, do_buf), (o, o_buf))
        )
    ]
    for c in loads:
        c.start()
    bar = pltpu.get_barrier_semaphore()
    signal_peers(bar, y, x, z, core, me)

    def cols(ref, g, width):
        return ref.at[:, pl.ds(pl.multiple_of(g * width, 128), width)]

    def to(n):
        return ((x + n[0]) % NX) * 2 + (core + n[1]) % 2

    def of(n):
        return ((x + NX - n[0]) % NX) * 2 + (core + n[1]) % 2

    def at(p):
        return device(y, p // 2, z, p % 2)

    def kv_slot(s, piece, zz):
        return kvg.at[zz, piece, s // 2, pl.ds((s % 2) * TOK, TOK), :]

    def kv_copy(p, piece):
        return remote(
            cols((k, v)[piece], p, HD), kv_slot(me, piece, z),
            kv_s.at[piece, p], kv_r.at[piece, me], at(p),
        )

    def kv_recv(s, piece):
        return remote(
            cols((k, v)[piece], s, HD), kv_slot(s, piece, z),
            kv_s.at[piece, s], kv_r.at[piece, s], at(s),
        )

    def big_copy(p, which):
        src, dst = ((q, qg), (do, dog))[which]
        return remote(
            cols(src, p, GW), dst.at[0, me], big_s.at[which, p], big_r.at[which, me], at(p)
        )

    def big_recv(s, which):
        src, dst = ((q, qg), (do, dog))[which]
        return remote(
            cols(src, s, GW), dst.at[0, s], big_s.at[which, s], big_r.at[which, s], at(s)
        )

    def st_copy(p):
        return remote(stat_src.at[p], stg.at[0, me], st_s.at[p], st_r.at[me], at(p))

    def st_recv(s):
        return remote(stat_src.at[s], stg.at[0, s], st_s.at[s], st_r.at[s], at(s))

    def ls_copy(d):
        xx = (x + d) % NX
        return remote(list_src, lsg.at[0, x], ls_s.at[xx], ls_r.at[x], device(y, xx, z, core))

    def ls_recv(d):
        xx = (x + NX - d) % NX
        return remote(list_src, lsg.at[0, xx], ls_s.at[xx], ls_r.at[xx], device(y, xx, z, core))

    def cross_copy(s, which):
        ref = (qg, dog)[which]
        return remote(
            ref.at[0, s], ref.at[1, s], cr_s.at[which, s], cr_r.at[which, s],
            device(3 - y, x, z, core),
        )

    kv_local = [
        pltpu.make_async_copy(cols((k, v)[piece], me, HD), kv_slot(me, piece, z), kv_l.at[piece])
        for piece in (0, 1)
    ]
    big_local = [
        pltpu.make_async_copy(cols(q, me, GW), qg.at[0, me], big_l.at[0]),
        pltpu.make_async_copy(cols(do, me, GW), dog.at[0, me], big_l.at[1]),
    ]
    for c in kv_local + big_local:
        c.start()

    loads[0].wait()
    list_src[...] = jnp.full((8, 128), -1, jnp.int32)
    list_src[0:2, 0:LISTW] = rows_buf[...]

    wait_peers(bar, y)
    for piece in (0, 1):
        for n in NEAR[1:] + NEAR[:1]:
            kv_copy(to(n), piece).start()
    for n in NEAR[:5]:
        for which in (0, 1):
            big_copy(to(n), which).start()
    for c in big_local:
        c.wait()

    @pl.when(y == 2)
    def _():
        for which in (0, 1):
            cross_copy(me, which).start()

    for d in range(1, NX):
        ls_copy(d).start()
    ls_local = pltpu.make_async_copy(list_src, lsg.at[0, x], ls_l)
    ls_local.start()

    for c in loads[1:]:
        c.wait()
    lane = lax.broadcasted_iota(jnp.int32, (TOK, 128), 1)
    for g in range(KVH):
        block = jnp.zeros((TOK, 128), F32)
        for r in range(GS):
            h = g * GS + r
            own = slice(h * HD, (h + 1) * HD)
            delta = jnp.sum(
                do_buf[:, own].astype(F32) * o_buf[:, own].astype(F32), axis=1, keepdims=True
            )
            block = jnp.where(lane == r, lse_buf[:, h : h + 1] * LOG2E, block)
            block = jnp.where(lane == 8 + r, delta, block)
        stat_src[g] = block

    for n in NEAR:
        st_copy(to(n)).start()
    st_local = pltpu.make_async_copy(stat_src.at[me], stg.at[0, me], st_l)
    st_local.start()
    for n in NEAR[5:]:
        for which in (0, 1):
            big_copy(to(n), which).start()

    def ring_copy(direction, piece, step):
        sign = (1, NZ - 1)[direction]
        back = (NZ - 1, 1)[direction]
        chunk = (z + back * step) % NZ
        part = kvg.at[chunk, piece]
        return remote(
            part, part, ring_s.at[direction, piece, step], ring_r.at[direction, piece, step],
            device(y, x, (z + sign) % NZ, core),
        )

    def ring_recv(direction, piece, step):
        back = (NZ - 1, 1)[direction]
        chunk = (z + back * (step + 1)) % NZ
        part = kvg.at[chunk, piece]
        return remote(
            part, part, ring_s.at[direction, piece, step], ring_r.at[direction, piece, step],
            device(y, x, (z + back) % NZ, core),
        )

    def forward(some):
        for n in some:
            s = of(n)
            for which in (0, 1):
                big_recv(s, which).wait_recv()

            @pl.when(y == 2)
            def _():
                for which in (0, 1):
                    cross_copy(s, which).start()

    def ring_start(piece):
        for n in NEAR:
            kv_recv(of(n), piece).wait_recv()
        kv_local[piece].wait()
        for direction in (0, 1):
            ring_copy(direction, piece, 0).start()

    def ring_step(step, piece):
        for direction, pc, steps in CHAINS:
            if pc == piece and step < steps:
                ring_recv(direction, piece, step).wait_recv()
                if step + 1 < steps:
                    ring_copy(direction, piece, step + 1).start()

    ring_start(0)
    ring_start(1)
    for ref in (dka, dva, dqa):
        ref[...] = jnp.zeros_like(ref)
    eye = identity()
    half = (z % 4) // 2
    base = y * 16
    row_tok = (z % 2) * PIECE + lax.broadcasted_iota(jnp.int32, (ROWS, 128), 0) % PIECE
    key_tok = lax.broadcasted_iota(jnp.int32, (ROWS, 128), 1)
    diag[0] = jnp.where(key_tok <= row_tok, 0.0, BIG)
    diag[1] = jnp.zeros((ROWS, 128), F32)

    forward(NEAR[:3])
    ring_step(0, 0)
    forward(NEAR[3:4])
    ring_step(0, 1)
    forward(NEAR[4:5])
    ring_step(1, 0)
    forward(NEAR[5:6])
    ring_step(1, 1)
    forward(NEAR[6:])

    for n in NEAR:
        st_recv(of(n)).wait_recv()
    for d in range(1, NX):
        ls_recv(d).wait_recv()
    st_local.wait()
    ls_local.wait()

    crst = remote(stg.at[0], stg.at[1], crst_s, crst_r, device(3 - y, x, z, core))
    crls = remote(lsg.at[0], lsg.at[1], crls_s, crls_r, device(3 - y, x, z, core))

    @pl.when(y == 2)
    def _():
        crst.start()
        crls.start()

    state = (qs, dos, qt, dot, lseb, delb)
    for piece in (0, 1):
        for i in (0, 1):
            load_rows(piece * 2 + i, 0, qg, dog, stg, eye, *state)
        turn_rows(piece * 2, piece * 2 + 2, eye, *state[:4])
        ring_step(2, piece)
    for xx in range(NX):
        bias[xx] = jnp.where(seen_bias(lsg, 0, xx, half, base) > 0.0, 0.0, BIG)

    own = z // 2
    side = (z % 2) * 2 - 1

    def column(i, carry):
        @pl.when(i == 3)
        def _():
            ring_step(3, 0)
            ring_step(3, 1)

        move = jnp.where(i == 1, side, jnp.where(i == 2, -side, jnp.where(i == 3, 2, 0)))
        zz = (own + move + 4) % 4
        cut = diag.at[jnp.where(i == 0, 0, 1)]
        rest = (pbuf, dsbuf, dqa, dka, dva)
        tile((0, 1, 2, 3), zz, zz + 4, kvg, bias, cut, *state, *rest)
        tile((2, 3), zz + 8, zz + 12, kvg, bias, cut, *state, *rest)
        return carry

    lax.fori_loop(0, 4, column, 0)
    put_dq(dq, dqa)

    def cross_dq(s):
        return remote(far_dq.at[s], land.at[me], dq_s.at[s], dq_r.at[me], device(3 - y, s // 2, z, s % 2))

    def cross_dq_recv(s):
        return remote(far_dq.at[s], land.at[s], dq_s.at[s], dq_r.at[s], device(3 - y, s // 2, z, s % 2))

    def dq_copy(p):
        return remote(dq.at[p], cols(gq, me, GW), out_s.at[p], out_r.at[me], at(p))

    def dq_recv(s):
        return remote(dq.at[s], cols(gq, s, GW), out_s.at[s], out_r.at[s], at(s))

    dq_local = pltpu.make_async_copy(dq.at[me], cols(gq, me, GW), out_l)
    for n in NEAR:
        dq_copy(to(n)).start()
    dq_local.start()

    @pl.when(y == 1)
    def _():
        for s in range(PEERS):
            for which in (0, 1):
                cross_copy(s, which).wait_recv()
        crst.wait_recv()
        crls.wait_recv()
        for xx in range(NX):
            load_rows(xx, 1, qg, dog, stg, eye, *state)
            bias[xx] = jnp.where(seen_bias(lsg, 1, xx, half, base) > 0.0, 0.0, BIG)
        turn_rows(0, NX, eye, *state[:4])
        dqa[...] = jnp.zeros_like(dqa)

    def red_copy(direction, piece, steps, step):
        sign = (1, NZ - 1)[direction]
        owner = (z + sign * (steps - step)) % NZ
        if step == 0:
            src = dkv.at[owner, piece]
        else:
            src = acc_out.at[direction, piece, step]
        return remote(
            src, acc_in.at[direction, piece, step],
            red_s.at[direction, piece, step], red_r.at[direction, piece, step],
            device(y, x, (z + sign) % NZ, core),
        )

    def red_step(direction, piece, steps, step):
        sign = (1, NZ - 1)[direction]
        owner = (z + sign * (steps - step)) % NZ
        red_copy(direction, piece, steps, step - 1).wait_recv()
        acc_out[direction, piece, step] = (
            acc_in[direction, piece, step - 1].astype(F32) + dkv[owner, piece].astype(F32)
        ).astype(BF16)
        red_copy(direction, piece, steps, step).start()

    def turn_column(zz):
        for xx in range(NX):
            for piece, ref, scale in ((0, dka, SCALE), (1, dva, 1.0)):
                low = (ref[zz + 4 * xx] * scale).astype(BF16)
                turned = lax.dot_general(eye, low, NT, preferred_element_type=F32).astype(BF16)
                dkv[2 * zz, piece, xx] = turned[:PIECE]
                dkv[2 * zz + 1, piece, xx] = turned[PIECE:]

    def finish(zz):
        @pl.when(y == 1)
        def _():
            rest = (pbuf, dsbuf, dqa, dka, dva)
            tile((0, 1, 2, 3), zz, zz + 4, kvg, bias, None, *state, *rest)
            tile((0, 1, 2, 3), zz + 8, zz + 12, kvg, bias, None, *state, *rest)
            turn_column(zz)

        @pl.when(y != 1)
        def _():
            turn_column(zz)

    long = ((0, 0, 4), (1, 1, 4))
    short = ((0, 1, 3), (1, 0, 3))

    def reduce_column(i, carry):
        move = jnp.where(i == 0, 2, jnp.where(i == 1, -side, jnp.where(i == 2, side, 0)))
        finish((own + move + 4) % 4)

        @pl.when(i == 0)
        def _():
            for c in long:
                red_copy(*c, 0).start()

        @pl.when(i == 1)
        def _():
            for c in short:
                red_copy(*c, 0).start()
            for c in long:
                red_step(*c, 1)

        @pl.when(i == 2)
        def _():
            for c in short:
                red_step(*c, 1)
            for c in long:
                red_step(*c, 2)

        return carry

    lax.fori_loop(0, 4, reduce_column, 0)

    @pl.when(y == 1)
    def _():
        put_dq(far_dq, dqa)
        for s in range(PEERS):
            cross_dq(s).start()

    for c in short:
        red_step(*c, 2)
    for c in long:
        red_step(*c, 3)

    def grad_copy(piece, p):
        return remote(
            final.at[piece, p // 2, pl.ds((p % 2) * TOK, TOK), :],
            cols((gk, gv)[piece], me, HD),
            kvo_s.at[piece, p], kvo_r.at[piece, me], at(p),
        )

    def grad_recv(piece, s):
        return remote(
            final.at[piece, s // 2, pl.ds((s % 2) * TOK, TOK), :],
            cols((gk, gv)[piece], s, HD),
            kvo_s.at[piece, s], kvo_r.at[piece, s], at(s),
        )

    grad_local = []
    for piece in (0, 1):
        (d0, s0), (d1, s1) = [(d, steps) for d, pc, steps in CHAINS if pc == piece]
        red_copy(d0, piece, s0, s0 - 1).wait_recv()
        red_copy(d1, piece, s1, s1 - 1).wait_recv()
        final[piece] = (
            acc_in[d0, piece, s0 - 1].astype(F32)
            + acc_in[d1, piece, s1 - 1].astype(F32)
            + dkv[z, piece].astype(F32)
        ).astype(BF16)
        for n in NEAR:
            grad_copy(piece, to(n)).start()
        grad_local.append(
            pltpu.make_async_copy(
                final.at[piece, x, pl.ds(core * TOK, TOK), :],
                cols((gk, gv)[piece], me, HD), kvo_l.at[piece],
            )
        )
        grad_local[piece].start()

    for n in NEAR:
        for i in (0, 1):
            kv_copy(to(n), i).wait_send()
            big_copy(to(n), i).wait_send()
        st_copy(to(n)).wait_send()
    for d in range(1, NX):
        ls_copy(d).wait_send()
    for direction, piece, steps in CHAINS:
        for step in range(steps):
            ring_copy(direction, piece, step).wait_send()

    @pl.when(y == 2)
    def _():
        for s in range(PEERS):
            for which in (0, 1):
                cross_copy(s, which).wait_send()
        crst.wait_send()
        crls.wait_send()


    @pl.when(y == 1)
    def _():
        for s in range(PEERS):
            cross_dq(s).wait_send()

    for direction, piece, steps in CHAINS:
        for step in range(steps):
            red_copy(direction, piece, steps, step).wait_send()
    for n in NEAR:
        for piece in (0, 1):
            grad_copy(piece, to(n)).wait_send()
            grad_recv(piece, of(n)).wait_recv()
        dq_copy(to(n)).wait_send()
        dq_recv(of(n)).wait_recv()
    for c in grad_local:
        c.wait()
    dq_local.wait()

    @pl.when(y == 2)
    def _():
        for g in range(PEERS):
            cross_dq_recv(g).wait_recv()
            own_cols = slice(g * GW, (g + 1) * GW)
            gq[:, own_cols] = (gq[:, own_cols].astype(F32) + land[g].astype(F32)).astype(BF16)


def whole(*args):
    vmem = pl.BlockSpec(memory_space=pltpu.VMEM)
    hbm = pl.BlockSpec(memory_space=pltpu.HBM)
    dma = pltpu.SemaphoreType.DMA
    return pl.pallas_call(
        whole_kernel,
        out_shape=(
            jax.ShapeDtypeStruct((TOK, QH * HD), BF16),
            jax.ShapeDtypeStruct((TOK, KVH * HD), BF16),
            jax.ShapeDtypeStruct((TOK, KVH * HD), BF16),
        ),
        in_specs=[hbm] * 7,
        out_specs=(vmem,) * 3,
        scratch_shapes=[
            pltpu.VMEM((2, PEERS, TOK, GW), BF16),
            pltpu.VMEM((2, PEERS, TOK, GW), BF16),
            pltpu.VMEM((2, PEERS, TOK, 128), F32),
            pltpu.VMEM((NZ, 2, NX, PIECE, HD), BF16),
            pltpu.VMEM((PEERS, TOK, GW), BF16),
            pltpu.VMEM((PEERS, TOK, GW), BF16),
            pltpu.VMEM((16, HD, BLOCK), F32),
            pltpu.VMEM((16, HD, BLOCK), F32),
            pltpu.VMEM((NZ, 2, NX, PIECE, HD), BF16),
            pltpu.VMEM((PEERS, TOK, GW), BF16),
            pltpu.VMEM((2, 2, 4, NX, PIECE, HD), BF16),
            pltpu.VMEM((2, 2, 4, NX, PIECE, HD), BF16),
            pltpu.VMEM((2, NX, PIECE, HD), BF16),
            pltpu.VMEM((TOK, QH * HD), BF16),
            pltpu.VMEM((TOK, QH * HD), BF16),
            pltpu.VMEM((TOK, QH), F32),
            pltpu.VMEM((2, LISTW), jnp.int32),
            pltpu.VMEM((KVH, TOK, 128), F32),
            pltpu.VMEM((8, 128), jnp.int32),
            pltpu.VMEM((2, NX, 8, 128), jnp.int32),
            pltpu.VMEM((NX, 16, 128), F32),
            pltpu.VMEM((2, ROWS, 128), F32),
            *TILE_SCRATCH,
            dma((4,)),
            dma((2, PEERS)), dma((2, PEERS)), dma((2,)),
            dma((2, PEERS)), dma((2, PEERS)), dma((2,)),
            dma((PEERS,)), dma((PEERS,)), dma,
            dma((NX,)), dma((NX,)), dma,
            dma((2, 2, 4)), dma((2, 2, 4)),
            dma((2, PEERS)), dma((2, PEERS)),
            dma, dma, dma, dma,
            dma((PEERS,)), dma((PEERS,)),
            dma((2, 2, 4)), dma((2, 2, 4)),
            dma((PEERS,)), dma((PEERS,)), dma,
            dma((2, PEERS)), dma((2, PEERS)), dma((2,)),
        ],
        compiler_params=pltpu.CompilerParams(
            collective_id=0, has_side_effects=True, vmem_limit_bytes=40 << 20
        ),
        name="whole",
    )(*args)


def emit_kernel(a, b, c, x, y, z, sem):
    copies = [
        pltpu.make_async_copy(src, dst, sem.at[i]) for i, (src, dst) in enumerate(((a, x), (b, y), (c, z)))
    ]
    for one in copies:
        one.start()
    for one in copies:
        one.wait()


def emit(*arrays):
    return pl.pallas_call(
        emit_kernel,
        out_shape=tuple(jax.ShapeDtypeStruct(a.shape, a.dtype) for a in arrays),
        in_specs=[pl.BlockSpec(memory_space=pltpu.VMEM)] * 3,
        out_specs=(pl.BlockSpec(memory_space=pltpu.HBM),) * 3,
        scratch_shapes=[pltpu.SemaphoreType.DMA((3,))],
        compiler_params=pltpu.CompilerParams(vmem_limit_bytes=1 << 20),
        name="emit",
    )(*arrays)


def local(query_act, key_act, value_act, attn_out, grad_out, log_sum, kv_lists):
    args = (query_act, key_act, value_act, attn_out, grad_out, log_sum, kv_lists)
    return emit(*whole(*(pltpu.with_memory_space_constraint(a, pltpu.HBM) for a in args)))


def solution(mesh):
    row = P(("blk", "head"), None)
    return jax.shard_map(
        local,
        mesh=mesh,
        in_specs=(row,) * 6 + (P("blk", None),),
        out_specs=(row,) * 3,
        check_vma=False,
    )
```

```python
import jax
import jax.numpy as jnp
from jax import lax
from jax.experimental import pallas as pl
from jax.experimental.pallas import tpu as pltpu
from jax.sharding import PartitionSpec as P

QH = 40
KVH = 8
HD = 128
BLOCK = 128
GS = QH // KVH
TOK = 32
GW = GS * HD
PIECE = 64
ROWS = GS * PIECE
NX = 4
NZ = 8
PEERS = 8
LISTW = 32
SCALE = HD ** -0.5
LOG2E = 1.4426950408889634
MESH = pl.DeviceIdType.MESH
F32 = jnp.float32
BF16 = jnp.bfloat16
NT = (((1,), (1,)), ((), ()))
NN = (((1,), (0,)), ((), ()))


def coords():
    blk = lax.axis_index("blk")
    head = lax.axis_index("head")
    y = blk // 8
    x = (blk // 2) % 4
    z = (blk % 2) * 4 + head // 2
    return y, x, z, head % 2


def device(y, x, z, core):
    return {"blk": (y * 4 + x) * 2 + z // 4, "head": (z % 4) * 2 + core}


def remote(src, dst, send_sem, recv_sem, device_id):
    return pltpu.make_async_remote_copy(
        src_ref=src,
        dst_ref=dst,
        send_sem=send_sem,
        recv_sem=recv_sem,
        device_id=device_id,
        device_id_type=MESH,
    )


def signal_peers(bar, y, x, z, core, me):
    for d in range(1, PEERS):
        p = (me + d) % PEERS
        pl.semaphore_signal(bar, inc=1, device_id=device(y, p // 2, z, p % 2), device_id_type=MESH)
    for step in (1, NZ - 1):
        pl.semaphore_signal(
            bar, inc=1, device_id=device(y, x, (z + step) % NZ, core), device_id_type=MESH
        )

    @pl.when((y == 1) | (y == 2))
    def _():
        for p in range(PEERS):
            pl.semaphore_signal(
                bar, inc=1, device_id=device(3 - y, p // 2, z, p % 2), device_id_type=MESH
            )


def wait_peers(bar, y):
    pl.semaphore_wait(bar, PEERS - 1 + 2 + PEERS * ((y == 1) | (y == 2)).astype(jnp.int32))


CHAINS = ((0, 0, 4), (0, 1, 3), (1, 1, 4), (1, 0, 3))


BIG = 1e30
ALLROWS = NX * ROWS


def rows_of(x):
    return slice(x * ROWS, (x + 1) * ROWS)


def seen_bias(lists, part, x, half, base):
    entries = lists[part, x, pl.ds(half, 1), :]
    block = base + lax.broadcasted_iota(jnp.int32, (16, 128), 0)
    hit = jnp.max(jnp.where(entries == block, 1.0, 0.0), axis=1, keepdims=True)
    return jnp.broadcast_to(hit, (16, 128))


def load_rows(x, part, qg, dog, stg, eye, qs, dos, qt, dot, lseb, delb):
    for c in range(2):
        st = stg[part, x * 2 + c]
        for r in range(GS):
            start = x * ROWS + r * PIECE + c * TOK
            at = slice(start, start + TOK)
            col = slice(r * HD, (r + 1) * HD)
            qs[at, :] = qg[part, x * 2 + c, :, col]
            dos[at, :] = dog[part, x * 2 + c, :, col]
            lseb[at, :] = jnp.broadcast_to(st[:, r : r + 1], (TOK, 128))
            delb[at, :] = jnp.broadcast_to(st[:, 8 + r : 9 + r], (TOK, 128))


def turn_rows(lo, hi, eye, qs, dos, qt, dot):
    at = slice(lo * ROWS, hi * ROWS)
    qt[:, at] = lax.dot_general(eye, qs[at, :], NT, preferred_element_type=F32).astype(BF16)
    dot[:, at] = lax.dot_general(eye, dos[at, :], NT, preferred_element_type=F32).astype(BF16)


def identity():
    r_id = lax.broadcasted_iota(jnp.int32, (128, 128), 0)
    c_id = lax.broadcasted_iota(jnp.int32, (128, 128), 1)
    return jnp.where(r_id == c_id, 1.0, 0.0).astype(BF16)


def key_block(kvg, piece, b):
    zz = (b % 4) * 2
    return jnp.concatenate([kvg[zz, piece, b // 4], kvg[zz + 1, piece, b // 4]], axis=0)


def tile(xs, a, b, kvg, bias, diag, eye, qs, dos, qt, dot, lseb, delb, pbuf, dsbuf, dqa, dka, dva):
    keys = jnp.concatenate([key_block(kvg, 0, a), key_block(kvg, 0, b)], axis=0)
    values = jnp.concatenate([key_block(kvg, 1, a), key_block(kvg, 1, b)], axis=0)
    turned = lax.dot_general(eye, keys, NT, preferred_element_type=F32).astype(BF16)
    for x in xs:
        at = rows_of(x)
        s = lax.dot_general(qs[at, :], keys, NT, preferred_element_type=F32)
        dp = lax.dot_general(dos[at, :], values, NT, preferred_element_type=F32)
        lse_a = lseb[at, :] + bias[x, pl.ds(a, 1), :]
        lse_b = lseb[at, :] + bias[x, pl.ds(b, 1), :]
        if diag is not None:
            if x % 2 == 0 and x == xs[0]:
                lse_a = lse_a + diag[...]
            if x % 2 == 1 and x == xs[0] + 1:
                lse_b = lse_b + diag[...]
        p = jnp.exp2(s * (SCALE * LOG2E) - jnp.concatenate([lse_a, lse_b], axis=1))
        delta = delb[at, :]
        ds = (p * (dp - jnp.concatenate([delta, delta], axis=1))).astype(BF16)
        pbuf[at, :] = p.astype(BF16)
        dsbuf[at, :] = ds
    at = slice(xs[0] * ROWS, (xs[-1] + 1) * ROWS)
    dvt = lax.dot_general(dot[:, at], pbuf[at, :], NN, preferred_element_type=F32)
    dkt = lax.dot_general(qt[:, at], dsbuf[at, :], NN, preferred_element_type=F32)
    dqa[:, at] += lax.dot_general(turned, dsbuf[at, :], NT, preferred_element_type=F32)
    dva[a] += dvt[:, :BLOCK]
    dka[a] += dkt[:, :BLOCK]
    dva[b] += dvt[:, BLOCK:]
    dka[b] += dkt[:, BLOCK:]


def put_dq(dq, dqa, eye):
    for j in range(ALLROWS // 128):
        low = (dqa[:, j * 128 : (j + 1) * 128] * SCALE).astype(BF16)
        rows = lax.dot_general(eye, low, NT, preferred_element_type=F32).astype(BF16)
        for i in range(128 // TOK):
            x, rest = divmod(j * 4 + i, 2 * GS)
            r, c = divmod(rest, 2)
            dq[x * 2 + c, :, r * HD : (r + 1) * HD] = rows[i * TOK : (i + 1) * TOK]


TILE_SCRATCH = [
    pltpu.VMEM((ALLROWS, HD), BF16),
    pltpu.VMEM((ALLROWS, HD), BF16),
    pltpu.VMEM((HD, ALLROWS), BF16),
    pltpu.VMEM((HD, ALLROWS), BF16),
    pltpu.VMEM((ALLROWS, 128), F32),
    pltpu.VMEM((ALLROWS, 128), F32),
    pltpu.VMEM((2, ALLROWS, 2 * BLOCK), BF16),
    pltpu.VMEM((2, ALLROWS, 2 * BLOCK), BF16),
    pltpu.VMEM((HD, ALLROWS), F32),
]


NEAR = ((0, 1), (1, 0), (3, 0), (1, 1), (3, 1), (2, 0), (2, 1))


def whole_kernel(
    q, k, v, o, do, lse, lists,
    gq, gk, gv,
    qg, dog, stg, kvg, dq, far_dq, dka, dva, dkv, land, acc_in, acc_out, final,
    o_buf, do_buf, lse_buf, rows_buf, stat_src, list_src, lsg, bias, diag,
    qs, dos, qt, dot, lseb, delb, pbuf, dsbuf, dqa, in_sem,
    kv_s, kv_r, kv_l, big_s, big_r, big_l, st_s, st_r, st_l, ls_s, ls_r, ls_l,
    ring_s, ring_r, cr_s, cr_r, crst_s, crst_r, crls_s, crls_r,
    dq_s, dq_r, red_s, red_r, out_s, out_r, out_l, kvo_s, kvo_r, kvo_l,
):
    y, x, z, core = coords()
    me = x * 2 + core
    loads = [
        pltpu.make_async_copy(src, dst, in_sem.at[i])
        for i, (src, dst) in enumerate(
            ((lists, rows_buf), (lse, lse_buf), (do, do_buf), (o, o_buf))
        )
    ]
    for c in loads:
        c.start()
    bar = pltpu.get_barrier_semaphore()
    signal_peers(bar, y, x, z, core, me)

    def cols(ref, g, width):
        return ref.at[:, pl.ds(pl.multiple_of(g * width, 128), width)]

    def to(n):
        return ((x + n[0]) % NX) * 2 + (core + n[1]) % 2

    def of(n):
        return ((x + NX - n[0]) % NX) * 2 + (core + n[1]) % 2

    def at(p):
        return device(y, p // 2, z, p % 2)

    def kv_slot(s, piece, zz):
        return kvg.at[zz, piece, s // 2, pl.ds((s % 2) * TOK, TOK), :]

    def kv_copy(p, piece):
        return remote(
            cols((k, v)[piece], p, HD), kv_slot(me, piece, z),
            kv_s.at[piece, p], kv_r.at[piece, me], at(p),
        )

    def kv_recv(s, piece):
        return remote(
            cols((k, v)[piece], s, HD), kv_slot(s, piece, z),
            kv_s.at[piece, s], kv_r.at[piece, s], at(s),
        )

    def big_copy(p, which):
        src, dst = ((q, qg), (do, dog))[which]
        return remote(
            cols(src, p, GW), dst.at[0, me], big_s.at[which, p], big_r.at[which, me], at(p)
        )

    def big_recv(s, which):
        src, dst = ((q, qg), (do, dog))[which]
        return remote(
            cols(src, s, GW), dst.at[0, s], big_s.at[which, s], big_r.at[which, s], at(s)
        )

    def st_copy(p):
        return remote(stat_src.at[p], stg.at[0, me], st_s.at[p], st_r.at[me], at(p))

    def st_recv(s):
        return remote(stat_src.at[s], stg.at[0, s], st_s.at[s], st_r.at[s], at(s))

    def ls_copy(d):
        xx = (x + d) % NX
        return remote(list_src, lsg.at[0, x], ls_s.at[xx], ls_r.at[x], device(y, xx, z, core))

    def ls_recv(d):
        xx = (x + NX - d) % NX
        return remote(list_src, lsg.at[0, xx], ls_s.at[xx], ls_r.at[xx], device(y, xx, z, core))

    def cross_copy(s, which):
        ref = (qg, dog)[which]
        return remote(
            ref.at[0, s], ref.at[1, s], cr_s.at[which, s], cr_r.at[which, s],
            device(3 - y, x, z, core),
        )

    kv_local = [
        pltpu.make_async_copy(cols((k, v)[piece], me, HD), kv_slot(me, piece, z), kv_l.at[piece])
        for piece in (0, 1)
    ]
    big_local = [
        pltpu.make_async_copy(cols(q, me, GW), qg.at[0, me], big_l.at[0]),
        pltpu.make_async_copy(cols(do, me, GW), dog.at[0, me], big_l.at[1]),
    ]
    for c in kv_local + big_local:
        c.start()

    loads[0].wait()
    list_src[...] = jnp.full((8, 128), -1, jnp.int32)
    list_src[0:2, 0:LISTW] = rows_buf[...]

    wait_peers(bar, y)
    for piece in (0, 1):
        for n in NEAR[1:] + NEAR[:1]:
            kv_copy(to(n), piece).start()
    for n in NEAR[:5]:
        for which in (0, 1):
            big_copy(to(n), which).start()
    for c in big_local:
        c.wait()

    @pl.when(y == 2)
    def _():
        for which in (0, 1):
            cross_copy(me, which).start()

    for d in range(1, NX):
        ls_copy(d).start()
    ls_local = pltpu.make_async_copy(list_src, lsg.at[0, x], ls_l)
    ls_local.start()

    for c in loads[1:]:
        c.wait()
    lane = lax.broadcasted_iota(jnp.int32, (TOK, 128), 1)
    for g in range(KVH):
        block = jnp.zeros((TOK, 128), F32)
        for r in range(GS):
            h = g * GS + r
            own = slice(h * HD, (h + 1) * HD)
            delta = jnp.sum(
                do_buf[:, own].astype(F32) * o_buf[:, own].astype(F32), axis=1, keepdims=True
            )
            block = jnp.where(lane == r, lse_buf[:, h : h + 1] * LOG2E, block)
            block = jnp.where(lane == 8 + r, delta, block)
        stat_src[g] = block

    for n in NEAR:
        st_copy(to(n)).start()
    st_local = pltpu.make_async_copy(stat_src.at[me], stg.at[0, me], st_l)
    st_local.start()
    for n in NEAR[5:]:
        for which in (0, 1):
            big_copy(to(n), which).start()

    def ring_copy(direction, piece, step):
        sign = (1, NZ - 1)[direction]
        back = (NZ - 1, 1)[direction]
        chunk = (z + back * step) % NZ
        part = kvg.at[chunk, piece]
        return remote(
            part, part, ring_s.at[direction, piece, step], ring_r.at[direction, piece, step],
            device(y, x, (z + sign) % NZ, core),
        )

    def ring_recv(direction, piece, step):
        back = (NZ - 1, 1)[direction]
        chunk = (z + back * (step + 1)) % NZ
        part = kvg.at[chunk, piece]
        return remote(
            part, part, ring_s.at[direction, piece, step], ring_r.at[direction, piece, step],
            device(y, x, (z + back) % NZ, core),
        )

    def forward(some):
        for n in some:
            s = of(n)
            for which in (0, 1):
                big_recv(s, which).wait_recv()

            @pl.when(y == 2)
            def _():
                for which in (0, 1):
                    cross_copy(s, which).start()

    def ring_start(piece):
        for n in NEAR:
            kv_recv(of(n), piece).wait_recv()
        kv_local[piece].wait()
        for direction in (0, 1):
            ring_copy(direction, piece, 0).start()

    def ring_step(step, piece):
        for direction, pc, steps in CHAINS:
            if pc == piece and step < steps:
                ring_recv(direction, piece, step).wait_recv()
                if step + 1 < steps:
                    ring_copy(direction, piece, step + 1).start()

    ring_start(0)
    ring_start(1)
    for ref in (dka, dva, dqa):
        ref[...] = jnp.zeros_like(ref)
    eye = identity()
    half = (z % 4) // 2
    base = y * 16
    row_tok = (z % 2) * PIECE + lax.broadcasted_iota(jnp.int32, (ROWS, 128), 0) % PIECE
    key_tok = lax.broadcasted_iota(jnp.int32, (ROWS, 128), 1)
    diag[0] = jnp.where(key_tok <= row_tok, 0.0, BIG)
    diag[1] = jnp.zeros((ROWS, 128), F32)

    forward(NEAR[:3])
    ring_step(0, 0)
    forward(NEAR[3:4])
    ring_step(0, 1)
    forward(NEAR[4:5])
    ring_step(1, 0)
    forward(NEAR[5:6])
    ring_step(1, 1)
    forward(NEAR[6:])

    for n in NEAR:
        st_recv(of(n)).wait_recv()
    for d in range(1, NX):
        ls_recv(d).wait_recv()
    st_local.wait()
    ls_local.wait()

    crst = remote(stg.at[0], stg.at[1], crst_s, crst_r, device(3 - y, x, z, core))
    crls = remote(lsg.at[0], lsg.at[1], crls_s, crls_r, device(3 - y, x, z, core))

    @pl.when(y == 2)
    def _():
        crst.start()
        crls.start()

    state = (qs, dos, qt, dot, lseb, delb)
    for piece in (0, 1):
        for i in (0, 1):
            load_rows(piece * 2 + i, 0, qg, dog, stg, eye, *state)
        turn_rows(piece * 2, piece * 2 + 2, eye, *state[:4])
        ring_step(2, piece)
    for xx in range(NX):
        bias[xx] = jnp.where(seen_bias(lsg, 0, xx, half, base) > 0.0, 0.0, BIG)

    own = z // 2
    side = (z % 2) * 2 - 1

    def column(i, carry):
        @pl.when(i == 3)
        def _():
            ring_step(3, 0)
            ring_step(3, 1)

        move = jnp.where(i == 1, side, jnp.where(i == 2, -side, jnp.where(i == 3, 2, 0)))
        zz = (own + move + 4) % 4
        cut = diag.at[jnp.where(i == 0, 0, 1)]
        rest = [(pbuf.at[n], dsbuf.at[n], dqa, dka, dva) for n in (0, 1)]
        tile((0, 1, 2, 3), zz, zz + 4, kvg, bias, cut, eye, *state, *rest[0])
        tile((2, 3), zz + 8, zz + 12, kvg, bias, cut, eye, *state, *rest[1])
        return carry

    lax.fori_loop(0, 4, column, 0)
    put_dq(dq, dqa, eye)

    def cross_dq(s):
        return remote(far_dq.at[s], land.at[me], dq_s.at[s], dq_r.at[me], device(3 - y, s // 2, z, s % 2))

    def cross_dq_recv(s):
        return remote(far_dq.at[s], land.at[s], dq_s.at[s], dq_r.at[s], device(3 - y, s // 2, z, s % 2))

    def dq_copy(p):
        return remote(dq.at[p], cols(gq, me, GW), out_s.at[p], out_r.at[me], at(p))

    def dq_recv(s):
        return remote(dq.at[s], cols(gq, s, GW), out_s.at[s], out_r.at[s], at(s))

    dq_local = pltpu.make_async_copy(dq.at[me], cols(gq, me, GW), out_l)
    for n in NEAR:
        dq_copy(to(n)).start()
    dq_local.start()

    @pl.when(y == 1)
    def _():
        for s in range(PEERS):
            for which in (0, 1):
                cross_copy(s, which).wait_recv()
        crst.wait_recv()
        crls.wait_recv()
        for xx in range(NX):
            load_rows(xx, 1, qg, dog, stg, eye, *state)
            bias[xx] = jnp.where(seen_bias(lsg, 1, xx, half, base) > 0.0, 0.0, BIG)
        turn_rows(0, NX, eye, *state[:4])
        dqa[...] = jnp.zeros_like(dqa)

    def red_copy(direction, piece, steps, step):
        sign = (1, NZ - 1)[direction]
        owner = (z + sign * (steps - step)) % NZ
        if step == 0:
            src = dkv.at[owner, piece]
        else:
            src = acc_out.at[direction, piece, step]
        return remote(
            src, acc_in.at[direction, piece, step],
            red_s.at[direction, piece, step], red_r.at[direction, piece, step],
            device(y, x, (z + sign) % NZ, core),
        )

    def red_step(direction, piece, steps, step):
        sign = (1, NZ - 1)[direction]
        owner = (z + sign * (steps - step)) % NZ
        red_copy(direction, piece, steps, step - 1).wait_recv()
        acc_out[direction, piece, step] = (
            acc_in[direction, piece, step - 1].astype(F32) + dkv[owner, piece].astype(F32)
        ).astype(BF16)
        red_copy(direction, piece, steps, step).start()

    def turn_column(zz):
        for xx in range(NX):
            for piece, ref, scale in ((0, dka, SCALE), (1, dva, 1.0)):
                low = (ref[zz + 4 * xx] * scale).astype(BF16)
                turned = lax.dot_general(eye, low, NT, preferred_element_type=F32).astype(BF16)
                dkv[2 * zz, piece, xx] = turned[:PIECE]
                dkv[2 * zz + 1, piece, xx] = turned[PIECE:]

    def finish(zz):
        @pl.when(y == 1)
        def _():
            rest = [(pbuf.at[n], dsbuf.at[n], dqa, dka, dva) for n in (0, 1)]
            tile((0, 1, 2, 3), zz, zz + 4, kvg, bias, None, eye, *state, *rest[0])
            tile((0, 1, 2, 3), zz + 8, zz + 12, kvg, bias, None, eye, *state, *rest[1])
            turn_column(zz)

        @pl.when(y != 1)
        def _():
            turn_column(zz)

    long = ((0, 0, 4), (1, 1, 4))
    short = ((0, 1, 3), (1, 0, 3))

    def reduce_column(i, carry):
        move = jnp.where(i == 0, 2, jnp.where(i == 1, -side, jnp.where(i == 2, side, 0)))
        finish((own + move + 4) % 4)

        @pl.when(i == 0)
        def _():
            for c in long:
                red_copy(*c, 0).start()

        @pl.when(i == 1)
        def _():
            for c in short:
                red_copy(*c, 0).start()
            for c in long:
                red_step(*c, 1)

        @pl.when(i == 2)
        def _():
            for c in short:
                red_step(*c, 1)
            for c in long:
                red_step(*c, 2)

        return carry

    lax.fori_loop(0, 4, reduce_column, 0)

    @pl.when(y == 1)
    def _():
        put_dq(far_dq, dqa, eye)
        for s in range(PEERS):
            cross_dq(s).start()

    for c in short:
        red_step(*c, 2)
    for c in long:
        red_step(*c, 3)

    def grad_copy(piece, p):
        return remote(
            final.at[piece, p // 2, pl.ds((p % 2) * TOK, TOK), :],
            cols((gk, gv)[piece], me, HD),
            kvo_s.at[piece, p], kvo_r.at[piece, me], at(p),
        )

    def grad_recv(piece, s):
        return remote(
            final.at[piece, s // 2, pl.ds((s % 2) * TOK, TOK), :],
            cols((gk, gv)[piece], s, HD),
            kvo_s.at[piece, s], kvo_r.at[piece, s], at(s),
        )

    grad_local = []
    for piece in (0, 1):
        (d0, s0), (d1, s1) = [(d, steps) for d, pc, steps in CHAINS if pc == piece]
        red_copy(d0, piece, s0, s0 - 1).wait_recv()
        red_copy(d1, piece, s1, s1 - 1).wait_recv()
        final[piece] = (
            acc_in[d0, piece, s0 - 1].astype(F32)
            + acc_in[d1, piece, s1 - 1].astype(F32)
            + dkv[z, piece].astype(F32)
        ).astype(BF16)
        for n in NEAR:
            grad_copy(piece, to(n)).start()
        grad_local.append(
            pltpu.make_async_copy(
                final.at[piece, x, pl.ds(core * TOK, TOK), :],
                cols((gk, gv)[piece], me, HD), kvo_l.at[piece],
            )
        )
        grad_local[piece].start()

    for n in NEAR:
        for i in (0, 1):
            kv_copy(to(n), i).wait_send()
            big_copy(to(n), i).wait_send()
        st_copy(to(n)).wait_send()
    for d in range(1, NX):
        ls_copy(d).wait_send()
    for direction, piece, steps in CHAINS:
        for step in range(steps):
            ring_copy(direction, piece, step).wait_send()

    @pl.when(y == 2)
    def _():
        for s in range(PEERS):
            for which in (0, 1):
                cross_copy(s, which).wait_send()
        crst.wait_send()
        crls.wait_send()


    @pl.when(y == 1)
    def _():
        for s in range(PEERS):
            cross_dq(s).wait_send()

    for direction, piece, steps in CHAINS:
        for step in range(steps):
            red_copy(direction, piece, steps, step).wait_send()
    for n in NEAR:
        for piece in (0, 1):
            grad_copy(piece, to(n)).wait_send()
            grad_recv(piece, of(n)).wait_recv()
        dq_copy(to(n)).wait_send()
        dq_recv(of(n)).wait_recv()
    for c in grad_local:
        c.wait()
    dq_local.wait()

    @pl.when(y == 2)
    def _():
        for g in range(PEERS):
            cross_dq_recv(g).wait_recv()
            own_cols = slice(g * GW, (g + 1) * GW)
            gq[:, own_cols] = (gq[:, own_cols].astype(F32) + land[g].astype(F32)).astype(BF16)


def whole(*args):
    vmem = pl.BlockSpec(memory_space=pltpu.VMEM)
    hbm = pl.BlockSpec(memory_space=pltpu.HBM)
    dma = pltpu.SemaphoreType.DMA
    return pl.pallas_call(
        whole_kernel,
        out_shape=(
            jax.ShapeDtypeStruct((TOK, QH * HD), BF16),
            jax.ShapeDtypeStruct((TOK, KVH * HD), BF16),
            jax.ShapeDtypeStruct((TOK, KVH * HD), BF16),
        ),
        in_specs=[hbm] * 7,
        out_specs=(vmem,) * 3,
        scratch_shapes=[
            pltpu.VMEM((2, PEERS, TOK, GW), BF16),
            pltpu.VMEM((2, PEERS, TOK, GW), BF16),
            pltpu.VMEM((2, PEERS, TOK, 128), F32),
            pltpu.VMEM((NZ, 2, NX, PIECE, HD), BF16),
            pltpu.VMEM((PEERS, TOK, GW), BF16),
            pltpu.VMEM((PEERS, TOK, GW), BF16),
            pltpu.VMEM((16, HD, BLOCK), F32),
            pltpu.VMEM((16, HD, BLOCK), F32),
            pltpu.VMEM((NZ, 2, NX, PIECE, HD), BF16),
            pltpu.VMEM((PEERS, TOK, GW), BF16),
            pltpu.VMEM((2, 2, 4, NX, PIECE, HD), BF16),
            pltpu.VMEM((2, 2, 4, NX, PIECE, HD), BF16),
            pltpu.VMEM((2, NX, PIECE, HD), BF16),
            pltpu.VMEM((TOK, QH * HD), BF16),
            pltpu.VMEM((TOK, QH * HD), BF16),
            pltpu.VMEM((TOK, QH), F32),
            pltpu.VMEM((2, LISTW), jnp.int32),
            pltpu.VMEM((KVH, TOK, 128), F32),
            pltpu.VMEM((8, 128), jnp.int32),
            pltpu.VMEM((2, NX, 8, 128), jnp.int32),
            pltpu.VMEM((NX, 16, 128), F32),
            pltpu.VMEM((2, ROWS, 128), F32),
            *TILE_SCRATCH,
            dma((4,)),
            dma((2, PEERS)), dma((2, PEERS)), dma((2,)),
            dma((2, PEERS)), dma((2, PEERS)), dma((2,)),
            dma((PEERS,)), dma((PEERS,)), dma,
            dma((NX,)), dma((NX,)), dma,
            dma((2, 2, 4)), dma((2, 2, 4)),
            dma((2, PEERS)), dma((2, PEERS)),
            dma, dma, dma, dma,
            dma((PEERS,)), dma((PEERS,)),
            dma((2, 2, 4)), dma((2, 2, 4)),
            dma((PEERS,)), dma((PEERS,)), dma,
            dma((2, PEERS)), dma((2, PEERS)), dma((2,)),
        ],
        compiler_params=pltpu.CompilerParams(
            collective_id=0, has_side_effects=True, vmem_limit_bytes=40 << 20
        ),
        name="whole",
    )(*args)


def emit_kernel(a, b, c, x, y, z, sem):
    copies = [
        pltpu.make_async_copy(src, dst, sem.at[i]) for i, (src, dst) in enumerate(((a, x), (b, y), (c, z)))
    ]
    for one in copies:
        one.start()
    for one in copies:
        one.wait()


def emit(*arrays):
    return pl.pallas_call(
        emit_kernel,
        out_shape=tuple(jax.ShapeDtypeStruct(a.shape, a.dtype) for a in arrays),
        in_specs=[pl.BlockSpec(memory_space=pltpu.VMEM)] * 3,
        out_specs=(pl.BlockSpec(memory_space=pltpu.HBM),) * 3,
        scratch_shapes=[pltpu.SemaphoreType.DMA((3,))],
        compiler_params=pltpu.CompilerParams(vmem_limit_bytes=1 << 20),
        name="emit",
    )(*arrays)


def local(query_act, key_act, value_act, attn_out, grad_out, log_sum, kv_lists):
    args = (query_act, key_act, value_act, attn_out, grad_out, log_sum, kv_lists)
    return emit(*whole(*(pltpu.with_memory_space_constraint(a, pltpu.HBM) for a in args)))


def solution(mesh):
    row = P(("blk", "head"), None)
    return jax.shard_map(
        local,
        mesh=mesh,
        in_specs=(row,) * 6 + (P("blk", None),),
        out_specs=(row,) * 3,
        check_vma=False,
    )
```

```python
import jax
import jax.numpy as jnp
from jax import lax
from jax.experimental import pallas as pl
from jax.experimental.pallas import tpu as pltpu
from jax.sharding import PartitionSpec as P

QH = 40
KVH = 8
HD = 128
BLOCK = 128
GS = QH // KVH
TOK = 32
GW = GS * HD
PIECE = 64
ROWS = GS * PIECE
NX = 4
NZ = 8
PEERS = 8
LISTW = 32
SCALE = HD ** -0.5
LOG2E = 1.4426950408889634
MESH = pl.DeviceIdType.MESH
F32 = jnp.float32
BF16 = jnp.bfloat16
NT = (((1,), (1,)), ((), ()))
NN = (((1,), (0,)), ((), ()))


def coords():
    blk = lax.axis_index("blk")
    head = lax.axis_index("head")
    y = blk // 8
    x = (blk // 2) % 4
    z = (blk % 2) * 4 + head // 2
    return y, x, z, head % 2


def device(y, x, z, core):
    return {"blk": (y * 4 + x) * 2 + z // 4, "head": (z % 4) * 2 + core}


def remote(src, dst, send_sem, recv_sem, device_id):
    return pltpu.make_async_remote_copy(
        src_ref=src,
        dst_ref=dst,
        send_sem=send_sem,
        recv_sem=recv_sem,
        device_id=device_id,
        device_id_type=MESH,
    )


def signal_peers(bar, y, x, z, core, me):
    for d in range(1, PEERS):
        p = (me + d) % PEERS
        pl.semaphore_signal(bar, inc=1, device_id=device(y, p // 2, z, p % 2), device_id_type=MESH)
    for step in (1, NZ - 1):
        pl.semaphore_signal(
            bar, inc=1, device_id=device(y, x, (z + step) % NZ, core), device_id_type=MESH
        )

    @pl.when((y == 1) | (y == 2))
    def _():
        for p in range(PEERS):
            pl.semaphore_signal(
                bar, inc=1, device_id=device(3 - y, p // 2, z, p % 2), device_id_type=MESH
            )


def wait_peers(bar, y):
    pl.semaphore_wait(bar, PEERS - 1 + 2 + PEERS * ((y == 1) | (y == 2)).astype(jnp.int32))


CHAINS = ((0, 0, 4), (0, 1, 3), (1, 1, 4), (1, 0, 3))


BIG = 1e30
ALLROWS = NX * ROWS


def rows_of(x):
    return slice(x * ROWS, (x + 1) * ROWS)


def seen_bias(lists, part, x, half, base):
    entries = lists[part, x, pl.ds(half, 1), :]
    block = base + lax.broadcasted_iota(jnp.int32, (16, 128), 0)
    hit = jnp.max(jnp.where(entries == block, 1.0, 0.0), axis=1, keepdims=True)
    return jnp.broadcast_to(hit, (16, 128))


def load_rows(x, part, qg, dog, stg, eye, qs, dos, qt, dot, lseb, delb):
    for c in range(2):
        st = stg[part, x * 2 + c]
        for r in range(GS):
            start = x * ROWS + r * PIECE + c * TOK
            at = slice(start, start + TOK)
            col = slice(r * HD, (r + 1) * HD)
            qs[at, :] = qg[part, x * 2 + c, :, col]
            dos[at, :] = dog[part, x * 2 + c, :, col]
            lseb[at, :] = jnp.broadcast_to(st[:, r : r + 1], (TOK, 128))
            delb[at, :] = jnp.broadcast_to(st[:, 8 + r : 9 + r], (TOK, 128))


def turn_rows(lo, hi, eye, qs, dos, qt, dot):
    at = slice(lo * ROWS, hi * ROWS)
    qt[:, at] = lax.dot_general(eye, qs[at, :], NT, preferred_element_type=F32).astype(BF16)
    dot[:, at] = lax.dot_general(eye, dos[at, :], NT, preferred_element_type=F32).astype(BF16)


def identity():
    r_id = lax.broadcasted_iota(jnp.int32, (128, 128), 0)
    c_id = lax.broadcasted_iota(jnp.int32, (128, 128), 1)
    return jnp.where(r_id == c_id, 1.0, 0.0).astype(BF16)


def key_block(kvg, piece, b):
    zz = (b % 4) * 2
    return jnp.concatenate([kvg[zz, piece, b // 4], kvg[zz + 1, piece, b // 4]], axis=0)


def tile(xs, a, b, kvg, bias, diag, eye, qs, dos, qt, dot, lseb, delb, pbuf, dsbuf, dqa, dka, dva):
    keys = jnp.concatenate([key_block(kvg, 0, a), key_block(kvg, 0, b)], axis=0)
    values = jnp.concatenate([key_block(kvg, 1, a), key_block(kvg, 1, b)], axis=0)
    turned = lax.dot_general(eye, keys, NT, preferred_element_type=F32).astype(BF16)
    for x in xs:
        at = rows_of(x)
        s = lax.dot_general(qs[at, :], keys, NT, preferred_element_type=F32)
        dp = lax.dot_general(dos[at, :], values, NT, preferred_element_type=F32)
        lse_a = lseb[at, :] + bias[x, pl.ds(a, 1), :]
        lse_b = lseb[at, :] + bias[x, pl.ds(b, 1), :]
        if diag is not None:
            if x % 2 == 0 and x == xs[0]:
                lse_a = lse_a + diag[...]
            if x % 2 == 1 and x == xs[0] + 1:
                lse_b = lse_b + diag[...]
        p = jnp.exp2(s * (SCALE * LOG2E) - jnp.concatenate([lse_a, lse_b], axis=1))
        delta = delb[at, :]
        ds = (p * (dp - jnp.concatenate([delta, delta], axis=1))).astype(BF16)
        pbuf[at, :] = p.astype(BF16)
        dsbuf[at, :] = ds
    at = slice(xs[0] * ROWS, (xs[-1] + 1) * ROWS)
    dvt = lax.dot_general(dot[:, at], pbuf[at, :], NN, preferred_element_type=F32)
    dkt = lax.dot_general(qt[:, at], dsbuf[at, :], NN, preferred_element_type=F32)
    dqa[:, at] += lax.dot_general(turned, dsbuf[at, :], NT, preferred_element_type=F32)
    dva[a] += dvt[:, :BLOCK]
    dka[a] += dkt[:, :BLOCK]
    dva[b] += dvt[:, BLOCK:]
    dka[b] += dkt[:, BLOCK:]


def put_dq(dq, dqa, eye):
    for j in range(ALLROWS // 128):
        low = (dqa[:, j * 128 : (j + 1) * 128] * SCALE).astype(BF16)
        rows = lax.dot_general(eye, low, NT, preferred_element_type=F32).astype(BF16)
        for i in range(128 // TOK):
            x, rest = divmod(j * 4 + i, 2 * GS)
            r, c = divmod(rest, 2)
            dq[x * 2 + c, :, r * HD : (r + 1) * HD] = rows[i * TOK : (i + 1) * TOK]


TILE_SCRATCH = [
    pltpu.VMEM((ALLROWS, HD), BF16),
    pltpu.VMEM((ALLROWS, HD), BF16),
    pltpu.VMEM((HD, ALLROWS), BF16),
    pltpu.VMEM((HD, ALLROWS), BF16),
    pltpu.VMEM((ALLROWS, 128), F32),
    pltpu.VMEM((ALLROWS, 128), F32),
    pltpu.VMEM((2, ALLROWS, 2 * BLOCK), BF16),
    pltpu.VMEM((2, ALLROWS, 2 * BLOCK), BF16),
    pltpu.VMEM((2, HD, ALLROWS), F32),
]


NEAR = ((0, 1), (1, 0), (3, 0), (1, 1), (3, 1), (2, 0), (2, 1))


def whole_kernel(
    q, k, v, o, do, lse, lists,
    gq, gk, gv,
    qg, dog, stg, kvg, dq, far_dq, dka, dva, dkv, land, acc_in, acc_out, final,
    o_buf, do_buf, lse_buf, rows_buf, stat_src, list_src, lsg, bias, diag,
    qs, dos, qt, dot, lseb, delb, pbuf, dsbuf, dqa, in_sem,
    kv_s, kv_r, kv_l, big_s, big_r, big_l, st_s, st_r, st_l, ls_s, ls_r, ls_l,
    ring_s, ring_r, cr_s, cr_r, crst_s, crst_r, crls_s, crls_r,
    dq_s, dq_r, red_s, red_r, out_s, out_r, out_l, kvo_s, kvo_r, kvo_l,
):
    y, x, z, core = coords()
    me = x * 2 + core
    loads = [
        pltpu.make_async_copy(src, dst, in_sem.at[i])
        for i, (src, dst) in enumerate(
            ((lists, rows_buf), (lse, lse_buf), (do, do_buf), (o, o_buf))
        )
    ]
    for c in loads:
        c.start()
    bar = pltpu.get_barrier_semaphore()
    signal_peers(bar, y, x, z, core, me)

    def cols(ref, g, width):
        return ref.at[:, pl.ds(pl.multiple_of(g * width, 128), width)]

    def to(n):
        return ((x + n[0]) % NX) * 2 + (core + n[1]) % 2

    def of(n):
        return ((x + NX - n[0]) % NX) * 2 + (core + n[1]) % 2

    def at(p):
        return device(y, p // 2, z, p % 2)

    def kv_slot(s, piece, zz):
        return kvg.at[zz, piece, s // 2, pl.ds((s % 2) * TOK, TOK), :]

    def kv_copy(p, piece):
        return remote(
            cols((k, v)[piece], p, HD), kv_slot(me, piece, z),
            kv_s.at[piece, p], kv_r.at[piece, me], at(p),
        )

    def kv_recv(s, piece):
        return remote(
            cols((k, v)[piece], s, HD), kv_slot(s, piece, z),
            kv_s.at[piece, s], kv_r.at[piece, s], at(s),
        )

    def big_copy(p, which):
        src, dst = ((q, qg), (do, dog))[which]
        return remote(
            cols(src, p, GW), dst.at[0, me], big_s.at[which, p], big_r.at[which, me], at(p)
        )

    def big_recv(s, which):
        src, dst = ((q, qg), (do, dog))[which]
        return remote(
            cols(src, s, GW), dst.at[0, s], big_s.at[which, s], big_r.at[which, s], at(s)
        )

    def st_copy(p):
        return remote(stat_src.at[p], stg.at[0, me], st_s.at[p], st_r.at[me], at(p))

    def st_recv(s):
        return remote(stat_src.at[s], stg.at[0, s], st_s.at[s], st_r.at[s], at(s))

    def ls_copy(d):
        xx = (x + d) % NX
        return remote(list_src, lsg.at[0, x], ls_s.at[xx], ls_r.at[x], device(y, xx, z, core))

    def ls_recv(d):
        xx = (x + NX - d) % NX
        return remote(list_src, lsg.at[0, xx], ls_s.at[xx], ls_r.at[xx], device(y, xx, z, core))

    def cross_copy(s, which):
        ref = (qg, dog)[which]
        return remote(
            ref.at[0, s], ref.at[1, s], cr_s.at[which, s], cr_r.at[which, s],
            device(3 - y, x, z, core),
        )

    kv_local = [
        pltpu.make_async_copy(cols((k, v)[piece], me, HD), kv_slot(me, piece, z), kv_l.at[piece])
        for piece in (0, 1)
    ]
    big_local = [
        pltpu.make_async_copy(cols(q, me, GW), qg.at[0, me], big_l.at[0]),
        pltpu.make_async_copy(cols(do, me, GW), dog.at[0, me], big_l.at[1]),
    ]
    for c in kv_local + big_local:
        c.start()

    wait_peers(bar, y)
    for piece in (0, 1):
        for n in NEAR[1:] + NEAR[:1]:
            kv_copy(to(n), piece).start()
    for n in NEAR[:5]:
        for which in (0, 1):
            big_copy(to(n), which).start()
    for c in big_local:
        c.wait()

    @pl.when(y == 2)
    def _():
        for which in (0, 1):
            cross_copy(me, which).start()

    loads[0].wait()
    list_src[...] = jnp.full((8, 128), -1, jnp.int32)
    list_src[0:2, 0:LISTW] = rows_buf[...]

    for d in range(1, NX):
        ls_copy(d).start()
    ls_local = pltpu.make_async_copy(list_src, lsg.at[0, x], ls_l)
    ls_local.start()

    for c in loads[1:]:
        c.wait()
    lane = lax.broadcasted_iota(jnp.int32, (TOK, 128), 1)
    for g in range(KVH):
        block = jnp.zeros((TOK, 128), F32)
        for r in range(GS):
            h = g * GS + r
            own = slice(h * HD, (h + 1) * HD)
            delta = jnp.sum(
                do_buf[:, own].astype(F32) * o_buf[:, own].astype(F32), axis=1, keepdims=True
            )
            block = jnp.where(lane == r, lse_buf[:, h : h + 1] * LOG2E, block)
            block = jnp.where(lane == 8 + r, delta, block)
        stat_src[g] = block

    for n in NEAR:
        st_copy(to(n)).start()
    st_local = pltpu.make_async_copy(stat_src.at[me], stg.at[0, me], st_l)
    st_local.start()
    for n in NEAR[5:]:
        for which in (0, 1):
            big_copy(to(n), which).start()

    def ring_copy(direction, piece, step):
        sign = (1, NZ - 1)[direction]
        back = (NZ - 1, 1)[direction]
        chunk = (z + back * step) % NZ
        part = kvg.at[chunk, piece]
        return remote(
            part, part, ring_s.at[direction, piece, step], ring_r.at[direction, piece, step],
            device(y, x, (z + sign) % NZ, core),
        )

    def ring_recv(direction, piece, step):
        back = (NZ - 1, 1)[direction]
        chunk = (z + back * (step + 1)) % NZ
        part = kvg.at[chunk, piece]
        return remote(
            part, part, ring_s.at[direction, piece, step], ring_r.at[direction, piece, step],
            device(y, x, (z + back) % NZ, core),
        )

    def forward(some):
        for n in some:
            s = of(n)
            for which in (0, 1):
                big_recv(s, which).wait_recv()

            @pl.when(y == 2)
            def _():
                for which in (0, 1):
                    cross_copy(s, which).start()

    def ring_start(piece):
        for n in NEAR:
            kv_recv(of(n), piece).wait_recv()
        kv_local[piece].wait()
        for direction in (0, 1):
            ring_copy(direction, piece, 0).start()

    def ring_step(step, piece):
        for direction, pc, steps in CHAINS:
            if pc == piece and step < steps:
                ring_recv(direction, piece, step).wait_recv()
                if step + 1 < steps:
                    ring_copy(direction, piece, step + 1).start()

    ring_start(0)
    ring_start(1)
    for ref in (dka, dva, dqa):
        ref[...] = jnp.zeros_like(ref)
    eye = identity()
    half = (z % 4) // 2
    base = y * 16
    row_tok = (z % 2) * PIECE + lax.broadcasted_iota(jnp.int32, (ROWS, 128), 0) % PIECE
    key_tok = lax.broadcasted_iota(jnp.int32, (ROWS, 128), 1)
    diag[...] = jnp.where(key_tok <= row_tok, 0.0, BIG)

    forward(NEAR[:3])
    ring_step(0, 0)
    forward(NEAR[3:4])
    ring_step(0, 1)
    forward(NEAR[4:5])
    ring_step(1, 0)
    forward(NEAR[5:6])
    ring_step(1, 1)
    forward(NEAR[6:])

    for n in NEAR:
        st_recv(of(n)).wait_recv()
    for d in range(1, NX):
        ls_recv(d).wait_recv()
    st_local.wait()
    ls_local.wait()

    crst = remote(stg.at[0], stg.at[1], crst_s, crst_r, device(3 - y, x, z, core))
    crls = remote(lsg.at[0], lsg.at[1], crls_s, crls_r, device(3 - y, x, z, core))

    @pl.when(y == 2)
    def _():
        crst.start()
        crls.start()

    state = (qs, dos, qt, dot, lseb, delb)
    for piece in (0, 1):
        for i in (0, 1):
            load_rows(piece * 2 + i, 0, qg, dog, stg, eye, *state)
        turn_rows(piece * 2, piece * 2 + 2, eye, *state[:4])
    for xx in range(NX):
        bias[xx] = jnp.where(seen_bias(lsg, 0, xx, half, base) > 0.0, 0.0, BIG)

    own = z // 2
    side = (z % 2) * 2 - 1

    def own_tiles(zz, cut, between):
        rest = [(pbuf.at[n], dsbuf.at[n], dqa.at[0], dka, dva) for n in (0, 1)]
        tile((0, 1, 2, 3), zz, zz + 4, kvg, bias, cut, eye, *state, *rest[0])
        between()
        tile((2, 3), zz + 8, zz + 12, kvg, bias, cut, eye, *state, *rest[1])

    def third_hop():
        ring_step(2, 0)
        ring_step(2, 1)

    own_tiles(own, diag, third_hop)

    def column(i, carry):
        @pl.when(i == 3)
        def _():
            ring_step(3, 0)
            ring_step(3, 1)

        move = jnp.where(i == 1, side, jnp.where(i == 2, -side, 2))
        own_tiles((own + move + 4) % 4, None, lambda: None)
        return carry

    lax.fori_loop(1, 4, column, 0)

    def cross_dq(s):
        return remote(far_dq.at[s], land.at[me], dq_s.at[s], dq_r.at[me], device(3 - y, s // 2, z, s % 2))

    def cross_dq_recv(s):
        return remote(far_dq.at[s], land.at[s], dq_s.at[s], dq_r.at[s], device(3 - y, s // 2, z, s % 2))

    def dq_copy(p):
        return remote(dq.at[p], cols(gq, me, GW), out_s.at[p], out_r.at[me], at(p))

    def dq_recv(s):
        return remote(dq.at[s], cols(gq, s, GW), out_s.at[s], out_r.at[s], at(s))

    dq_local = pltpu.make_async_copy(dq.at[me], cols(gq, me, GW), out_l)

    def send_dq():
        put_dq(dq, dqa.at[0], eye)
        for n in NEAR:
            dq_copy(to(n)).start()
        dq_local.start()

    send_dq()

    @pl.when(y == 1)
    def _():
        for s in range(PEERS):
            for which in (0, 1):
                cross_copy(s, which).wait_recv()
        crst.wait_recv()
        crls.wait_recv()
        for xx in range(NX):
            load_rows(xx, 1, qg, dog, stg, eye, *state)
            bias[xx] = jnp.where(seen_bias(lsg, 1, xx, half, base) > 0.0, 0.0, BIG)
        turn_rows(0, NX, eye, *state[:4])

    def red_copy(direction, piece, steps, step):
        sign = (1, NZ - 1)[direction]
        owner = (z + sign * (steps - step)) % NZ
        if step == 0:
            src = dkv.at[owner, piece]
        else:
            src = acc_out.at[direction, piece, step]
        return remote(
            src, acc_in.at[direction, piece, step],
            red_s.at[direction, piece, step], red_r.at[direction, piece, step],
            device(y, x, (z + sign) % NZ, core),
        )

    def red_step(direction, piece, steps, step):
        sign = (1, NZ - 1)[direction]
        owner = (z + sign * (steps - step)) % NZ
        red_copy(direction, piece, steps, step - 1).wait_recv()
        acc_out[direction, piece, step] = (
            acc_in[direction, piece, step - 1].astype(F32) + dkv[owner, piece].astype(F32)
        ).astype(BF16)
        red_copy(direction, piece, steps, step).start()

    def turn_column(zz):
        for xx in range(NX):
            for piece, ref, scale in ((0, dka, SCALE), (1, dva, 1.0)):
                low = (ref[zz + 4 * xx] * scale).astype(BF16)
                turned = lax.dot_general(eye, low, NT, preferred_element_type=F32).astype(BF16)
                dkv[2 * zz, piece, xx] = turned[:PIECE]
                dkv[2 * zz + 1, piece, xx] = turned[PIECE:]

    def finish(zz):
        @pl.when(y == 1)
        def _():
            rest = [(pbuf.at[n], dsbuf.at[n], dqa.at[1], dka, dva) for n in (0, 1)]
            tile((0, 1, 2, 3), zz, zz + 4, kvg, bias, None, eye, *state, *rest[0])
            tile((0, 1, 2, 3), zz + 8, zz + 12, kvg, bias, None, eye, *state, *rest[1])
            turn_column(zz)

        @pl.when(y != 1)
        def _():
            turn_column(zz)

    long = ((0, 0, 4), (1, 1, 4))
    short = ((0, 1, 3), (1, 0, 3))

    def reduce_column(i, carry):
        move = jnp.where(i == 0, 2, jnp.where(i == 1, -side, jnp.where(i == 2, side, 0)))
        finish((own + move + 4) % 4)

        @pl.when(i == 0)
        def _():
            for c in long:
                red_copy(*c, 0).start()

        @pl.when(i == 1)
        def _():
            for c in short:
                red_copy(*c, 0).start()
            for c in long:
                red_step(*c, 1)

        @pl.when(i == 2)
        def _():
            for c in short:
                red_step(*c, 1)
            for c in long:
                red_step(*c, 2)

        return carry

    lax.fori_loop(0, 4, reduce_column, 0)

    for c in short:
        red_step(*c, 2)
    for c in long:
        red_step(*c, 3)

    @pl.when(y == 1)
    def _():
        put_dq(far_dq, dqa.at[1], eye)
        for s in range(PEERS):
            cross_dq(s).start()

    def grad_copy(piece, p):
        return remote(
            final.at[piece, p // 2, pl.ds((p % 2) * TOK, TOK), :],
            cols((gk, gv)[piece], me, HD),
            kvo_s.at[piece, p], kvo_r.at[piece, me], at(p),
        )

    def grad_recv(piece, s):
        return remote(
            final.at[piece, s // 2, pl.ds((s % 2) * TOK, TOK), :],
            cols((gk, gv)[piece], s, HD),
            kvo_s.at[piece, s], kvo_r.at[piece, s], at(s),
        )

    grad_local = []
    for piece in (0, 1):
        (d0, s0), (d1, s1) = [(d, steps) for d, pc, steps in CHAINS if pc == piece]
        red_copy(d0, piece, s0, s0 - 1).wait_recv()
        red_copy(d1, piece, s1, s1 - 1).wait_recv()
        final[piece] = (
            acc_in[d0, piece, s0 - 1].astype(F32)
            + acc_in[d1, piece, s1 - 1].astype(F32)
            + dkv[z, piece].astype(F32)
        ).astype(BF16)
        for n in NEAR:
            grad_copy(piece, to(n)).start()
        grad_local.append(
            pltpu.make_async_copy(
                final.at[piece, x, pl.ds(core * TOK, TOK), :],
                cols((gk, gv)[piece], me, HD), kvo_l.at[piece],
            )
        )
        grad_local[piece].start()

    for n in NEAR:
        for i in (0, 1):
            kv_copy(to(n), i).wait_send()
            big_copy(to(n), i).wait_send()
        st_copy(to(n)).wait_send()
    for d in range(1, NX):
        ls_copy(d).wait_send()
    for direction, piece, steps in CHAINS:
        for step in range(steps):
            ring_copy(direction, piece, step).wait_send()

    @pl.when(y == 2)
    def _():
        for s in range(PEERS):
            for which in (0, 1):
                cross_copy(s, which).wait_send()
        crst.wait_send()
        crls.wait_send()


    @pl.when(y == 1)
    def _():
        for s in range(PEERS):
            cross_dq(s).wait_send()

    for direction, piece, steps in CHAINS:
        for step in range(steps):
            red_copy(direction, piece, steps, step).wait_send()
    for n in NEAR:
        for piece in (0, 1):
            grad_copy(piece, to(n)).wait_send()
            grad_recv(piece, of(n)).wait_recv()
        dq_copy(to(n)).wait_send()
        dq_recv(of(n)).wait_recv()
    for c in grad_local:
        c.wait()
    dq_local.wait()

    @pl.when(y == 2)
    def _():
        for g in range(PEERS):
            cross_dq_recv(g).wait_recv()
            own_cols = slice(g * GW, (g + 1) * GW)
            gq[:, own_cols] = (gq[:, own_cols].astype(F32) + land[g].astype(F32)).astype(BF16)


def whole(*args):
    vmem = pl.BlockSpec(memory_space=pltpu.VMEM)
    hbm = pl.BlockSpec(memory_space=pltpu.HBM)
    dma = pltpu.SemaphoreType.DMA
    return pl.pallas_call(
        whole_kernel,
        out_shape=(
            jax.ShapeDtypeStruct((TOK, QH * HD), BF16),
            jax.ShapeDtypeStruct((TOK, KVH * HD), BF16),
            jax.ShapeDtypeStruct((TOK, KVH * HD), BF16),
        ),
        in_specs=[hbm] * 7,
        out_specs=(vmem,) * 3,
        scratch_shapes=[
            pltpu.VMEM((2, PEERS, TOK, GW), BF16),
            pltpu.VMEM((2, PEERS, TOK, GW), BF16),
            pltpu.VMEM((2, PEERS, TOK, 128), F32),
            pltpu.VMEM((NZ, 2, NX, PIECE, HD), BF16),
            pltpu.VMEM((PEERS, TOK, GW), BF16),
            pltpu.VMEM((PEERS, TOK, GW), BF16),
            pltpu.VMEM((16, HD, BLOCK), F32),
            pltpu.VMEM((16, HD, BLOCK), F32),
            pltpu.VMEM((NZ, 2, NX, PIECE, HD), BF16),
            pltpu.VMEM((PEERS, TOK, GW), BF16),
            pltpu.VMEM((2, 2, 4, NX, PIECE, HD), BF16),
            pltpu.VMEM((2, 2, 4, NX, PIECE, HD), BF16),
            pltpu.VMEM((2, NX, PIECE, HD), BF16),
            pltpu.VMEM((TOK, QH * HD), BF16),
            pltpu.VMEM((TOK, QH * HD), BF16),
            pltpu.VMEM((TOK, QH), F32),
            pltpu.VMEM((2, LISTW), jnp.int32),
            pltpu.VMEM((KVH, TOK, 128), F32),
            pltpu.VMEM((8, 128), jnp.int32),
            pltpu.VMEM((2, NX, 8, 128), jnp.int32),
            pltpu.VMEM((NX, 16, 128), F32),
            pltpu.VMEM((ROWS, 128), F32),
            *TILE_SCRATCH,
            dma((4,)),
            dma((2, PEERS)), dma((2, PEERS)), dma((2,)),
            dma((2, PEERS)), dma((2, PEERS)), dma((2,)),
            dma((PEERS,)), dma((PEERS,)), dma,
            dma((NX,)), dma((NX,)), dma,
            dma((2, 2, 4)), dma((2, 2, 4)),
            dma((2, PEERS)), dma((2, PEERS)),
            dma, dma, dma, dma,
            dma((PEERS,)), dma((PEERS,)),
            dma((2, 2, 4)), dma((2, 2, 4)),
            dma((PEERS,)), dma((PEERS,)), dma,
            dma((2, PEERS)), dma((2, PEERS)), dma((2,)),
        ],
        compiler_params=pltpu.CompilerParams(
            collective_id=0, has_side_effects=True, vmem_limit_bytes=40 << 20
        ),
        name="whole",
    )(*args)


def emit_kernel(a, b, c, x, y, z, sem):
    copies = [
        pltpu.make_async_copy(src, dst, sem.at[i]) for i, (src, dst) in enumerate(((a, x), (b, y), (c, z)))
    ]
    for one in copies:
        one.start()
    for one in copies:
        one.wait()


def emit(*arrays):
    return pl.pallas_call(
        emit_kernel,
        out_shape=tuple(jax.ShapeDtypeStruct(a.shape, a.dtype) for a in arrays),
        in_specs=[pl.BlockSpec(memory_space=pltpu.VMEM)] * 3,
        out_specs=(pl.BlockSpec(memory_space=pltpu.HBM),) * 3,
        scratch_shapes=[pltpu.SemaphoreType.DMA((3,))],
        compiler_params=pltpu.CompilerParams(vmem_limit_bytes=1 << 20),
        name="emit",
    )(*arrays)


def local(query_act, key_act, value_act, attn_out, grad_out, log_sum, kv_lists):
    args = (query_act, key_act, value_act, attn_out, grad_out, log_sum, kv_lists)
    return emit(*whole(*(pltpu.with_memory_space_constraint(a, pltpu.HBM) for a in args)))


def solution(mesh):
    row = P(("blk", "head"), None)
    return jax.shard_map(
        local,
        mesh=mesh,
        in_specs=(row,) * 6 + (P("blk", None),),
        out_specs=(row,) * 3,
        check_vma=False,
    )
```

```python
import jax
import jax.numpy as jnp
from jax import lax
from jax.experimental import pallas as pl
from jax.experimental.pallas import tpu as pltpu
from jax.sharding import PartitionSpec as P

QH = 40
KVH = 8
HD = 128
BLOCK = 128
GS = QH // KVH
TOK = 32
GW = GS * HD
PIECE = 64
ROWS = GS * PIECE
NX = 4
NZ = 8
PEERS = 8
LISTW = 32
SCALE = HD ** -0.5
LOG2E = 1.4426950408889634
MESH = pl.DeviceIdType.MESH
F32 = jnp.float32
BF16 = jnp.bfloat16
NT = (((1,), (1,)), ((), ()))
NN = (((1,), (0,)), ((), ()))


def coords():
    blk = lax.axis_index("blk")
    head = lax.axis_index("head")
    y = blk // 8
    x = (blk // 2) % 4
    z = (blk % 2) * 4 + head // 2
    return y, x, z, head % 2


def device(y, x, z, core):
    return {"blk": (y * 4 + x) * 2 + z // 4, "head": (z % 4) * 2 + core}


def remote(src, dst, send_sem, recv_sem, device_id):
    return pltpu.make_async_remote_copy(
        src_ref=src,
        dst_ref=dst,
        send_sem=send_sem,
        recv_sem=recv_sem,
        device_id=device_id,
        device_id_type=MESH,
    )


def signal_peers(bar, y, x, z, core, me):
    for d in range(1, PEERS):
        p = (me + d) % PEERS
        pl.semaphore_signal(bar, inc=1, device_id=device(y, p // 2, z, p % 2), device_id_type=MESH)
    for step in (1, NZ - 1):
        pl.semaphore_signal(
            bar, inc=1, device_id=device(y, x, (z + step) % NZ, core), device_id_type=MESH
        )

    @pl.when((y == 1) | (y == 2))
    def _():
        for p in range(PEERS):
            pl.semaphore_signal(
                bar, inc=1, device_id=device(3 - y, p // 2, z, p % 2), device_id_type=MESH
            )


def wait_peers(bar, y):
    pl.semaphore_wait(bar, PEERS - 1 + 2 + PEERS * ((y == 1) | (y == 2)).astype(jnp.int32))


CHAINS = ((0, 0, 4), (0, 1, 3), (1, 1, 4), (1, 0, 3))


BIG = 1e30
ALLROWS = NX * ROWS


def rows_of(x):
    return slice(x * ROWS, (x + 1) * ROWS)


def seen_bias(lists, part, x, half, base):
    entries = lists[part, x, pl.ds(half, 1), :]
    block = base + lax.broadcasted_iota(jnp.int32, (16, 128), 0)
    hit = jnp.max(jnp.where(entries == block, 1.0, 0.0), axis=1, keepdims=True)
    return jnp.broadcast_to(hit, (16, 128))


def load_rows(x, part, qg, dog, stg, eye, qs, dos, qt, dot, lseb, delb):
    for c in range(2):
        st = stg[part, x * 2 + c]
        for r in range(GS):
            start = x * ROWS + r * PIECE + c * TOK
            at = slice(start, start + TOK)
            col = slice(r * HD, (r + 1) * HD)
            qs[at, :] = qg[part, x * 2 + c, :, col]
            dos[at, :] = dog[part, x * 2 + c, :, col]
            lseb[at, :] = jnp.broadcast_to(st[:, r : r + 1], (TOK, 128))
            delb[at, :] = jnp.broadcast_to(st[:, 8 + r : 9 + r], (TOK, 128))


def turn_rows(lo, hi, eye, qs, dos, qt, dot):
    at = slice(lo * ROWS, hi * ROWS)
    qt[:, at] = lax.dot_general(eye, qs[at, :], NT, preferred_element_type=F32).astype(BF16)
    dot[:, at] = lax.dot_general(eye, dos[at, :], NT, preferred_element_type=F32).astype(BF16)


def identity():
    r_id = lax.broadcasted_iota(jnp.int32, (128, 128), 0)
    c_id = lax.broadcasted_iota(jnp.int32, (128, 128), 1)
    return jnp.where(r_id == c_id, 1.0, 0.0).astype(BF16)


def key_block(kvg, piece, b):
    zz = (b % 4) * 2
    return jnp.concatenate([kvg[zz, piece, b // 4], kvg[zz + 1, piece, b // 4]], axis=0)


def tile(xs, a, b, kvg, bias, diag, eye, qs, dos, qt, dot, lseb, delb, pbuf, dsbuf, dqa, dka, dva):
    keys = jnp.concatenate([key_block(kvg, 0, a), key_block(kvg, 0, b)], axis=0)
    values = jnp.concatenate([key_block(kvg, 1, a), key_block(kvg, 1, b)], axis=0)
    turned = lax.dot_general(eye, keys, NT, preferred_element_type=F32).astype(BF16)
    for x in xs:
        at = rows_of(x)
        s = lax.dot_general(qs[at, :], keys, NT, preferred_element_type=F32)
        dp = lax.dot_general(dos[at, :], values, NT, preferred_element_type=F32)
        lse_a = lseb[at, :] + bias[x, pl.ds(a, 1), :]
        lse_b = lseb[at, :] + bias[x, pl.ds(b, 1), :]
        if diag is not None:
            if x % 2 == 0 and x == xs[0]:
                lse_a = lse_a + diag[...]
            if x % 2 == 1 and x == xs[0] + 1:
                lse_b = lse_b + diag[...]
        p = jnp.exp2(s * (SCALE * LOG2E) - jnp.concatenate([lse_a, lse_b], axis=1))
        delta = delb[at, :]
        ds = (p * (dp - jnp.concatenate([delta, delta], axis=1))).astype(BF16)
        pbuf[at, :] = p.astype(BF16)
        dsbuf[at, :] = ds
    at = slice(xs[0] * ROWS, (xs[-1] + 1) * ROWS)
    dvt = lax.dot_general(dot[:, at], pbuf[at, :], NN, preferred_element_type=F32)
    dkt = lax.dot_general(qt[:, at], dsbuf[at, :], NN, preferred_element_type=F32)
    dqa[:, at] += lax.dot_general(turned, dsbuf[at, :], NT, preferred_element_type=F32)
    dva[a] += dvt[:, :BLOCK]
    dka[a] += dkt[:, :BLOCK]
    dva[b] += dvt[:, BLOCK:]
    dka[b] += dkt[:, BLOCK:]


def put_dq(dq, dqa, eye):
    for j in range(ALLROWS // 128):
        low = (dqa[:, j * 128 : (j + 1) * 128] * SCALE).astype(BF16)
        rows = lax.dot_general(eye, low, NT, preferred_element_type=F32).astype(BF16)
        for i in range(128 // TOK):
            x, rest = divmod(j * 4 + i, 2 * GS)
            r, c = divmod(rest, 2)
            dq[x * 2 + c, :, r * HD : (r + 1) * HD] = rows[i * TOK : (i + 1) * TOK]


TILE_SCRATCH = [
    pltpu.VMEM((ALLROWS, HD), BF16),
    pltpu.VMEM((ALLROWS, HD), BF16),
    pltpu.VMEM((HD, ALLROWS), BF16),
    pltpu.VMEM((HD, ALLROWS), BF16),
    pltpu.VMEM((ALLROWS, 128), F32),
    pltpu.VMEM((ALLROWS, 128), F32),
    pltpu.VMEM((2, ALLROWS, 2 * BLOCK), BF16),
    pltpu.VMEM((2, ALLROWS, 2 * BLOCK), BF16),
    pltpu.VMEM((2, HD, ALLROWS), F32),
]


NEAR = ((0, 1), (1, 0), (3, 0), (1, 1), (3, 1), (2, 0), (2, 1))


def whole_kernel(
    q, k, v, o, do, lse, lists,
    gq, gk, gv,
    qg, dog, stg, kvg, dq, far_dq, dka, dva, dkv, land, acc_in, acc_out, final,
    o_buf, do_buf, lse_buf, rows_buf, stat_src, list_src, lsg, bias, diag,
    qs, dos, qt, dot, lseb, delb, pbuf, dsbuf, dqa, in_sem,
    kv_s, kv_r, kv_l, big_s, big_r, big_l, st_s, st_r, st_l, ls_s, ls_r, ls_l,
    ring_s, ring_r, cr_s, cr_r, crst_s, crst_r, crls_s, crls_r,
    dq_s, dq_r, red_s, red_r, out_s, out_r, out_l, kvo_s, kvo_r, kvo_l,
):
    y, x, z, core = coords()
    me = x * 2 + core
    loads = [
        pltpu.make_async_copy(src, dst, in_sem.at[i])
        for i, (src, dst) in enumerate(
            ((lists, rows_buf), (lse, lse_buf), (do, do_buf), (o, o_buf))
        )
    ]
    for c in loads:
        c.start()
    bar = pltpu.get_barrier_semaphore()
    signal_peers(bar, y, x, z, core, me)

    def cols(ref, g, width):
        return ref.at[:, pl.ds(pl.multiple_of(g * width, 128), width)]

    def to(n):
        return ((x + n[0]) % NX) * 2 + (core + n[1]) % 2

    def of(n):
        return ((x + NX - n[0]) % NX) * 2 + (core + n[1]) % 2

    def at(p):
        return device(y, p // 2, z, p % 2)

    def kv_slot(s, piece, zz):
        return kvg.at[zz, piece, s // 2, pl.ds((s % 2) * TOK, TOK), :]

    def kv_copy(p, piece):
        return remote(
            cols((k, v)[piece], p, HD), kv_slot(me, piece, z),
            kv_s.at[piece, p], kv_r.at[piece, me], at(p),
        )

    def kv_recv(s, piece):
        return remote(
            cols((k, v)[piece], s, HD), kv_slot(s, piece, z),
            kv_s.at[piece, s], kv_r.at[piece, s], at(s),
        )

    def big_copy(p, which):
        src, dst = ((q, qg), (do, dog))[which]
        return remote(
            cols(src, p, GW), dst.at[0, me], big_s.at[which, p], big_r.at[which, me], at(p)
        )

    def big_recv(s, which):
        src, dst = ((q, qg), (do, dog))[which]
        return remote(
            cols(src, s, GW), dst.at[0, s], big_s.at[which, s], big_r.at[which, s], at(s)
        )

    def st_copy(p):
        return remote(stat_src.at[p], stg.at[0, me], st_s.at[p], st_r.at[me], at(p))

    def st_recv(s):
        return remote(stat_src.at[s], stg.at[0, s], st_s.at[s], st_r.at[s], at(s))

    def ls_copy(d):
        xx = (x + d) % NX
        return remote(list_src, lsg.at[0, x], ls_s.at[xx], ls_r.at[x], device(y, xx, z, core))

    def ls_recv(d):
        xx = (x + NX - d) % NX
        return remote(list_src, lsg.at[0, xx], ls_s.at[xx], ls_r.at[xx], device(y, xx, z, core))

    def cross_copy(s, which):
        ref = (qg, dog)[which]
        return remote(
            ref.at[0, s], ref.at[1, s], cr_s.at[which, s], cr_r.at[which, s],
            device(3 - y, x, z, core),
        )

    kv_local = [
        pltpu.make_async_copy(cols((k, v)[piece], me, HD), kv_slot(me, piece, z), kv_l.at[piece])
        for piece in (0, 1)
    ]
    big_local = [
        pltpu.make_async_copy(cols(q, me, GW), qg.at[0, me], big_l.at[0]),
        pltpu.make_async_copy(cols(do, me, GW), dog.at[0, me], big_l.at[1]),
    ]
    for c in kv_local + big_local:
        c.start()

    wait_peers(bar, y)
    for piece in (0, 1):
        for n in NEAR[1:] + NEAR[:1]:
            kv_copy(to(n), piece).start()
    for n in NEAR[:5]:
        for which in (0, 1):
            big_copy(to(n), which).start()
    for c in big_local:
        c.wait()

    @pl.when(y == 2)
    def _():
        for which in (0, 1):
            cross_copy(me, which).start()

    loads[0].wait()
    list_src[...] = jnp.full((8, 128), -1, jnp.int32)
    list_src[0:2, 0:LISTW] = rows_buf[...]

    for d in range(1, NX):
        ls_copy(d).start()
    ls_local = pltpu.make_async_copy(list_src, lsg.at[0, x], ls_l)
    ls_local.start()

    for c in loads[1:]:
        c.wait()
    lane = lax.broadcasted_iota(jnp.int32, (TOK, 128), 1)
    for g in range(KVH):
        block = jnp.zeros((TOK, 128), F32)
        for r in range(GS):
            h = g * GS + r
            own = slice(h * HD, (h + 1) * HD)
            delta = jnp.sum(
                do_buf[:, own].astype(F32) * o_buf[:, own].astype(F32), axis=1, keepdims=True
            )
            block = jnp.where(lane == r, lse_buf[:, h : h + 1] * LOG2E, block)
            block = jnp.where(lane == 8 + r, delta, block)
        stat_src[g] = block

    for n in NEAR:
        st_copy(to(n)).start()
    st_local = pltpu.make_async_copy(stat_src.at[me], stg.at[0, me], st_l)
    st_local.start()
    for n in NEAR[5:]:
        for which in (0, 1):
            big_copy(to(n), which).start()

    def ring_copy(direction, piece, step):
        sign = (1, NZ - 1)[direction]
        back = (NZ - 1, 1)[direction]
        chunk = (z + back * step) % NZ
        part = kvg.at[chunk, piece]
        return remote(
            part, part, ring_s.at[direction, piece, step], ring_r.at[direction, piece, step],
            device(y, x, (z + sign) % NZ, core),
        )

    def ring_recv(direction, piece, step):
        back = (NZ - 1, 1)[direction]
        chunk = (z + back * (step + 1)) % NZ
        part = kvg.at[chunk, piece]
        return remote(
            part, part, ring_s.at[direction, piece, step], ring_r.at[direction, piece, step],
            device(y, x, (z + back) % NZ, core),
        )

    def forward(some):
        for n in some:
            s = of(n)
            for which in (0, 1):
                big_recv(s, which).wait_recv()

            @pl.when(y == 2)
            def _():
                for which in (0, 1):
                    cross_copy(s, which).start()

    def ring_start(piece):
        for n in NEAR:
            kv_recv(of(n), piece).wait_recv()
        kv_local[piece].wait()
        for direction in (0, 1):
            ring_copy(direction, piece, 0).start()

    def ring_step(step, piece):
        for direction, pc, steps in CHAINS:
            if pc == piece and step < steps:
                ring_recv(direction, piece, step).wait_recv()
                if step + 1 < steps:
                    ring_copy(direction, piece, step + 1).start()

    forward(NEAR[:1])
    ring_start(0)
    ring_start(1)
    forward(NEAR[1:3])
    for ref in (dka, dva, dqa):
        ref[...] = jnp.zeros_like(ref)
    eye = identity()
    half = (z % 4) // 2
    base = y * 16
    row_tok = (z % 2) * PIECE + lax.broadcasted_iota(jnp.int32, (ROWS, 128), 0) % PIECE
    key_tok = lax.broadcasted_iota(jnp.int32, (ROWS, 128), 1)
    diag[...] = jnp.where(key_tok <= row_tok, 0.0, BIG)

    ring_step(0, 0)
    forward(NEAR[3:4])
    ring_step(0, 1)
    forward(NEAR[4:5])
    ring_step(1, 0)
    forward(NEAR[5:6])
    ring_step(1, 1)
    forward(NEAR[6:])

    for n in NEAR:
        st_recv(of(n)).wait_recv()
    for d in range(1, NX):
        ls_recv(d).wait_recv()
    st_local.wait()
    ls_local.wait()

    crst = remote(stg.at[0], stg.at[1], crst_s, crst_r, device(3 - y, x, z, core))
    crls = remote(lsg.at[0], lsg.at[1], crls_s, crls_r, device(3 - y, x, z, core))

    @pl.when(y == 2)
    def _():
        crst.start()
        crls.start()

    state = (qs, dos, qt, dot, lseb, delb)
    for piece in (0, 1):
        for i in (0, 1):
            load_rows(piece * 2 + i, 0, qg, dog, stg, eye, *state)
        turn_rows(piece * 2, piece * 2 + 2, eye, *state[:4])
    for xx in range(NX):
        bias[xx] = jnp.where(seen_bias(lsg, 0, xx, half, base) > 0.0, 0.0, BIG)

    own = z // 2
    side = (z % 2) * 2 - 1

    def own_tiles(zz, cut, between):
        rest = [(pbuf.at[n], dsbuf.at[n], dqa.at[0], dka, dva) for n in (0, 1)]
        tile((0, 1, 2, 3), zz, zz + 4, kvg, bias, cut, eye, *state, *rest[0])
        between()
        tile((2, 3), zz + 8, zz + 12, kvg, bias, cut, eye, *state, *rest[1])

    def third_hop():
        ring_step(2, 0)
        ring_step(2, 1)

    own_tiles(own, diag, third_hop)

    def column(i, carry):
        @pl.when(i == 3)
        def _():
            ring_step(3, 0)
            ring_step(3, 1)

        move = jnp.where(i == 1, side, jnp.where(i == 2, -side, 2))
        own_tiles((own + move + 4) % 4, None, lambda: None)
        return carry

    lax.fori_loop(1, 4, column, 0)

    def cross_dq(s):
        return remote(far_dq.at[s], land.at[me], dq_s.at[s], dq_r.at[me], device(3 - y, s // 2, z, s % 2))

    def cross_dq_recv(s):
        return remote(far_dq.at[s], land.at[s], dq_s.at[s], dq_r.at[s], device(3 - y, s // 2, z, s % 2))

    def dq_copy(p):
        return remote(dq.at[p], cols(gq, me, GW), out_s.at[p], out_r.at[me], at(p))

    def dq_recv(s):
        return remote(dq.at[s], cols(gq, s, GW), out_s.at[s], out_r.at[s], at(s))

    dq_local = pltpu.make_async_copy(dq.at[me], cols(gq, me, GW), out_l)

    def send_dq():
        put_dq(dq, dqa.at[0], eye)
        for n in NEAR:
            dq_copy(to(n)).start()
        dq_local.start()

    send_dq()

    @pl.when(y == 1)
    def _():
        for s in range(PEERS):
            for which in (0, 1):
                cross_copy(s, which).wait_recv()
        crst.wait_recv()
        crls.wait_recv()
        for xx in range(NX):
            load_rows(xx, 1, qg, dog, stg, eye, *state)
            bias[xx] = jnp.where(seen_bias(lsg, 1, xx, half, base) > 0.0, 0.0, BIG)
        turn_rows(0, NX, eye, *state[:4])

    def red_copy(direction, piece, steps, step):
        sign = (1, NZ - 1)[direction]
        owner = (z + sign * (steps - step)) % NZ
        if step == 0:
            src = dkv.at[owner, piece]
        else:
            src = acc_out.at[direction, piece, step]
        return remote(
            src, acc_in.at[direction, piece, step],
            red_s.at[direction, piece, step], red_r.at[direction, piece, step],
            device(y, x, (z + sign) % NZ, core),
        )

    def red_step(direction, piece, steps, step):
        sign = (1, NZ - 1)[direction]
        owner = (z + sign * (steps - step)) % NZ
        red_copy(direction, piece, steps, step - 1).wait_recv()
        acc_out[direction, piece, step] = (
            acc_in[direction, piece, step - 1].astype(F32) + dkv[owner, piece].astype(F32)
        ).astype(BF16)
        red_copy(direction, piece, steps, step).start()

    def turn_column(zz):
        for xx in range(NX):
            for piece, ref, scale in ((0, dka, SCALE), (1, dva, 1.0)):
                low = (ref[zz + 4 * xx] * scale).astype(BF16)
                turned = lax.dot_general(eye, low, NT, preferred_element_type=F32).astype(BF16)
                dkv[2 * zz, piece, xx] = turned[:PIECE]
                dkv[2 * zz + 1, piece, xx] = turned[PIECE:]

    def finish(zz):
        @pl.when(y == 1)
        def _():
            rest = [(pbuf.at[n], dsbuf.at[n], dqa.at[1], dka, dva) for n in (0, 1)]
            tile((0, 1, 2, 3), zz, zz + 4, kvg, bias, None, eye, *state, *rest[0])
            tile((0, 1, 2, 3), zz + 8, zz + 12, kvg, bias, None, eye, *state, *rest[1])
            turn_column(zz)

        @pl.when(y != 1)
        def _():
            turn_column(zz)

    long = ((0, 0, 4), (1, 1, 4))
    short = ((0, 1, 3), (1, 0, 3))

    def reduce_column(i, carry):
        move = jnp.where(i == 0, 2, jnp.where(i == 1, -side, jnp.where(i == 2, side, 0)))
        finish((own + move + 4) % 4)

        @pl.when(i == 0)
        def _():
            for c in long:
                red_copy(*c, 0).start()

        @pl.when(i == 1)
        def _():
            for c in short:
                red_copy(*c, 0).start()
            for c in long:
                red_step(*c, 1)

        @pl.when(i == 2)
        def _():
            for c in short:
                red_step(*c, 1)
            for c in long:
                red_step(*c, 2)

        return carry

    lax.fori_loop(0, 4, reduce_column, 0)

    for c in short:
        red_step(*c, 2)
    for c in long:
        red_step(*c, 3)

    @pl.when(y == 1)
    def _():
        put_dq(far_dq, dqa.at[1], eye)
        for s in range(PEERS):
            cross_dq(s).start()

    def grad_copy(piece, p):
        return remote(
            final.at[piece, p // 2, pl.ds((p % 2) * TOK, TOK), :],
            cols((gk, gv)[piece], me, HD),
            kvo_s.at[piece, p], kvo_r.at[piece, me], at(p),
        )

    def grad_recv(piece, s):
        return remote(
            final.at[piece, s // 2, pl.ds((s % 2) * TOK, TOK), :],
            cols((gk, gv)[piece], s, HD),
            kvo_s.at[piece, s], kvo_r.at[piece, s], at(s),
        )

    grad_local = []
    for piece in (0, 1):
        (d0, s0), (d1, s1) = [(d, steps) for d, pc, steps in CHAINS if pc == piece]
        red_copy(d0, piece, s0, s0 - 1).wait_recv()
        red_copy(d1, piece, s1, s1 - 1).wait_recv()
        final[piece] = (
            acc_in[d0, piece, s0 - 1].astype(F32)
            + acc_in[d1, piece, s1 - 1].astype(F32)
            + dkv[z, piece].astype(F32)
        ).astype(BF16)
        for n in NEAR:
            grad_copy(piece, to(n)).start()
        grad_local.append(
            pltpu.make_async_copy(
                final.at[piece, x, pl.ds(core * TOK, TOK), :],
                cols((gk, gv)[piece], me, HD), kvo_l.at[piece],
            )
        )
        grad_local[piece].start()

    for n in NEAR:
        for i in (0, 1):
            kv_copy(to(n), i).wait_send()
            big_copy(to(n), i).wait_send()
        st_copy(to(n)).wait_send()
    for d in range(1, NX):
        ls_copy(d).wait_send()
    for direction, piece, steps in CHAINS:
        for step in range(steps):
            ring_copy(direction, piece, step).wait_send()

    @pl.when(y == 2)
    def _():
        for s in range(PEERS):
            for which in (0, 1):
                cross_copy(s, which).wait_send()
        crst.wait_send()
        crls.wait_send()


    @pl.when(y == 1)
    def _():
        for s in range(PEERS):
            cross_dq(s).wait_send()

    for direction, piece, steps in CHAINS:
        for step in range(steps):
            red_copy(direction, piece, steps, step).wait_send()
    for n in NEAR:
        for piece in (0, 1):
            grad_copy(piece, to(n)).wait_send()
            grad_recv(piece, of(n)).wait_recv()
        dq_copy(to(n)).wait_send()
        dq_recv(of(n)).wait_recv()
    for c in grad_local:
        c.wait()
    dq_local.wait()

    @pl.when(y == 2)
    def _():
        for g in range(PEERS):
            cross_dq_recv(g).wait_recv()
            own_cols = slice(g * GW, (g + 1) * GW)
            gq[:, own_cols] = (gq[:, own_cols].astype(F32) + land[g].astype(F32)).astype(BF16)


def whole(*args):
    vmem = pl.BlockSpec(memory_space=pltpu.VMEM)
    hbm = pl.BlockSpec(memory_space=pltpu.HBM)
    dma = pltpu.SemaphoreType.DMA
    return pl.pallas_call(
        whole_kernel,
        out_shape=(
            jax.ShapeDtypeStruct((TOK, QH * HD), BF16),
            jax.ShapeDtypeStruct((TOK, KVH * HD), BF16),
            jax.ShapeDtypeStruct((TOK, KVH * HD), BF16),
        ),
        in_specs=[hbm] * 7,
        out_specs=(vmem,) * 3,
        scratch_shapes=[
            pltpu.VMEM((2, PEERS, TOK, GW), BF16),
            pltpu.VMEM((2, PEERS, TOK, GW), BF16),
            pltpu.VMEM((2, PEERS, TOK, 128), F32),
            pltpu.VMEM((NZ, 2, NX, PIECE, HD), BF16),
            pltpu.VMEM((PEERS, TOK, GW), BF16),
            pltpu.VMEM((PEERS, TOK, GW), BF16),
            pltpu.VMEM((16, HD, BLOCK), F32),
            pltpu.VMEM((16, HD, BLOCK), F32),
            pltpu.VMEM((NZ, 2, NX, PIECE, HD), BF16),
            pltpu.VMEM((PEERS, TOK, GW), BF16),
            pltpu.VMEM((2, 2, 4, NX, PIECE, HD), BF16),
            pltpu.VMEM((2, 2, 4, NX, PIECE, HD), BF16),
            pltpu.VMEM((2, NX, PIECE, HD), BF16),
            pltpu.VMEM((TOK, QH * HD), BF16),
            pltpu.VMEM((TOK, QH * HD), BF16),
            pltpu.VMEM((TOK, QH), F32),
            pltpu.VMEM((2, LISTW), jnp.int32),
            pltpu.VMEM((KVH, TOK, 128), F32),
            pltpu.VMEM((8, 128), jnp.int32),
            pltpu.VMEM((2, NX, 8, 128), jnp.int32),
            pltpu.VMEM((NX, 16, 128), F32),
            pltpu.VMEM((ROWS, 128), F32),
            *TILE_SCRATCH,
            dma((4,)),
            dma((2, PEERS)), dma((2, PEERS)), dma((2,)),
            dma((2, PEERS)), dma((2, PEERS)), dma((2,)),
            dma((PEERS,)), dma((PEERS,)), dma,
            dma((NX,)), dma((NX,)), dma,
            dma((2, 2, 4)), dma((2, 2, 4)),
            dma((2, PEERS)), dma((2, PEERS)),
            dma, dma, dma, dma,
            dma((PEERS,)), dma((PEERS,)),
            dma((2, 2, 4)), dma((2, 2, 4)),
            dma((PEERS,)), dma((PEERS,)), dma,
            dma((2, PEERS)), dma((2, PEERS)), dma((2,)),
        ],
        compiler_params=pltpu.CompilerParams(
            collective_id=0, has_side_effects=True, vmem_limit_bytes=40 << 20
        ),
        name="whole",
    )(*args)


def emit_kernel(a, b, c, x, y, z, sem):
    copies = [
        pltpu.make_async_copy(src, dst, sem.at[i]) for i, (src, dst) in enumerate(((a, x), (b, y), (c, z)))
    ]
    for one in copies:
        one.start()
    for one in copies:
        one.wait()


def emit(*arrays):
    return pl.pallas_call(
        emit_kernel,
        out_shape=tuple(jax.ShapeDtypeStruct(a.shape, a.dtype) for a in arrays),
        in_specs=[pl.BlockSpec(memory_space=pltpu.VMEM)] * 3,
        out_specs=(pl.BlockSpec(memory_space=pltpu.HBM),) * 3,
        scratch_shapes=[pltpu.SemaphoreType.DMA((3,))],
        compiler_params=pltpu.CompilerParams(vmem_limit_bytes=1 << 20),
        name="emit",
    )(*arrays)


def local(query_act, key_act, value_act, attn_out, grad_out, log_sum, kv_lists):
    args = (query_act, key_act, value_act, attn_out, grad_out, log_sum, kv_lists)
    return emit(*whole(*(pltpu.with_memory_space_constraint(a, pltpu.HBM) for a in args)))


def solution(mesh):
    row = P(("blk", "head"), None)
    return jax.shard_map(
        local,
        mesh=mesh,
        in_specs=(row,) * 6 + (P("blk", None),),
        out_specs=(row,) * 3,
        check_vma=False,
    )
```
